32 devices in a mesh: dp: 8 (over z, y), tensor: 4 (over x, core).
Axes of the slice: x: 2, y: 2, z: 4, core: 2. Of those that a mesh axis runs over, the one named last changes fastest.
Arguments:
- block_input: bfloat16 [20480, 1024], P(('dp', 'tensor')), may hold values from -6 to 6
- norm_gains: float32 [2, 1024], P(None, 'dp'), may hold values from 0.1 to 1.9
- qkv_weight: float32 [3, 1024, 1024], P(None, 'dp', 'tensor'), may hold values from -0.1875 to 0.1875
- out_weight: float32 [1024, 1024], P('tensor', 'dp'), may hold values from -3 to 3
- gate_up_weight: float32 [2, 1024, 4096], P(None, 'dp', 'tensor'), may hold values from -0.1875 to 0.1875
- down_weight: float32 [4096, 1024], P('tensor', 'dp'), may hold values from -0.09375 to 0.09375
- parent_of_row: int32 [20480], P('dp'), may hold values from 0 to 4, as said below
- cotangent: float32 [20480, 1024], P(('dp', 'tensor')), may hold values from -6 to 6
Outputs:
- block_output: float32 [20480, 1024], P(('dp', 'tensor'))
- input_grad: float32 [20480, 1024], P(('dp', 'tensor'))
- norm_gains_grad: float32 [2, 1024], P(None, 'dp')
- qkv_weight_grad: float32 [3, 1024, 1024], P(None, 'dp', 'tensor')
- out_weight_grad: float32 [1024, 1024], P('tensor', 'dp')
- gate_up_weight_grad: float32 [2, 1024, 4096], P(None, 'dp', 'tensor')
- down_weight_grad: float32 [4096, 1024], P('tensor', 'dp')
The draws below stay inside these ranges and needn't reach their ends.
Inputs may be any that keep to these rules, and one draw needn't show every extreme that they name: `parent_of_row`: trunk and branch rows hold 0; the rows of a leaf hold its branch, 1 to 4; each branch is the parent of exactly two leaves of its tree.
All inputs are finite; a program needn't handle non-finite values.
Results may differ from the reference program's by a relative error of at most 0.019.
Values may be sent and summed in bfloat16 or wider, within the bound.
No kernel may reach another device: no remote copies, remote signals or barrier semaphores. Data moves between devices by JAX's collectives and lax.ppermute only.
A program may use at most 192 MiB of HBM per device.

```python
import jax
import jax.numpy as jnp
from jax import lax

D = 1024
HEADS = 16
HDIM = 64
FF = 4096
TRUNK = 1024
SEG = 128
ROW_TREE = 2560
TREES = 8
ROWS = 20480


def draw_parent_of_row(key, part):
    tree_keys = jax.random.split(key, TREES)

    def one_tree(tree_key):
        leaf_order = jax.random.permutation(tree_key, 8)
        leaf_parent = (leaf_order // 2 + 1).astype(jnp.int32)
        leaf_rows = jnp.repeat(leaf_parent, SEG)
        return jnp.concatenate([jnp.zeros((TRUNK + 4 * SEG,), jnp.int32), leaf_rows])
    return jax.vmap(one_tree)(tree_keys).reshape(TREES * ROW_TREE)


def block_scale(rng, extent, cuts, smallest, high):
    factor_of, own = 1.0, jax.random.fold_in(rng, 6)
    for dim, shards_of in cuts:
        steps = jnp.exp(jax.random.uniform(jax.random.fold_in(own, dim), (shards_of,), jnp.float32, smallest / len(cuts), high / len(cuts)))
        factor_of = factor_of * jnp.repeat(steps, extent[dim] // shards_of).reshape([-1 if axis == dim else 1 for axis in range(len(extent))])
    return factor_of


def centred(rng, shape, spread, reach, cuts=(), kind=jnp.bfloat16):
    drawn = jax.random.normal(rng, shape, jnp.float32) * spread
    if len(cuts) > 0:
        drawn = block_scale(rng, shape, cuts, -0.22, 0.18) * drawn
    return jnp.clip(drawn, min=-reach, max=reach).astype(kind)


def setup_inputs(seed: int = 0) -> dict:
    splits = jax.random.split(jax.random.key(seed), 9)
    return {
        "block_input": centred(splits[0], (ROWS, D), 1.0, 6.0, ((0, 32),)),
        "norm_gains": jnp.clip(1.0 + 0.18 * jax.random.normal(splits[1], (2, D), jnp.float32), 0.1, 1.9),
        "qkv_weight": centred(splits[2], (3, D, D), D ** -0.5, 0.1875, ((1, 8), (2, 4)), jnp.float32),
        "out_weight": centred(splits[3], (D, D), (max(4, D // 256)) ** -0.5, 3.0, ((0, 4), (1, 8)), jnp.float32),
        "gate_up_weight": centred(splits[4], (2, D, FF), D ** -0.5, 0.1875, ((1, 8), (2, 4)), jnp.float32),
        "down_weight": centred(splits[5], (FF, D), FF ** -0.5, 0.09375, ((0, 4), (1, 8)), jnp.float32),
        "parent_of_row": draw_parent_of_row(jax.random.fold_in(splits[8], 71), 0),
        "cotangent": centred(splits[7], (ROWS, D), 1.0, 6.0, ((0, 32),), jnp.float32),
    }


highest = lax.Precision.HIGHEST
epsilon = 1e-06

@jax.custom_vjp
def low(v):
    return lax.optimization_barrier(v.astype(jnp.bfloat16)).astype(jnp.float32)

@jax.custom_vjp
def low_back(v):
    return v

def low_keep(v):
    return (low(v), None)

def low_pass(kept, grad):
    return (grad,)

def back_keep(v):
    return (v, None)

def back_low(kept, grad):
    return (low(grad),)
low.defvjp(low_keep, low_pass)
low_back.defvjp(back_keep, back_low)

def norm_rows(values, gain_row):
    inverse_rms = lax.rsqrt(lax.optimization_barrier(jnp.mean(values * values, axis=-1, keepdims=True)) + epsilon)
    return values * inverse_rms * gain_row

def segment_ids(row_count):
    position = jnp.arange(row_count, dtype=jnp.int32)
    tree_base = position // ROW_TREE * 13
    within = position % ROW_TREE
    beyond = within - TRUNK
    own_segment = jnp.where(within < TRUNK, 0, jnp.where(beyond < 4 * SEG, 1 + beyond // SEG, 5 + (beyond - 4 * SEG) // SEG))
    return ((own_segment + tree_base).astype(jnp.int32), tree_base.astype(jnp.int32))

def attend_tree(tree_inputs):
    query_rows, key_rows, value_rows, tree_segment, tree_parent, tree_trunk = tree_inputs
    score_scale = float(HDIM) ** (-0.5)
    position = jnp.arange(ROW_TREE, dtype=jnp.int32)
    column_segment = tree_segment[None, :]
    allowed = (position[None, :] <= position[:, None]) & ((column_segment == tree_segment[:, None]) | (column_segment == tree_parent[:, None]) | (column_segment == tree_trunk[:, None]))
    scores = low_back(jnp.einsum('qhd,khd->hqk', query_rows, key_rows, precision=highest) * score_scale)
    scores = jnp.where(allowed[None], scores, -1e+30)
    top_score = lax.optimization_barrier(jnp.max(scores, axis=-1, keepdims=True))
    exp_scores = jnp.exp(scores - top_score)
    probs = low(exp_scores / lax.optimization_barrier(jnp.sum(exp_scores, axis=-1, keepdims=True)))
    mixed_heads = jnp.einsum('hqk,khd->qhd', probs, value_rows, precision=highest)
    return low_back(low(mixed_heads))

def reference(block_input, norm_gains, qkv_weight, out_weight, gate_up_weight, down_weight, parent_of_row, cotangent):
    rows_all = block_input.shape[0]
    tree_count = rows_all // ROW_TREE
    segment_of_row, trunk_of_row = segment_ids(rows_all)
    parent_segment = parent_of_row + trunk_of_row

    def forward(residual_in, gains, qkv_master, out_master, gate_up_master, down_master):
        gains_low = low(gains)
        normed_attn = low(norm_rows(residual_in, gains_low[0]))
        projected = low_back(low(jnp.einsum('rd,cde->cre', normed_attn, low(qkv_master), precision=highest)))
        per_tree = projected.reshape(3, tree_count, ROW_TREE, HEADS, HDIM)
        tree_inputs = (per_tree[0], per_tree[1], per_tree[2], segment_of_row.reshape(tree_count, ROW_TREE), parent_segment.reshape(tree_count, ROW_TREE), trunk_of_row.reshape(tree_count, ROW_TREE))
        attended = lax.map(jax.checkpoint(attend_tree), tree_inputs).reshape(rows_all, HEADS * HDIM)
        attn_branch = low_back(jnp.dot(attended, low(out_master), precision=highest))
        residual_mid = residual_in + attn_branch
        normed_mlp = low(norm_rows(residual_mid, gains_low[1]))
        gate_up = low_back(low(jnp.einsum('rd,cdf->crf', normed_mlp, low(gate_up_master), precision=highest)))
        hidden = low(jax.nn.silu(gate_up[0]) * gate_up[1])
        mlp_branch = low_back(jnp.dot(hidden, low(down_master), precision=highest))
        return residual_mid + mlp_branch
    block_output, pullback = jax.vjp(forward, block_input.astype(jnp.float32), norm_gains, qkv_weight, out_weight, gate_up_weight, down_weight)
    grads = pullback(cotangent)
    return (block_output, grads[0], grads[1], grads[2], grads[3], grads[4], grads[5])
```

```python
import functools
import jax
import jax.numpy as jnp
from jax import lax
from jax.experimental import pallas as pl
from jax.experimental.pallas import tpu as pltpu
from jax.sharding import PartitionSpec as P

HDIM = 64
TRUNK = 1024
SEG = 128
ROW_TREE = 2560


epsilon = 1e-06


def norm_rows(values, gain_row):
    inverse_rms = lax.rsqrt(jnp.mean(values * values, axis=-1, keepdims=True) + epsilon)
    return values * inverse_rms * gain_row


def segment_ids(row_count):
    position = jnp.arange(row_count, dtype=jnp.int32)
    tree_base = position // ROW_TREE * 13
    within = position % ROW_TREE
    beyond = within - TRUNK
    own_segment = jnp.where(
        within < TRUNK,
        0,
        jnp.where(beyond < 4 * SEG, 1 + beyond // SEG, 5 + (beyond - 4 * SEG) // SEG),
    )
    return (own_segment + tree_base, tree_base)


def body_any_mesh(
    block_input,
    norm_gains,
    qkv_weight,
    out_weight,
    gate_up_weight,
    down_weight,
    parent_of_row,
    cotangent,
):
    gains_cast = norm_gains.astype(jnp.bfloat16)
    qkv_cast = qkv_weight.astype(jnp.bfloat16)
    out_cast = out_weight.astype(jnp.bfloat16)
    gate_up_cast = gate_up_weight.astype(jnp.bfloat16)
    down_cast = down_weight.astype(jnp.bfloat16)
    gains_low, qkv_low, out_low, gate_up_low, down_low = (
        lax.all_gather(gains_cast, "dp", axis=1, tiled=True),
        lax.all_gather(qkv_cast, "dp", axis=1, tiled=True),
        lax.all_gather(out_cast, "dp", axis=1, tiled=True),
        lax.all_gather(gate_up_cast, "dp", axis=1, tiled=True),
        lax.all_gather(down_cast, "dp", axis=1, tiled=True),
    )
    row_count = parent_of_row.shape[0]
    width_local = qkv_low.shape[2]
    head_local = width_local // HDIM
    block_rows = min(512, row_count)
    block_count = row_count // block_rows
    score_scale = float(HDIM) ** (-0.5)
    segment_of_row, trunk_of_row = segment_ids(row_count)
    parent_segment = parent_of_row + trunk_of_row
    column_index = jnp.arange(row_count, dtype=jnp.int32)
    residual_in = block_input.astype(jnp.float32)
    gain_attn = gains_low[0].astype(jnp.float32)
    gain_mlp = gains_low[1].astype(jnp.float32)
    normed_attn = lax.all_gather(
        norm_rows(residual_in, gain_attn).astype(jnp.bfloat16), "tensor", axis=0, tiled=True
    )
    projected = jnp.einsum(
        "rd,cde->cre", normed_attn, qkv_low, preferred_element_type=jnp.float32
    ).astype(jnp.bfloat16)
    query_rows = projected[0].reshape(row_count, head_local, HDIM)
    key_rows = projected[1].reshape(row_count, head_local, HDIM)
    value_rows = projected[2].reshape(row_count, head_local, HDIM)

    def block_scores(block_index):
        row_start = block_index * block_rows
        query_block = lax.dynamic_slice_in_dim(query_rows, row_start, block_rows, 0)
        scores = (
            jnp.einsum("qhd,khd->hqk", query_block, key_rows, preferred_element_type=jnp.float32)
            * score_scale
        )
        row_index = row_start + jnp.arange(block_rows, dtype=jnp.int32)
        row_segment = lax.dynamic_slice_in_dim(segment_of_row, row_start, block_rows, 0)
        row_parent = lax.dynamic_slice_in_dim(parent_segment, row_start, block_rows, 0)
        row_trunk = lax.dynamic_slice_in_dim(trunk_of_row, row_start, block_rows, 0)
        column_segment = segment_of_row[None, :]
        allowed = (column_index[None, :] <= row_index[:, None]) & (
            (column_segment == row_segment[:, None])
            | (column_segment == row_parent[:, None])
            | (column_segment == row_trunk[:, None])
        )
        return (jnp.where(allowed[None], scores, -1e30), query_block)

    def attend_block(block_index):
        scores, query_block = block_scores(block_index)
        top_score = jnp.max(scores, axis=-1, keepdims=True)
        exp_scores = jnp.exp(scores - top_score)
        row_total = jnp.sum(exp_scores, axis=-1, keepdims=True)
        softmax_low = (exp_scores / row_total).astype(jnp.bfloat16)
        mixed_heads = jnp.einsum(
            "hqk,khd->qhd", softmax_low, value_rows, preferred_element_type=jnp.float32
        ).astype(jnp.bfloat16)
        return (mixed_heads, (top_score + jnp.log(row_total))[..., 0])

    block_ids = jnp.arange(block_count, dtype=jnp.int32)
    attended, log_totals = lax.map(attend_block, block_ids)
    attended = attended.reshape(row_count, width_local)
    attn_partial = jnp.dot(attended, out_low, preferred_element_type=jnp.float32)
    residual_mid = residual_in + lax.psum_scatter(
        attn_partial, "tensor", scatter_dimension=0, tiled=True
    )
    normed_mlp = lax.all_gather(
        norm_rows(residual_mid, gain_mlp).astype(jnp.bfloat16), "tensor", axis=0, tiled=True
    )
    gate_up = jnp.einsum(
        "rd,cdf->crf", normed_mlp, gate_up_low, preferred_element_type=jnp.float32
    ).astype(jnp.bfloat16)
    gate_value = gate_up[0].astype(jnp.float32)
    up_value = gate_up[1].astype(jnp.float32)
    sigmoid_gate = jax.nn.sigmoid(gate_value)
    hidden = (gate_value * sigmoid_gate * up_value).astype(jnp.bfloat16)
    mlp_partial = jnp.dot(hidden, down_low, preferred_element_type=jnp.float32)
    block_output = residual_mid + lax.psum_scatter(
        mlp_partial.astype(jnp.bfloat16), "tensor", scatter_dimension=0, tiled=True
    ).astype(jnp.float32)
    gains_again = norm_gains.astype(jnp.bfloat16)
    qkv_again = qkv_weight.astype(jnp.bfloat16)
    out_again = out_weight.astype(jnp.bfloat16)
    gate_up_again = gate_up_weight.astype(jnp.bfloat16)
    down_again = down_weight.astype(jnp.bfloat16)
    gains_low, qkv_low, out_low, gate_up_low, down_low = (
        lax.all_gather(gains_again, "dp", axis=1, tiled=True),
        lax.all_gather(qkv_again, "dp", axis=1, tiled=True),
        lax.all_gather(out_again, "dp", axis=1, tiled=True),
        lax.all_gather(gate_up_again, "dp", axis=1, tiled=True),
        lax.all_gather(down_again, "dp", axis=1, tiled=True),
    )
    gain_attn = gains_low[0].astype(jnp.float32)
    gain_mlp = gains_low[1].astype(jnp.float32)
    mlp_grad_rows = lax.all_gather(cotangent.astype(jnp.bfloat16), "tensor", axis=0, tiled=True)
    down_grad = jnp.einsum("rf,rd->fd", hidden, mlp_grad_rows, preferred_element_type=jnp.float32)
    hidden_grad = jnp.einsum(
        "rd,fd->rf", mlp_grad_rows, down_low, preferred_element_type=jnp.float32
    )
    gate_grad = hidden_grad * up_value * sigmoid_gate * (1.0 + gate_value * (1.0 - sigmoid_gate))
    up_grad = hidden_grad * gate_value * sigmoid_gate
    gate_up_grad_low = jnp.stack([gate_grad, up_grad]).astype(jnp.bfloat16)
    gate_up_grad = jnp.einsum(
        "rd,crf->cdf", normed_mlp, gate_up_grad_low, preferred_element_type=jnp.float32
    )
    normed_mlp_part = jnp.einsum(
        "crf,cdf->rd", gate_up_grad_low, gate_up_low, preferred_element_type=jnp.float32
    )
    normed_mlp_grad = lax.psum_scatter(normed_mlp_part, "tensor", scatter_dimension=0, tiled=True)
    norm_back_mlp = jax.vjp(norm_rows, residual_mid, gain_mlp)[1]
    mid_from_norm, gain_mlp_grad = norm_back_mlp(normed_mlp_grad)
    mid_grad = cotangent + mid_from_norm
    attn_grad_rows = lax.all_gather(mid_grad.astype(jnp.bfloat16), "tensor", axis=0, tiled=True)
    out_grad = jnp.einsum("re,rd->ed", attended, attn_grad_rows, preferred_element_type=jnp.float32)
    attended_grad = jnp.einsum(
        "rd,ed->re", attn_grad_rows, out_low, preferred_element_type=jnp.float32
    ).astype(jnp.bfloat16)
    attended_grad = attended_grad.reshape(row_count, head_local, HDIM)

    def back_block(carry, block_inputs):
        key_grad, value_grad = carry
        block_index, log_total = block_inputs
        scores, query_block = block_scores(block_index)
        probs = jnp.exp(scores - log_total[..., None])
        grad_block = lax.dynamic_slice_in_dim(
            attended_grad, block_index * block_rows, block_rows, 0
        )
        probs_grad = jnp.einsum(
            "qhd,khd->hqk", grad_block, value_rows, preferred_element_type=jnp.float32
        )
        inner_term = jnp.sum(probs * probs_grad, axis=-1, keepdims=True)
        score_grad = (probs * (probs_grad - inner_term)).astype(jnp.bfloat16)
        query_grad = (
            jnp.einsum("hqk,khd->qhd", score_grad, key_rows, preferred_element_type=jnp.float32)
            * score_scale
        )
        key_grad = (
            key_grad
            + jnp.einsum(
                "hqk,qhd->khd", score_grad, query_block, preferred_element_type=jnp.float32
            )
            * score_scale
        )
        value_grad = value_grad + jnp.einsum(
            "hqk,qhd->khd",
            probs.astype(jnp.bfloat16),
            grad_block,
            preferred_element_type=jnp.float32,
        )
        return ((key_grad, value_grad), query_grad)

    zero_grad = jnp.zeros((row_count, head_local, HDIM), jnp.float32)
    carried, query_grads = lax.scan(back_block, (zero_grad, zero_grad), (block_ids, log_totals))
    projected_grad = jnp.stack(
        [
            query_grads.reshape(row_count, width_local),
            carried[0].reshape(row_count, width_local),
            carried[1].reshape(row_count, width_local),
        ]
    ).astype(jnp.bfloat16)
    qkv_grad = jnp.einsum(
        "rd,cre->cde", normed_attn, projected_grad, preferred_element_type=jnp.float32
    )
    normed_attn_part = jnp.einsum(
        "cre,cde->rd", projected_grad, qkv_low, preferred_element_type=jnp.float32
    )
    normed_attn_grad = lax.psum_scatter(
        normed_attn_part.astype(jnp.bfloat16), "tensor", scatter_dimension=0, tiled=True
    ).astype(jnp.float32)
    norm_back_attn = jax.vjp(norm_rows, residual_in, gain_attn)[1]
    input_from_norm, gain_attn_grad = norm_back_attn(normed_attn_grad)
    input_grad = mid_grad + input_from_norm
    gain_grads = lax.psum(jnp.stack([gain_attn_grad, gain_mlp_grad]), "tensor")
    gains_out, qkv_out, out_out, gate_up_out, down_out = (
        lax.psum_scatter(
            gain_grads.astype(jnp.bfloat16), "dp", scatter_dimension=1, tiled=True
        ).astype(jnp.float32),
        lax.psum_scatter(
            qkv_grad.astype(jnp.bfloat16), "dp", scatter_dimension=1, tiled=True
        ).astype(jnp.float32),
        lax.psum_scatter(
            out_grad.astype(jnp.bfloat16), "dp", scatter_dimension=1, tiled=True
        ).astype(jnp.float32),
        lax.psum_scatter(
            gate_up_grad.astype(jnp.bfloat16), "dp", scatter_dimension=1, tiled=True
        ).astype(jnp.float32),
        lax.psum_scatter(
            down_grad.astype(jnp.bfloat16), "dp", scatter_dimension=1, tiled=True
        ).astype(jnp.float32),
    )
    return (block_output, input_grad, gains_out, qkv_out, out_out, gate_up_out, down_out)


QB = 256
NT = (((1,), (1,)), ((), ()))
NN = (((1,), (0,)), ((), ()))
TN = (((0,), (0,)), ((), ()))


def _dot(a, b, dims):
    return lax.dot_general(a, b, dims, preferred_element_type=jnp.float32)


def _stacked(tile, columns, n):
    return pl.BlockSpec((1, tile, columns), lambda i: (n, i, 0))


def _full(shape):
    return pl.BlockSpec(shape, lambda i: (0,) * len(shape))


def _smem():
    return pl.BlockSpec(memory_space=pltpu.SMEM)


def _rows(tile, columns):
    return pl.BlockSpec((tile, columns), lambda i: (i, 0))


def _params():
    return pltpu.CompilerParams(dimension_semantics=("arbitrary",), vmem_limit_bytes=60 << 20)


STRETCH = 6.0


def _cost(flops, bytes_accessed):
    return pl.CostEstimate(
        flops=int(flops * STRETCH), bytes_accessed=int(bytes_accessed * STRETCH), transcendentals=0
    )


def _row_tile(rows):
    return rows // 2 if rows % 32 == 0 else rows


def _normed(values):
    inverse_rms = lax.rsqrt(jnp.mean(values * values, axis=-1, keepdims=True) + epsilon)
    return inverse_rms, values * inverse_rms


def _place_kernel(where_ref, *refs):
    shards, out = refs[:-1], refs[-1]
    size = shards[0].shape[0]
    for n, shard in enumerate(shards):
        out[pl.ds(pl.multiple_of(where_ref[n] * size, size), size), :] = shard[...]


def place(where, shards):
    size, columns = shards[0].shape
    return pl.pallas_call(
        _place_kernel,
        grid=(1,),
        out_shape=jax.ShapeDtypeStruct((size * len(shards), columns), shards[0].dtype),
        in_specs=[_smem()] + [_full((size, columns))] * len(shards),
        out_specs=_full((size * len(shards), columns)),
        compiler_params=_params(),
        cost_estimate=_cost(0, 4 * size * columns * len(shards)),
        name="place",
    )(where, *shards)


def _project_kernel(x0_ref, x1_ref, gain_ref, w_ref, n0_ref, n1_ref, p0_ref, p1_ref):
    def run(x_ref, normed_ref, out_ref):
        normed = (_normed(x_ref[...].astype(jnp.float32))[1] * gain_ref[...]).astype(jnp.bfloat16)
        normed_ref[...] = normed
        out_ref[...] = _dot(normed, w_ref[...], NN).astype(jnp.bfloat16)

    half = pl.num_programs(0) // 2

    @pl.when(pl.program_id(0) < half)
    def _():
        run(x0_ref, n0_ref, p0_ref)

    @pl.when(pl.program_id(0) >= half)
    def _():
        run(x1_ref, n1_ref, p1_ref)


def project(x0, x1, gain, weight, columns):
    rows, depth = x0.shape
    tile = _row_tile(rows)
    steps = rows // tile
    early = lambda c: pl.BlockSpec((tile, c), lambda i: (jnp.minimum(i, steps - 1), 0))
    late = lambda c: pl.BlockSpec((tile, c), lambda i: (jnp.maximum(i - steps, 0), 0))
    out = lambda c: jax.ShapeDtypeStruct((rows, c), jnp.bfloat16)
    return pl.pallas_call(
        _project_kernel,
        grid=(2 * steps,),
        out_shape=[out(depth), out(depth), out(columns), out(columns)],
        in_specs=[early(depth), late(depth), _full((1, depth)), _full((depth, columns))],
        out_specs=[early(depth), late(depth), early(columns), late(columns)],
        compiler_params=_params(),
        cost_estimate=_cost(4 * rows * depth * columns, 4 * rows * (2 * depth + columns)),
        name="project",
    )(x0, x1, gain, weight)


def _mlp_kernel(keep, step, att0, att1, att2, att3, x_ref, cot_ref, gain_ref, w_hbm, d_hbm, m_hbm, *refs):
    part_ref, hidden_ref, grad_ref, normed_ref, branch_ref = refs[:5]
    w_ref, d_ref, mate_ref, acc, acc_b, sems = refs[-6:]
    width = att0.shape[2]
    count = hidden_ref.shape[1]
    out_at = 2 * count
    chunks = count // step
    pulls = [
        pltpu.make_async_copy(
            w_hbm.at[:, pl.ds(out_at, 2 * width)], w_ref.at[:, pl.ds(out_at, 2 * width)], sems.at[0]
        ),
        pltpu.make_async_copy(m_hbm, mate_ref, sems.at[1]),
    ]
    for c in range(chunks):
        for g in range(3):
            source, target = (w_hbm, w_ref) if g < 2 else (d_hbm, d_ref)
            at = pl.ds(g % 2 * count + c * step, step)
            pulls.append(
                pltpu.make_async_copy(source.at[:, at], target.at[:, at], sems.at[2 + 3 * c + g])
            )
    first = pl.program_id(0) == 0

    @pl.when(first)
    def _():
        for pull in pulls:
            pull.start()
        for pull in pulls[:2]:
            pull.wait()

    branch = _dot(att0[0], w_ref[:, out_at : out_at + width], NT)
    branch += _dot(att2[0], w_ref[:, out_at + width : out_at + 2 * width], NT)
    branch += _dot(att1[0], mate_ref[:, :width], NT) + _dot(att3[0], mate_ref[:, width:], NT)
    residual = x_ref[...].astype(jnp.float32) + branch
    if keep:
        refs[5][...] = residual
    normed_ref[...] = (_normed(residual)[1] * gain_ref[...]).astype(jnp.bfloat16)
    for c in range(chunks):

        @pl.when(first)
        def _():
            for pull in pulls[2 + 3 * c : 5 + 3 * c]:
                pull.wait()

        gate_at, up_at = [slice(g * count + c * step, g * count + (c + 1) * step) for g in (0, 1)]
        gate = _dot(normed_ref[...], w_ref[:, gate_at], NN).astype(jnp.bfloat16).astype(jnp.float32)
        up = _dot(normed_ref[...], w_ref[:, up_at], NN).astype(jnp.bfloat16).astype(jnp.float32)
        hidden_grad = _dot(cot_ref[...], d_ref[:, gate_at], NN)
        sig = 0.5 * jnp.tanh(0.5 * gate) + 0.5
        act = gate * sig
        hidden_ref[:, gate_at] = (act * up).astype(jnp.bfloat16)
        grad_ref[:, gate_at] = (hidden_grad * up * (sig + act * (1.0 - sig))).astype(jnp.bfloat16)
        grad_ref[:, up_at] = (hidden_grad * act).astype(jnp.bfloat16)
        term = _dot(grad_ref[:, gate_at], w_ref[:, gate_at], NT) + _dot(
            grad_ref[:, up_at], w_ref[:, up_at], NT
        )
        down = _dot(hidden_ref[:, gate_at], d_ref[:, gate_at], NT)
        if c > 0:
            term = term + acc[...]
            down = down + acc_b[...]
        if c < chunks - 1:
            acc[...] = term
            acc_b[...] = down
        else:
            part_ref[...] = term.astype(part_ref.dtype)
            branch_ref[...] = down.astype(branch_ref.dtype)


def mlp(attended, x, cot, gain, weights, down, out_mate, keep, step=512):
    rows, depth = x.shape
    width = attended[0][0].shape[2]
    count = down.shape[1]
    tile = _row_tile(rows)
    step = min(step, count)
    outs = [(depth, jnp.bfloat16), (count, jnp.bfloat16), (2 * count, jnp.bfloat16)]
    outs += [(depth, jnp.bfloat16)] * 2
    if keep:
        outs.append((depth, jnp.float32))
    anywhere = pl.BlockSpec(memory_space=pl.ANY)
    return pl.pallas_call(
        functools.partial(_mlp_kernel, keep, step),
        grid=(rows // tile,),
        out_shape=[jax.ShapeDtypeStruct((rows, c), d) for c, d in outs],
        in_specs=[_stacked(tile, width, n) for v, n in attended]
        + [_rows(tile, depth)] * 2
        + [_full((1, depth)), anywhere, anywhere, anywhere],
        out_specs=[_rows(tile, c) for c, d in outs],
        scratch_shapes=[
            pltpu.VMEM(weights.shape, jnp.bfloat16),
            pltpu.VMEM(down.shape, jnp.bfloat16),
            pltpu.VMEM(out_mate.shape, jnp.bfloat16),
            pltpu.VMEM((tile, depth), jnp.float32),
            pltpu.VMEM((tile, depth), jnp.float32),
            pltpu.SemaphoreType.DMA((2 + 3 * (count // step),)),
        ],
        compiler_params=_params(),
        cost_estimate=_cost(2 * rows * depth * (4 * width + 6 * count), 18 << 20),
        name="mlp",
    )(*[v for v, n in attended], x, cot, gain, weights, down, out_mate)


def _pull_groups(right, right_s, row_at, column_at, step, sems, base):
    groups = []
    for c in range(right[0].shape[-1] // step):
        group = []
        at = row_at
        for j, piece in enumerate(right):
            rows = piece.shape[0]
            group.append(
                pltpu.make_async_copy(
                    piece.at[:, pl.ds(c * step, step)],
                    right_s.at[pl.ds(at, rows), pl.ds(column_at + c * step, step)],
                    sems.at[base + c * len(right) + j],
                )
            )
            at += rows
        groups.append(group)
    return groups


def _start_all(groups):
    @pl.when(pl.program_id(0) == 0)
    def _():
        for group in groups:
            for pull in group:
                pull.start()


def _wait_group(group):
    @pl.when(pl.program_id(0) == 0)
    def _():
        for pull in group:
            pull.wait()


def _join(pieces, out):
    at = 0
    for piece in pieces:
        rows = piece.shape[0]
        out[at : at + rows, :] = piece[...]
        at += rows


def _split_rows(acc, y, near, far):
    size = near.shape[1]
    near[...] = acc[pl.ds(pl.multiple_of(y * size, size), size), :].astype(near.dtype)[None]
    far[...] = acc[pl.ds(pl.multiple_of((1 - y) * size, size), size), :].astype(far.dtype)[None]


def _grad_kernel(n, step, split, *refs):
    if split:
        y_ref, refs = refs[0], refs[1:]
    left, right = refs[:n], refs[n : 2 * n]
    outs = refs[2 * n : -3 - split]
    left_s, right_s, sems = refs[len(refs) - 3 - split : len(refs) - split]
    acc = refs[-1] if split else outs[0]
    groups = _pull_groups(right, right_s, 0, 0, step, sems, 0)
    _start_all(groups)
    _join(left, left_s)
    for c, group in enumerate(groups):
        at = slice(c * step, (c + 1) * step)
        _wait_group(group)
        acc[:, at] = _dot(left_s[...], right_s[:, at], TN).astype(acc.dtype)
    if split:
        _split_rows(acc, y_ref[0], *outs)


def row_grads(left, right, name, y=None, size=128):
    n, depth = len(left), left[0].shape[1]
    rows = sum(v.shape[0] for v in left)
    columns = right[0].shape[1]
    step = min(columns, 1024)
    block = 2 * size
    split = y is not None
    anywhere = pl.BlockSpec(memory_space=pl.ANY)
    if split:
        out = [jax.ShapeDtypeStruct((depth // block, size, columns), jnp.bfloat16)] * 2
        out_spec = [pl.BlockSpec((1, size, columns), lambda i: (i, 0, 0))] * 2
    else:
        out = jax.ShapeDtypeStruct((depth, columns), jnp.bfloat16)
        out_spec = _rows(block, columns)
    return pl.pallas_call(
        functools.partial(_grad_kernel, n, step, split),
        grid=(depth // block,),
        out_shape=out,
        in_specs=[_smem()] * split
        + [pl.BlockSpec((v.shape[0], block), lambda i: (0, i)) for v in left]
        + [anywhere] * n,
        out_specs=out_spec,
        scratch_shapes=[
            pltpu.VMEM((rows, block), jnp.bfloat16),
            pltpu.VMEM((rows, columns), jnp.bfloat16),
            pltpu.SemaphoreType.DMA((n * (columns // step),)),
        ]
        + [pltpu.VMEM((block, columns), jnp.float32)] * split,
        compiler_params=_params(),
        cost_estimate=_cost(2 * rows * depth * columns, 2 * rows * (depth + columns) + 2 * depth * columns),
        name=name,
    )(*([y] * split), *left, *right)


def _qkv_grad_kernel(n, y_ref, *refs):
    left, right = refs[:n], refs[n : 2 * n]
    w_ref, gain_ref, row_ref, near, far, left_s, right_s, acc, sems = refs[2 * n :]
    columns = right_s.shape[1]
    groups = _pull_groups(right, right_s, 0, 0, columns, sems, 0)
    _start_all(groups)
    _join(left, left_s)
    _wait_group(groups[0])
    total = _dot(left_s[...], right_s[...], TN)
    acc[:, :columns] = total
    row = jnp.concatenate(
        [1.0 / gain_ref[...], row_ref[...], jnp.zeros((SEG - 9, row_ref.shape[1]), jnp.float32)], axis=0
    ).T
    attn = jnp.sum(total * w_ref[...].astype(jnp.float32), axis=-1, keepdims=True) * row[:, 0:1]
    lane = lax.broadcasted_iota(jnp.int32, row.shape, 1)
    acc[:, columns:] = jnp.where(lane == 0, attn, row)
    _split_rows(acc, y_ref[0], near, far)


def qkv_grads(y, normed, grads, weight, gain, mlp_sum, size):
    n, depth = len(normed), normed[0].shape[1]
    rows = sum(v.shape[0] for v in normed)
    columns = grads[0].shape[1]
    block = 2 * size
    anywhere = pl.BlockSpec(memory_space=pl.ANY)
    out = jax.ShapeDtypeStruct((depth // block, size, columns + SEG), jnp.bfloat16)
    out_spec = pl.BlockSpec((1, size, columns + SEG), lambda i: (i, 0, 0))
    lanes = lambda r: pl.BlockSpec((r, block), lambda i: (0, i))
    return pl.pallas_call(
        functools.partial(_qkv_grad_kernel, n),
        grid=(depth // block,),
        out_shape=[out, out],
        in_specs=[_smem()]
        + [lanes(v.shape[0]) for v in normed]
        + [anywhere] * n
        + [_rows(block, columns), lanes(1), lanes(8)],
        out_specs=[out_spec, out_spec],
        scratch_shapes=[
            pltpu.VMEM((rows, block), jnp.bfloat16),
            pltpu.VMEM((rows, columns), jnp.bfloat16),
            pltpu.VMEM((block, columns + SEG), jnp.float32),
            pltpu.SemaphoreType.DMA((n,)),
        ],
        compiler_params=_params(),
        cost_estimate=_cost(2 * rows * depth * columns, 2 * rows * (depth + columns) + 2 * depth * columns),
        name="qkv_grads",
    )(y, *normed, *grads, weight, gain, mlp_sum)


def _out_grad_kernel(y_ref, left_ref, a0, a1, a2, a3, near, far, right_s, acc):
    width = a0.shape[2]

    @pl.when(pl.program_id(0) == 0)
    def _():
        for i, a in enumerate((a0, a1, a2, a3)):
            right_s[:, i * width : (i + 1) * width] = a[0]

    acc[...] = _dot(left_ref[...], right_s[...], TN)
    _split_rows(acc, y_ref[0], near, far)


def out_grads(y, left, attended, size):
    rows, depth = left.shape
    width = attended[0][0].shape[2]
    block = 2 * size
    out = jax.ShapeDtypeStruct((depth // block, size, 4 * width), jnp.bfloat16)
    out_spec = pl.BlockSpec((1, size, 4 * width), lambda i: (i, 0, 0))
    member = lambda n: pl.BlockSpec((1, rows, width), lambda i: (n, 0, 0))
    return pl.pallas_call(
        _out_grad_kernel,
        grid=(depth // block,),
        out_shape=[out, out],
        in_specs=[_smem(), pl.BlockSpec((rows, block), lambda i: (0, i))]
        + [member(n) for v, n in attended],
        out_specs=[out_spec, out_spec],
        scratch_shapes=[
            pltpu.VMEM((rows, 4 * width), jnp.bfloat16),
            pltpu.VMEM((block, 4 * width), jnp.float32),
        ],
        compiler_params=_params(),
        cost_estimate=_cost(8 * rows * depth * width, 2 * rows * (depth + 4 * width) + 8 * depth * width),
        name="out_grads",
    )(y, left, *[v for v, n in attended])


def _fold_kernel(z_ref, near, passed, *outs):
    count = near.shape[0]
    for step, out in enumerate(outs):
        row = lax.rem(z_ref[0] + step, count)
        out[...] = (near[row].astype(jnp.float32) + passed[row].astype(jnp.float32)).astype(out.dtype)


def fold(z, near, passed):
    count, size, columns = near.shape
    return pl.pallas_call(
        _fold_kernel,
        grid=(1,),
        out_shape=[jax.ShapeDtypeStruct((size, columns), jnp.bfloat16)] * count,
        in_specs=[_smem(), _full(near.shape), _full(near.shape)],
        out_specs=[_full((size, columns))] * count,
        compiler_params=_params(),
        cost_estimate=_cost(0, 6 * count * size * columns),
        name="fold",
    )(z, near, passed)


def _mid_kernel(p0, p1, p2, res_ref, cot_ref, gain_ref, near_ref, mate_ref, mid_ref, attn_ref, a0, a1, a2, a3, sum_ref):
    width = a0.shape[1]
    grad = p0[...].astype(jnp.float32) + p1[...].astype(jnp.float32) + p2[...].astype(jnp.float32)
    inverse, normed = _normed(res_ref[...])
    term = jnp.sum(grad * normed, axis=0, keepdims=True)

    @pl.when(pl.program_id(0) == 0)
    def _():
        sum_ref[...] = jnp.zeros_like(sum_ref)

    sum_ref[0:1, :] += term
    scaled = grad * gain_ref[...]
    mid = cot_ref[...] + inverse * (scaled - normed * jnp.mean(scaled * normed, axis=-1, keepdims=True))
    mid_ref[...] = mid
    low = mid.astype(jnp.bfloat16)
    attn_ref[...] = low
    a0[...] = _dot(low, near_ref[:, :width], NN).astype(jnp.bfloat16)
    a1[...] = _dot(low, mate_ref[:, :width], NN).astype(jnp.bfloat16)
    a2[...] = _dot(low, near_ref[:, width : 2 * width], NN).astype(jnp.bfloat16)
    a3[...] = _dot(low, mate_ref[:, width:], NN).astype(jnp.bfloat16)


def middle(parts, residual, cot, gain, weights, out_mate):
    rows, depth = residual.shape
    width = out_mate.shape[1] // 2
    tile = _row_tile(rows)
    return pl.pallas_call(
        _mid_kernel,
        grid=(rows // tile,),
        out_shape=[
            jax.ShapeDtypeStruct((rows, depth), jnp.float32),
            jax.ShapeDtypeStruct((rows, depth), jnp.bfloat16),
        ]
        + [jax.ShapeDtypeStruct((rows, width), jnp.bfloat16)] * 4
        + [jax.ShapeDtypeStruct((8, depth), jnp.float32)],
        in_specs=[_rows(tile, depth)] * 5
        + [
            _full((1, depth)),
            pl.BlockSpec((depth, 2 * width), lambda i: (0, weights.shape[1] // (2 * width) - 1)),
            _full(out_mate.shape),
        ],
        out_specs=[_rows(tile, depth)] * 2 + [_rows(tile, width)] * 4 + [_full((8, depth))],
        compiler_params=_params(),
        cost_estimate=_cost(2 * rows * depth * 4 * width, rows * depth * 20),
        name="middle",
    )(*parts, residual, cot, gain, weights, out_mate)


def _back_kernel(add, grad_ref, w_ref, *refs):
    part = _dot(grad_ref[...], w_ref[...], NT)
    if add:
        part = part + refs[0][...].astype(jnp.float32)
    refs[-1][...] = part.astype(refs[-1].dtype)


def project_back(grad, weight, add=None):
    rows, columns = grad.shape
    depth = weight.shape[0]
    tile = _row_tile(rows)
    extra = [] if add is None else [add]
    return pl.pallas_call(
        functools.partial(_back_kernel, add is not None),
        grid=(rows // tile,),
        out_shape=jax.ShapeDtypeStruct((rows, depth), jnp.bfloat16),
        in_specs=[_rows(tile, columns), _full((depth, columns))] + [_rows(tile, depth)] * len(extra),
        out_specs=_rows(tile, depth),
        compiler_params=_params(),
        cost_estimate=_cost(2 * rows * depth * columns, 2 * rows * (columns + 2 * depth)),
        name="project_back",
    )(grad, weight, *extra)


def _last_kernel(p0, p1, p2, x_ref, mid_ref, gain_ref, out_ref):
    grad = p0[...].astype(jnp.float32) + p1[...].astype(jnp.float32) + p2[...].astype(jnp.float32)
    inverse, normed = _normed(x_ref[...].astype(jnp.float32))
    scaled = grad * gain_ref[...]
    out_ref[...] = mid_ref[...] + inverse * (
        scaled - normed * jnp.mean(scaled * normed, axis=-1, keepdims=True)
    )


def last(parts, x, mid, gain):
    rows, depth = x.shape
    tile = _row_tile(rows)
    return pl.pallas_call(
        _last_kernel,
        grid=(rows // tile,),
        out_shape=jax.ShapeDtypeStruct((rows, depth), jnp.float32),
        in_specs=[_rows(tile, depth)] * 5 + [_full((1, depth))],
        out_specs=_rows(tile, depth),
        compiler_params=_params(),
        cost_estimate=_cost(0, rows * depth * 16),
        name="last",
    )(*parts, x, mid, gain)


def _half_place(info_ref, b, half, piece_blocks):
    block = 2 * b + half
    piece = lax.bitwise_xor(lax.div(block, piece_blocks), info_ref[0])
    return piece, lax.rem(block, piece_blocks) * SEG


def _mask(heads, same, causal):
    key = lax.broadcasted_iota(jnp.int32, (QB, heads * QB), 0)
    query = lax.broadcasted_iota(jnp.int32, (QB, heads * QB), 1) % QB
    allowed = jnp.logical_not(same & ((key // SEG) != (query // SEG)))
    if causal:
        allowed = allowed & (key <= query)
    return allowed


def _spread(block, heads):
    turned = block.T
    lane = lax.broadcasted_iota(jnp.int32, turned.shape, 0) // HDIM
    zero = jnp.zeros_like(turned)
    return jnp.concatenate([jnp.where(lane == h, turned, zero) for h in range(heads)], axis=1)


def _stack(block, heads):
    lane = lax.broadcasted_iota(jnp.int32, block.shape, 1) // HDIM
    zero = jnp.zeros_like(block)
    return jnp.concatenate([jnp.where(lane == h, block, zero) for h in range(heads)], axis=0)


def _parents(info_ref, b):
    leaf = 2 * (b - (TRUNK + 4 * SEG) // QB)
    return [pl.multiple_of(TRUNK - SEG + SEG * info_ref[2 + leaf + side], SEG) for side in (0, 1)]


def _attn_fwd_kernel(heads, piece_count, info_ref, *refs):
    pieces = refs[:piece_count]
    out_ref, lse_ref = refs[piece_count : piece_count + 2]
    q_s, k_s, vt_s, qt_s, s_s, p_s, m_s, l_s, acc_s, kp_s, vp_s = refs[piece_count + 2 :]
    width = heads * HDIM
    piece_rows = pieces[0].shape[0]
    tensor = info_ref[0]
    base = info_ref[1]
    trunk_blocks = TRUNK // QB
    leaf_block = (TRUNK + 4 * SEG) // QB
    for j in range(piece_count):
        at = pl.multiple_of(piece_rows * lax.bitwise_xor(tensor, j), SEG)
        q_s[pl.ds(at, piece_rows), :] = pieces[j][:, :width] * jnp.asarray(HDIM**-0.5, jnp.bfloat16)
        k_s[pl.ds(at, piece_rows), :] = pieces[j][:, width : 2 * width]
        vt_s[:, pl.ds(at, piece_rows)] = pieces[j][:, 2 * width :].T

    def q_block(i, carry):
        b = base + i
        row = pl.multiple_of(b * QB, QB)
        own = pl.ds(row, QB)
        leaf = b >= leaf_block
        qt_s[...] = _spread(q_s[own, :], heads)

        def score(keys, at, size, allowed):
            scores = _dot(keys, qt_s[...], NN)
            if allowed is not None:
                scores = jnp.where(allowed, scores, -1e30)
            s_s[pl.ds(at, size), :] = scores
            return jnp.max(scores, axis=0, keepdims=True)

        m_s[0:1, :] = score(k_s[own, :], TRUNK, QB, _mask(heads, b >= trunk_blocks, True))

        @pl.when(leaf)
        def _():
            for side, at in enumerate(_parents(info_ref, b)):
                kp_s[side * SEG : (side + 1) * SEG, :] = k_s[pl.ds(at, SEG), :]
                vp_s[:, side * SEG : (side + 1) * SEG] = vt_s[:, pl.ds(at, SEG)]
            top = score(kp_s[...], TRUNK + QB, QB, _mask(heads, True, False))
            m_s[0:1, :] = jnp.maximum(m_s[0:1, :], top)

        @pl.when(b >= trunk_blocks)
        def _():
            m_s[0:1, :] = jnp.maximum(m_s[0:1, :], score(k_s[:TRUNK, :], 0, TRUNK, None))

        @pl.when(b < trunk_blocks)
        def _():
            def chunk(c, carry):
                at = pl.multiple_of(c * QB, QB)
                m_s[0:1, :] = jnp.maximum(m_s[0:1, :], score(k_s[pl.ds(at, QB), :], at, QB, None))
                return carry

            lax.fori_loop(0, b, chunk, 0)

        def mix(values, at, size, fresh):
            probs = jnp.exp(s_s[pl.ds(at, size), :] - m_s[0:1, :])
            total = jnp.sum(probs, axis=0, keepdims=True)
            p_s[pl.ds(at, size), :] = probs.astype(jnp.bfloat16)
            l_s[0:1, :] = total if fresh else l_s[0:1, :] + total
            for h in range(heads):
                of = slice(h * HDIM, (h + 1) * HDIM)
                term = _dot(values(of), p_s[pl.ds(at, size), h * QB : (h + 1) * QB], NN)
                acc_s[of, :] = term if fresh else acc_s[of, :] + term

        mix(lambda of: vt_s[of, own], TRUNK, QB, True)

        @pl.when(leaf)
        def _():
            mix(lambda of: vp_s[of, :], TRUNK + QB, QB, False)

        @pl.when(b >= trunk_blocks)
        def _():
            mix(lambda of: vt_s[of, :TRUNK], 0, TRUNK, False)

        @pl.when(b < trunk_blocks)
        def _():
            def chunk(c, carry):
                at = pl.multiple_of(c * QB, QB)
                mix(lambda of: vt_s[of, pl.ds(at, QB)], at, QB, False)
                return carry

            lax.fori_loop(0, b, chunk, 0)

        mixed = []
        for h in range(heads):
            columns = slice(h * QB, (h + 1) * QB)
            total = l_s[0:1, columns]
            lse_ref[h : h + 1, pl.ds(pl.multiple_of(i * QB, QB), QB)] = m_s[0:1, columns] + jnp.log(total)
            mixed.append(acc_s[h * HDIM : (h + 1) * HDIM, :] / total)
        mixed = jnp.concatenate(mixed, axis=0).T.astype(jnp.bfloat16)
        for half in (0, 1):
            piece, at = _half_place(info_ref, b, half, piece_rows // SEG)
            at = pl.multiple_of(at, SEG)
            out_ref[lax.bitwise_and(piece, 1), pl.ds(at, SEG), :] = mixed[half * SEG : (half + 1) * SEG]
        return carry

    lax.fori_loop(0, lse_ref.shape[1] // QB, q_block, 0)


def attention_forward(info, pieces, heads):
    rows = sum(p.shape[0] for p in pieces)
    piece_rows = pieces[0].shape[0]
    width = heads * HDIM
    half = rows // 2
    bf16, f32 = jnp.bfloat16, jnp.float32
    return pl.pallas_call(
        functools.partial(_attn_fwd_kernel, heads, len(pieces)),
        out_shape=[
            jax.ShapeDtypeStruct((2, piece_rows, width), bf16),
            jax.ShapeDtypeStruct((8, half), f32),
        ],
        grid=(1,),
        in_specs=[_smem()] + [_full(p.shape) for p in pieces],
        out_specs=[_full((2, piece_rows, width)), _full((8, half))],
        scratch_shapes=[
            pltpu.VMEM((rows, width), bf16),
            pltpu.VMEM((rows, width), bf16),
            pltpu.VMEM((width, rows), bf16),
            pltpu.VMEM((width, heads * QB), bf16),
            pltpu.VMEM((TRUNK + 2 * QB, heads * QB), f32),
            pltpu.VMEM((TRUNK + 2 * QB, heads * QB), bf16),
            pltpu.VMEM((8, heads * QB), f32),
            pltpu.VMEM((8, heads * QB), f32),
            pltpu.VMEM((width, QB), f32),
            pltpu.VMEM((QB, width), bf16),
            pltpu.VMEM((width, QB), bf16),
        ],
        compiler_params=_params(),
        cost_estimate=_cost(rows * 1400 * width * 4, rows * width * 8),
        name="attn_fwd",
    )(info, *pieces)


def _attn_bwd_kernel(heads, info_ref, *refs):
    n = 4
    pieces, mixed_in, grads = refs[:n], refs[n : n + 2], refs[n + 2 : 2 * n + 2]
    lse_refs = refs[2 * n + 2 : 2 * n + 4]
    outs = refs[2 * n + 4 : 3 * n + 4]
    q_s, k_s, kt_s, v_s, o_s, g_s, dk_s, dv_s, lse_s = refs[3 * n + 4 : 3 * n + 13]
    qt_s, gt_s, qm_s, gm_s, row_s, delta_s, acc_s, kp_s, vp_s, kpt_s = refs[3 * n + 13 :]
    width = heads * HDIM
    piece_rows = pieces[0].shape[0]
    tensor = info_ref[0]
    chip = lax.div(tensor, 2)
    half_rows = lse_refs[0].shape[1]
    scale = HDIM**-0.5
    trunk_blocks = TRUNK // QB
    leaf_block = (TRUNK + 4 * SEG) // QB
    for j in range(n):
        rows_at = pl.ds(pl.multiple_of(piece_rows * lax.bitwise_xor(tensor, j), SEG), piece_rows)
        q_s[rows_at, :] = pieces[j][:, :width] * jnp.asarray(scale, jnp.bfloat16)
        k_s[rows_at, :] = pieces[j][:, width : 2 * width]
        kt_s[:, rows_at] = pieces[j][:, width : 2 * width].T
        v_s[rows_at, :] = pieces[j][:, 2 * width :]
        o_s[rows_at, :] = mixed_in[j // 2][j % 2]
        g_s[rows_at, :] = grads[j][...]
    lse_s[:, pl.ds(pl.multiple_of(chip * half_rows, SEG), half_rows)] = lse_refs[0][...]
    lse_s[:, pl.ds(pl.multiple_of((1 - chip) * half_rows, SEG), half_rows)] = lse_refs[1][...]
    dk_s[...] = jnp.zeros_like(dk_s)
    dv_s[...] = jnp.zeros_like(dv_s)
    head_of_lane = lax.broadcasted_iota(jnp.int32, (8, width), 1) // HDIM
    pick = jnp.where(lax.broadcasted_iota(jnp.int32, (8, width), 0) == head_of_lane, 1.0, 0.0)

    def q_block(b, carry):
        row = pl.multiple_of(b * QB, QB)
        own = pl.ds(row, QB)
        both = o_s[own, :].astype(jnp.float32) * g_s[own, :].astype(jnp.float32)
        delta = lax.dot_general(
            pick, both, NT, precision=lax.Precision.HIGHEST, preferred_element_type=jnp.float32
        )
        for h in range(heads):
            columns = slice(h * QB, (h + 1) * QB)
            delta_s[0:1, columns] = delta[h : h + 1, :]
            row_s[0:1, columns] = lse_s[h : h + 1, own]
        qt_s[...] = _spread(q_s[own, :], heads)
        gt_s[...] = _spread(g_s[own, :], heads)
        qm_s[...] = _stack(q_s[own, :], heads)
        gm_s[...] = _stack(g_s[own, :], heads)

        def step(k, v, kt, allowed, fresh, targets):
            scores = _dot(k, qt_s[...], NN)
            probs_grad = _dot(v, gt_s[...], NN)
            probs = jnp.exp(scores - row_s[0:1, :])
            if allowed is not None:
                probs = jnp.where(allowed, probs, 0.0)
            ds = (probs * (probs_grad - delta_s[0:1, :])).astype(jnp.bfloat16)
            dv = _dot(probs.astype(jnp.bfloat16), gm_s[...], NN)
            dk = _dot(ds, qm_s[...], NN)
            for h in range(heads):
                of = slice(h * HDIM, (h + 1) * HDIM)
                term = _dot(kt(of), ds[:, h * QB : (h + 1) * QB], NN)
                acc_s[of, :] = term if fresh else acc_s[of, :] + term
            first = 0
            for at, size in targets:
                dv_s[pl.ds(at, size), :] += dv[first : first + size]
                dk_s[pl.ds(at, size), :] += dk[first : first + size]
                first += size

        step(
            k_s[own, :], v_s[own, :], lambda of: kt_s[of, own],
            _mask(heads, b >= trunk_blocks, True), True, [(row, QB)],
        )

        @pl.when(b >= leaf_block)
        def _():
            ats = _parents(info_ref, b)
            for side, at in enumerate(ats):
                part = slice(side * SEG, (side + 1) * SEG)
                kp_s[part, :] = k_s[pl.ds(at, SEG), :]
                vp_s[part, :] = v_s[pl.ds(at, SEG), :]
                kpt_s[:, part] = kt_s[:, pl.ds(at, SEG)]
            step(
                kp_s[...], vp_s[...], lambda of: kpt_s[of, :],
                _mask(heads, True, False), False, [(at, SEG) for at in ats],
            )

        def trunk_chunk(c, carry):
            at = pl.multiple_of(c * QB, QB)
            here = pl.ds(at, QB)
            step(k_s[here, :], v_s[here, :], lambda of: kt_s[of, here], None, False, [(at, QB)])
            return carry

        lax.fori_loop(0, jnp.minimum(b, trunk_blocks), trunk_chunk, 0)
        q_s[own, :] = (acc_s[...] * scale).T.astype(jnp.bfloat16)
        return carry

    lax.fori_loop(0, q_s.shape[0] // QB, q_block, 0)
    for j in range(n):
        rows_at = pl.ds(pl.multiple_of(piece_rows * lax.bitwise_xor(tensor, j), SEG), piece_rows)
        outs[j][:, :width] = q_s[rows_at, :]
        outs[j][:, width : 2 * width] = dk_s[rows_at, :].astype(jnp.bfloat16)
        outs[j][:, 2 * width :] = dv_s[rows_at, :].astype(jnp.bfloat16)


def attention_backward(info, pieces, mixed, grads, lses, heads):
    n = len(pieces)
    piece_rows = pieces[0].shape[0]
    rows = n * piece_rows
    width = heads * HDIM
    bf16, f32 = jnp.bfloat16, jnp.float32
    rows_low = pltpu.VMEM((rows, width), bf16)
    return pl.pallas_call(
        functools.partial(_attn_bwd_kernel, heads),
        out_shape=[jax.ShapeDtypeStruct((piece_rows, 3 * width), bf16)] * n,
        grid=(1,),
        in_specs=[_smem()] + [_full(v.shape) for v in (*pieces, *mixed, *grads, *lses)],
        out_specs=[_full((piece_rows, 3 * width))] * n,
        scratch_shapes=[
            rows_low,
            rows_low,
            pltpu.VMEM((width, rows), bf16),
            rows_low,
            rows_low,
            rows_low,
            pltpu.VMEM((rows, width), f32),
            pltpu.VMEM((rows, width), f32),
            pltpu.VMEM((8, rows), f32),
            pltpu.VMEM((width, heads * QB), bf16),
            pltpu.VMEM((width, heads * QB), bf16),
            pltpu.VMEM((heads * QB, width), bf16),
            pltpu.VMEM((heads * QB, width), bf16),
            pltpu.VMEM((8, heads * QB), f32),
            pltpu.VMEM((8, heads * QB), f32),
            pltpu.VMEM((width, QB), f32),
            pltpu.VMEM((QB, width), bf16),
            pltpu.VMEM((QB, width), bf16),
            pltpu.VMEM((width, QB), bf16),
        ],
        compiler_params=_params(),
        cost_estimate=_cost(rows * 1400 * width * 20, rows * width * 16),
        name="attn_bwd",
    )(info, *pieces, *mixed, *grads, *lses)


def mate(x):
    return lax.ppermute(x, "tensor", [(i, i ^ 1) for i in range(4)])


def across(x):
    return lax.ppermute(x, "tensor", [(i, i ^ 2) for i in range(4)])


def corner(x):
    return lax.ppermute(x, "tensor", [(i, i ^ 3) for i in range(4)])


def beside(x):
    return lax.ppermute(x, "dp", [(i, i ^ 1) for i in range(8)])


def ahead(x, step):
    return lax.ppermute(x, "dp", [(i, (i + 2 * step) % 8) for i in range(8)])


def after(x, *others):
    return lax.optimization_barrier((x, *others))[0]


def after_all(values, *others):
    return list(lax.optimization_barrier((*values, *others))[: len(values)])


def line_hops(x):
    return [x] + [ahead(x, step) for step in (1, 3, 2)]


def spread_hops(line, far):
    dp = lax.axis_index("dp")
    z, y = dp // 2, dp % 2
    order = jnp.array([0, 1, 3, 2], jnp.int32)
    from_z = (z - order) % 4
    where = jnp.concatenate([2 * from_z + y, 2 * from_z + 1 - y]).astype(jnp.int32)
    return place(where, line + far)


def fold_hops(near, passed):
    z = (lax.axis_index("dp") // 2).astype(jnp.int32)[None]
    return fold(z, near, passed)


def send_hops(chunks):
    return [chunks[0]] + [ahead(chunks[step], step) for step in (2, 1, 3)]


def sum_hops(received):
    return sum(v.astype(jnp.float32) for v in received)


def body(
    block_input,
    norm_gains,
    qkv_weight,
    out_weight,
    gate_up_weight,
    down_weight,
    parent_of_row,
    cotangent,
):
    bf16, f32 = jnp.bfloat16, jnp.float32
    shard = qkv_weight.shape[1]
    width = qkv_weight.shape[2]
    hidden_width = gate_up_weight.shape[2]
    heads = width // HDIM
    rows = parent_of_row.shape[0]
    tensor = lax.axis_index("tensor")
    chip = tensor // 2
    y = (lax.axis_index("dp") % 2).astype(jnp.int32)[None]
    leaf_first = TRUNK + 4 * SEG
    parents = parent_of_row[leaf_first::SEG]
    half_blocks = rows // (2 * QB)
    place_own = jnp.stack([tensor, half_blocks * chip]).astype(jnp.int32)
    place_far = jnp.stack([tensor, half_blocks * (1 - chip)]).astype(jnp.int32)
    info_own = jnp.concatenate([place_own, parents])
    info_far = jnp.concatenate([place_far, parents])

    half = block_input.shape[0] // 2
    gains_shard = jnp.pad(norm_gains.astype(bf16).T, ((0, 0), (0, SEG - 2)))
    qkv_shard = qkv_weight.astype(bf16).transpose(1, 0, 2).reshape(shard, 3 * width)
    out_shard = out_weight.astype(bf16).T
    gate_up_shard = gate_up_weight.astype(bf16).transpose(1, 0, 2).reshape(shard, 2 * hidden_width)
    first_line = line_hops(jnp.concatenate([qkv_shard, gains_shard], axis=1))
    beyond = [across(block_input[:half])]
    rest_shard = jnp.concatenate([gate_up_shard, out_shard, across(out_shard)], axis=1)
    rest = lax.all_gather(after(rest_shard, *first_line), "dp", axis=0, tiled=True)
    first_far = [beside(first_line[0])] + [beside(after(v, beyond[0])) for v in first_line[1:]]
    beyond.append(across(after(block_input[half:], beyond[0])))
    near_x = mate(block_input)
    first = spread_hops(first_line, first_far)
    down_line = line_hops(after(down_weight.astype(bf16).T, *first_far))
    gains_low = first[:, 3 * width : 3 * width + 2].T.astype(f32)
    gain_attn, gain_mlp = gains_low[0:1], gains_low[1:2]
    n0, n1, p0, p1 = project(block_input, near_x, gain_attn, first, 3 * width)
    beyond = jnp.concatenate([beyond[0], beyond[1]], axis=0)
    inputs = [block_input, near_x, beyond, mate(beyond)]
    n2, n3, p2, p3 = project(inputs[2], after(inputs[3], p1), gain_attn, first, 3 * width)
    normed_attn, projected = [n0, n1, n2, n3], [p0, p1, p2, p3]
    cot_low = cotangent.astype(bf16)
    cot_x = across(after(cot_low, beyond))

    own, lse_own = attention_forward(info_own, projected, heads)
    own_x, own_m = across(after(own, cot_x)), mate(own)
    down_far = [beside(after(v, own)) for v in down_line]
    cot_near = mate(after(cot_low, own))
    far, lse_far = attention_forward(after(info_far, own), projected, heads)
    far_m, own_xm = mate(far), mate(after(own_x, far))
    far_x = across(after(far, own_x))
    down_low = spread_hops(down_line, after_all(down_far, far))
    cot_rows = [cot_low, cot_near, cot_x, mate(after(cot_x, far))]
    out_far = mate(after(rest[:, 2 * hidden_width :], down_low))

    def run_mlp(attended, j, cot):
        return mlp(attended, inputs[j], cot, gain_mlp, rest, down_low, out_far, j == 0)

    stage = [None] * 4
    stage[3] = run_mlp([(far, 1), (far_m, 0), (own_x, 1), (own_xm, 0)], 3, cot_rows[3])
    stage[2] = run_mlp(
        [(far, 0), (far_m, 1), (own_x, 0), (own_xm, 1)], 2, after(cot_rows[2], stage[3][0])
    )
    far_xm = mate(after(far_x, stage[3][0]))
    passed = (stage[2][0].astype(f32) + mate(stage[3][0]).astype(f32)).astype(bf16)
    passed_x = [across(passed[:half])]
    stage[1] = run_mlp(
        [(own, 1), (own_m, 0), (far_x, 1), (far_xm, 0)], 1, after(cot_rows[1], passed)
    )
    passed_x.append(across(after(passed[half:], passed_x[0])))
    own_rows = [(own, 0), (own_m, 1), (far_x, 0), (far_xm, 1)]
    stage[0] = run_mlp(own_rows, 0, after(cot_rows[0], stage[1][0], passed_x[0]))
    part, hidden, grads_low, normed_mlp, branch = [[s[n] for s in stage] for n in range(5)]
    residual_mid = stage[0][5]
    mlp_parts = [part[0], mate(part[1]), jnp.concatenate(passed_x, axis=0)]

    mid_grad, attn_grad, g0, g1, g2, g3, mlp_sum = middle(
        mlp_parts, residual_mid, cotangent, gain_mlp, rest, out_far
    )
    g_x, g_c, g_m = across(g2), corner(g3), mate(g1)
    down_pair = row_grads([after(cot_low, attn_grad), *cot_rows[1:]], hidden, "down_grads", y, shard)
    down_y = beside(down_pair[1])
    gate_up_grad = row_grads(
        [after(normed_mlp[0], down_pair[1]), *normed_mlp[1:]], grads_low, "gate_up_grads"
    )
    gate_up_sum = lax.psum_scatter(gate_up_grad, "dp", scatter_dimension=0, tiled=True)
    down_chunks = fold_hops(down_pair[0], after(down_y, gate_up_grad))
    branch_passed = (branch[2].astype(f32) + mate(branch[3]).astype(f32)).astype(bf16)
    out_pair = out_grads(y, after(attn_grad, down_chunks[1]), own_rows, shard)
    out_y = beside(out_pair[1])
    branch_x = across(after(branch_passed, g_x, g_c))

    bwd_grads = after_all([g0, g_m, g_x, g_c], out_pair[1], branch_passed)
    projected_grad = attention_backward(
        info_own, projected, [own, far], bwd_grads, [lse_own, lse_far], heads
    )
    out_chunks = fold_hops(out_pair[0], after(out_y, *projected_grad))
    out_received = send_hops(out_chunks)
    down_received = send_hops(down_chunks)
    qkv_pair = qkv_grads(
        y, [after(normed_attn[0], out_chunks[1]), *normed_attn[1:]], projected_grad, first, gain_attn, mlp_sum, shard
    )
    qkv_y = beside(qkv_pair[1])
    back3 = project_back(after(projected_grad[3], qkv_pair[1], branch_x), first)
    back2 = project_back(projected_grad[2], first, mate(back3))
    back_x = [across(back2[:half])]
    back1 = project_back(after(projected_grad[1], back2, *out_received), first)
    back_m = mate(back1)
    back0 = project_back(after(projected_grad[0], back1), first)
    back_x.append(across(after(back2[half:], back_x[0])))
    branch_sum = branch[0].astype(f32) + mate(branch[1]).astype(f32)
    block_output = residual_mid + branch_sum + after(branch_x, back0).astype(f32)
    qkv_chunks = fold_hops(qkv_pair[0], after(qkv_y, back_x[0], block_output))
    qkv_received = send_hops(qkv_chunks)
    down_out = sum_hops(after_all(down_received, qkv_chunks[1])).T
    gate_up_out = (
        after(gate_up_sum, qkv_chunks[1]).astype(f32).reshape(shard, 2, hidden_width).transpose(1, 0, 2)
    )
    out_sum = sum_hops(after_all(out_received, qkv_chunks[1]))
    quarter = lambda i: out_sum[:, i * width : (i + 1) * width]
    from_mate = mate(jnp.concatenate([quarter(1), quarter(3)], axis=1).astype(bf16)).astype(f32)
    out_out = quarter(0) + from_mate[:, :width]
    out_x = across((quarter(2) + from_mate[:, width:]).astype(bf16))
    out_out = (out_out + out_x.astype(f32)).T
    back_x = jnp.concatenate([back_x[0], after(back_x[1], out_x, gate_up_out, down_out)], axis=0)
    input_grad = last([back0, back_m, back_x], block_input, mid_grad, gain_attn)
    qkv_sum = sum_hops(after_all(qkv_received, input_grad))
    qkv_out = qkv_sum[:, : 3 * width].reshape(shard, 3, width).transpose(1, 0, 2)
    gains_out = qkv_sum[:, 3 * width :]
    gains_out = gains_out + mate(gains_out.astype(bf16)).astype(f32)
    gains_out = (gains_out + across(gains_out.astype(bf16)).astype(f32))[:, :2].T
    return (block_output, input_grad, gains_out, qkv_out, out_out, gate_up_out, down_out)


def solution(mesh):
    placed = (
        P(("dp", "tensor"), None),
        P(None, "dp"),
        P(None, "dp", "tensor"),
        P("tensor", "dp"),
        P(None, "dp", "tensor"),
        P("tensor", "dp"),
        P("dp"),
        P(("dp", "tensor"), None),
    )
    four_by_eight = mesh.shape["tensor"] == 4 and mesh.shape["dp"] == 8
    return jax.shard_map(
        body if four_by_eight else body_any_mesh,
        mesh=mesh,
        in_specs=placed,
        out_specs=(
            P(("dp", "tensor"), None),
            P(("dp", "tensor"), None),
            P(None, "dp"),
            P(None, "dp", "tensor"),
            P("tensor", "dp"),
            P(None, "dp", "tensor"),
            P("tensor", "dp"),
        ),
        check_vma=False,
    )
```

```python
import functools
import jax
import jax.numpy as jnp
from jax import lax
from jax.experimental import pallas as pl
from jax.experimental.pallas import tpu as pltpu
from jax.sharding import PartitionSpec as P

HDIM = 64
TRUNK = 1024
SEG = 128
ROW_TREE = 2560


epsilon = 1e-06


def norm_rows(values, gain_row):
    inverse_rms = lax.rsqrt(jnp.mean(values * values, axis=-1, keepdims=True) + epsilon)
    return values * inverse_rms * gain_row


def segment_ids(row_count):
    position = jnp.arange(row_count, dtype=jnp.int32)
    tree_base = position // ROW_TREE * 13
    within = position % ROW_TREE
    beyond = within - TRUNK
    own_segment = jnp.where(
        within < TRUNK,
        0,
        jnp.where(beyond < 4 * SEG, 1 + beyond // SEG, 5 + (beyond - 4 * SEG) // SEG),
    )
    return (own_segment + tree_base, tree_base)


def body_any_mesh(
    block_input,
    norm_gains,
    qkv_weight,
    out_weight,
    gate_up_weight,
    down_weight,
    parent_of_row,
    cotangent,
):
    gains_cast = norm_gains.astype(jnp.bfloat16)
    qkv_cast = qkv_weight.astype(jnp.bfloat16)
    out_cast = out_weight.astype(jnp.bfloat16)
    gate_up_cast = gate_up_weight.astype(jnp.bfloat16)
    down_cast = down_weight.astype(jnp.bfloat16)
    gains_low, qkv_low, out_low, gate_up_low, down_low = (
        lax.all_gather(gains_cast, "dp", axis=1, tiled=True),
        lax.all_gather(qkv_cast, "dp", axis=1, tiled=True),
        lax.all_gather(out_cast, "dp", axis=1, tiled=True),
        lax.all_gather(gate_up_cast, "dp", axis=1, tiled=True),
        lax.all_gather(down_cast, "dp", axis=1, tiled=True),
    )
    row_count = parent_of_row.shape[0]
    width_local = qkv_low.shape[2]
    head_local = width_local // HDIM
    block_rows = min(512, row_count)
    block_count = row_count // block_rows
    score_scale = float(HDIM) ** (-0.5)
    segment_of_row, trunk_of_row = segment_ids(row_count)
    parent_segment = parent_of_row + trunk_of_row
    column_index = jnp.arange(row_count, dtype=jnp.int32)
    residual_in = block_input.astype(jnp.float32)
    gain_attn = gains_low[0].astype(jnp.float32)
    gain_mlp = gains_low[1].astype(jnp.float32)
    normed_attn = lax.all_gather(
        norm_rows(residual_in, gain_attn).astype(jnp.bfloat16), "tensor", axis=0, tiled=True
    )
    projected = jnp.einsum(
        "rd,cde->cre", normed_attn, qkv_low, preferred_element_type=jnp.float32
    ).astype(jnp.bfloat16)
    query_rows = projected[0].reshape(row_count, head_local, HDIM)
    key_rows = projected[1].reshape(row_count, head_local, HDIM)
    value_rows = projected[2].reshape(row_count, head_local, HDIM)

    def block_scores(block_index):
        row_start = block_index * block_rows
        query_block = lax.dynamic_slice_in_dim(query_rows, row_start, block_rows, 0)
        scores = (
            jnp.einsum("qhd,khd->hqk", query_block, key_rows, preferred_element_type=jnp.float32)
            * score_scale
        )
        row_index = row_start + jnp.arange(block_rows, dtype=jnp.int32)
        row_segment = lax.dynamic_slice_in_dim(segment_of_row, row_start, block_rows, 0)
        row_parent = lax.dynamic_slice_in_dim(parent_segment, row_start, block_rows, 0)
        row_trunk = lax.dynamic_slice_in_dim(trunk_of_row, row_start, block_rows, 0)
        column_segment = segment_of_row[None, :]
        allowed = (column_index[None, :] <= row_index[:, None]) & (
            (column_segment == row_segment[:, None])
            | (column_segment == row_parent[:, None])
            | (column_segment == row_trunk[:, None])
        )
        return (jnp.where(allowed[None], scores, -1e30), query_block)

    def attend_block(block_index):
        scores, query_block = block_scores(block_index)
        top_score = jnp.max(scores, axis=-1, keepdims=True)
        exp_scores = jnp.exp(scores - top_score)
        row_total = jnp.sum(exp_scores, axis=-1, keepdims=True)
        softmax_low = (exp_scores / row_total).astype(jnp.bfloat16)
        mixed_heads = jnp.einsum(
            "hqk,khd->qhd", softmax_low, value_rows, preferred_element_type=jnp.float32
        ).astype(jnp.bfloat16)
        return (mixed_heads, (top_score + jnp.log(row_total))[..., 0])

    block_ids = jnp.arange(block_count, dtype=jnp.int32)
    attended, log_totals = lax.map(attend_block, block_ids)
    attended = attended.reshape(row_count, width_local)
    attn_partial = jnp.dot(attended, out_low, preferred_element_type=jnp.float32)
    residual_mid = residual_in + lax.psum_scatter(
        attn_partial, "tensor", scatter_dimension=0, tiled=True
    )
    normed_mlp = lax.all_gather(
        norm_rows(residual_mid, gain_mlp).astype(jnp.bfloat16), "tensor", axis=0, tiled=True
    )
    gate_up = jnp.einsum(
        "rd,cdf->crf", normed_mlp, gate_up_low, preferred_element_type=jnp.float32
    ).astype(jnp.bfloat16)
    gate_value = gate_up[0].astype(jnp.float32)
    up_value = gate_up[1].astype(jnp.float32)
    sigmoid_gate = jax.nn.sigmoid(gate_value)
    hidden = (gate_value * sigmoid_gate * up_value).astype(jnp.bfloat16)
    mlp_partial = jnp.dot(hidden, down_low, preferred_element_type=jnp.float32)
    block_output = residual_mid + lax.psum_scatter(
        mlp_partial.astype(jnp.bfloat16), "tensor", scatter_dimension=0, tiled=True
    ).astype(jnp.float32)
    gains_again = norm_gains.astype(jnp.bfloat16)
    qkv_again = qkv_weight.astype(jnp.bfloat16)
    out_again = out_weight.astype(jnp.bfloat16)
    gate_up_again = gate_up_weight.astype(jnp.bfloat16)
    down_again = down_weight.astype(jnp.bfloat16)
    gains_low, qkv_low, out_low, gate_up_low, down_low = (
        lax.all_gather(gains_again, "dp", axis=1, tiled=True),
        lax.all_gather(qkv_again, "dp", axis=1, tiled=True),
        lax.all_gather(out_again, "dp", axis=1, tiled=True),
        lax.all_gather(gate_up_again, "dp", axis=1, tiled=True),
        lax.all_gather(down_again, "dp", axis=1, tiled=True),
    )
    gain_attn = gains_low[0].astype(jnp.float32)
    gain_mlp = gains_low[1].astype(jnp.float32)
    mlp_grad_rows = lax.all_gather(cotangent.astype(jnp.bfloat16), "tensor", axis=0, tiled=True)
    down_grad = jnp.einsum("rf,rd->fd", hidden, mlp_grad_rows, preferred_element_type=jnp.float32)
    hidden_grad = jnp.einsum(
        "rd,fd->rf", mlp_grad_rows, down_low, preferred_element_type=jnp.float32
    )
    gate_grad = hidden_grad * up_value * sigmoid_gate * (1.0 + gate_value * (1.0 - sigmoid_gate))
    up_grad = hidden_grad * gate_value * sigmoid_gate
    gate_up_grad_low = jnp.stack([gate_grad, up_grad]).astype(jnp.bfloat16)
    gate_up_grad = jnp.einsum(
        "rd,crf->cdf", normed_mlp, gate_up_grad_low, preferred_element_type=jnp.float32
    )
    normed_mlp_part = jnp.einsum(
        "crf,cdf->rd", gate_up_grad_low, gate_up_low, preferred_element_type=jnp.float32
    )
    normed_mlp_grad = lax.psum_scatter(normed_mlp_part, "tensor", scatter_dimension=0, tiled=True)
    norm_back_mlp = jax.vjp(norm_rows, residual_mid, gain_mlp)[1]
    mid_from_norm, gain_mlp_grad = norm_back_mlp(normed_mlp_grad)
    mid_grad = cotangent + mid_from_norm
    attn_grad_rows = lax.all_gather(mid_grad.astype(jnp.bfloat16), "tensor", axis=0, tiled=True)
    out_grad = jnp.einsum("re,rd->ed", attended, attn_grad_rows, preferred_element_type=jnp.float32)
    attended_grad = jnp.einsum(
        "rd,ed->re", attn_grad_rows, out_low, preferred_element_type=jnp.float32
    ).astype(jnp.bfloat16)
    attended_grad = attended_grad.reshape(row_count, head_local, HDIM)

    def back_block(carry, block_inputs):
        key_grad, value_grad = carry
        block_index, log_total = block_inputs
        scores, query_block = block_scores(block_index)
        probs = jnp.exp(scores - log_total[..., None])
        grad_block = lax.dynamic_slice_in_dim(
            attended_grad, block_index * block_rows, block_rows, 0
        )
        probs_grad = jnp.einsum(
            "qhd,khd->hqk", grad_block, value_rows, preferred_element_type=jnp.float32
        )
        inner_term = jnp.sum(probs * probs_grad, axis=-1, keepdims=True)
        score_grad = (probs * (probs_grad - inner_term)).astype(jnp.bfloat16)
        query_grad = (
            jnp.einsum("hqk,khd->qhd", score_grad, key_rows, preferred_element_type=jnp.float32)
            * score_scale
        )
        key_grad = (
            key_grad
            + jnp.einsum(
                "hqk,qhd->khd", score_grad, query_block, preferred_element_type=jnp.float32
            )
            * score_scale
        )
        value_grad = value_grad + jnp.einsum(
            "hqk,qhd->khd",
            probs.astype(jnp.bfloat16),
            grad_block,
            preferred_element_type=jnp.float32,
        )
        return ((key_grad, value_grad), query_grad)

    zero_grad = jnp.zeros((row_count, head_local, HDIM), jnp.float32)
    carried, query_grads = lax.scan(back_block, (zero_grad, zero_grad), (block_ids, log_totals))
    projected_grad = jnp.stack(
        [
            query_grads.reshape(row_count, width_local),
            carried[0].reshape(row_count, width_local),
            carried[1].reshape(row_count, width_local),
        ]
    ).astype(jnp.bfloat16)
    qkv_grad = jnp.einsum(
        "rd,cre->cde", normed_attn, projected_grad, preferred_element_type=jnp.float32
    )
    normed_attn_part = jnp.einsum(
        "cre,cde->rd", projected_grad, qkv_low, preferred_element_type=jnp.float32
    )
    normed_attn_grad = lax.psum_scatter(
        normed_attn_part.astype(jnp.bfloat16), "tensor", scatter_dimension=0, tiled=True
    ).astype(jnp.float32)
    norm_back_attn = jax.vjp(norm_rows, residual_in, gain_attn)[1]
    input_from_norm, gain_attn_grad = norm_back_attn(normed_attn_grad)
    input_grad = mid_grad + input_from_norm
    gain_grads = lax.psum(jnp.stack([gain_attn_grad, gain_mlp_grad]), "tensor")
    gains_out, qkv_out, out_out, gate_up_out, down_out = (
        lax.psum_scatter(
            gain_grads.astype(jnp.bfloat16), "dp", scatter_dimension=1, tiled=True
        ).astype(jnp.float32),
        lax.psum_scatter(
            qkv_grad.astype(jnp.bfloat16), "dp", scatter_dimension=1, tiled=True
        ).astype(jnp.float32),
        lax.psum_scatter(
            out_grad.astype(jnp.bfloat16), "dp", scatter_dimension=1, tiled=True
        ).astype(jnp.float32),
        lax.psum_scatter(
            gate_up_grad.astype(jnp.bfloat16), "dp", scatter_dimension=1, tiled=True
        ).astype(jnp.float32),
        lax.psum_scatter(
            down_grad.astype(jnp.bfloat16), "dp", scatter_dimension=1, tiled=True
        ).astype(jnp.float32),
    )
    return (block_output, input_grad, gains_out, qkv_out, out_out, gate_up_out, down_out)


QB = 256
NT = (((1,), (1,)), ((), ()))
NN = (((1,), (0,)), ((), ()))
TN = (((0,), (0,)), ((), ()))


def _dot(a, b, dims):
    return lax.dot_general(a, b, dims, preferred_element_type=jnp.float32)


def _stacked(tile, columns, n):
    return pl.BlockSpec((1, tile, columns), lambda i: (n, i, 0))


def _full(shape):
    return pl.BlockSpec(shape, lambda i: (0,) * len(shape))


def _smem():
    return pl.BlockSpec(memory_space=pltpu.SMEM)


def _rows(tile, columns):
    return pl.BlockSpec((tile, columns), lambda i: (i, 0))


def _params():
    return pltpu.CompilerParams(dimension_semantics=("arbitrary",), vmem_limit_bytes=60 << 20)


STRETCH = 6.0


def _cost(flops, bytes_accessed):
    return pl.CostEstimate(
        flops=int(flops * STRETCH), bytes_accessed=int(bytes_accessed * STRETCH), transcendentals=0
    )


def _row_tile(rows):
    return rows // 2 if rows % 32 == 0 else rows


def _normed(values):
    inverse_rms = lax.rsqrt(jnp.mean(values * values, axis=-1, keepdims=True) + epsilon)
    return inverse_rms, values * inverse_rms


def _place_kernel(where_ref, *refs):
    shards, out = refs[:-1], refs[-1]
    size = shards[0].shape[0]
    for n, shard in enumerate(shards):
        out[pl.ds(pl.multiple_of(where_ref[n] * size, size), size), :] = shard[...]


def place(where, shards):
    size, columns = shards[0].shape
    return pl.pallas_call(
        _place_kernel,
        grid=(1,),
        out_shape=jax.ShapeDtypeStruct((size * len(shards), columns), shards[0].dtype),
        in_specs=[_smem()] + [_full((size, columns))] * len(shards),
        out_specs=_full((size * len(shards), columns)),
        compiler_params=_params(),
        cost_estimate=_cost(0, 4 * size * columns * len(shards)),
        name="place",
    )(where, *shards)


def _project_kernel(x0_ref, x1_ref, gain_ref, w_ref, n0_ref, n1_ref, p0_ref, p1_ref):
    def run(x_ref, normed_ref, out_ref):
        normed = (_normed(x_ref[...].astype(jnp.float32))[1] * gain_ref[...]).astype(jnp.bfloat16)
        normed_ref[...] = normed
        out_ref[...] = _dot(normed, w_ref[...], NN).astype(jnp.bfloat16)

    half = pl.num_programs(0) // 2

    @pl.when(pl.program_id(0) < half)
    def _():
        run(x0_ref, n0_ref, p0_ref)

    @pl.when(pl.program_id(0) >= half)
    def _():
        run(x1_ref, n1_ref, p1_ref)


def project(x0, x1, gain, weight, columns):
    rows, depth = x0.shape
    tile = _row_tile(rows)
    steps = rows // tile
    early = lambda c: pl.BlockSpec((tile, c), lambda i: (jnp.minimum(i, steps - 1), 0))
    late = lambda c: pl.BlockSpec((tile, c), lambda i: (jnp.maximum(i - steps, 0), 0))
    out = lambda c: jax.ShapeDtypeStruct((rows, c), jnp.bfloat16)
    return pl.pallas_call(
        _project_kernel,
        grid=(2 * steps,),
        out_shape=[out(depth), out(depth), out(columns), out(columns)],
        in_specs=[early(depth), late(depth), _full((1, depth)), _full((depth, columns))],
        out_specs=[early(depth), late(depth), early(columns), late(columns)],
        compiler_params=_params(),
        cost_estimate=_cost(4 * rows * depth * columns, 4 * rows * (2 * depth + columns)),
        name="project",
    )(x0, x1, gain, weight)


def _mlp_kernel(keep, *refs):
    att_a, att_b, (xa, xb, ca, cb) = refs[:4], refs[4:8], refs[8:12]
    gain_ref, w_hbm, d_hbm, m_hbm = refs[12:16]
    hidden_ref, grad_ref, normed_ref = refs[16:19]
    part_a, part_b, branch_a, branch_b = refs[19:23]
    att_s, x_s, cot_s, o_s, w_s, d_s, sems = refs[-7:]
    width = att_a[0].shape[2]
    count = hidden_ref.shape[2]
    pulls = [
        pltpu.make_async_copy(
            w_hbm.at[:, pl.ds(2 * count, 2 * width)], o_s.at[:, pl.ds(0, 2 * width)], sems.at[0]
        ),
        pltpu.make_async_copy(m_hbm, o_s.at[:, pl.ds(2 * width, 2 * width)], sems.at[1]),
        pltpu.make_async_copy(w_hbm.at[:, pl.ds(0, 2 * count)], w_s, sems.at[2]),
        pltpu.make_async_copy(d_hbm, d_s, sems.at[3]),
    ]
    first = pl.program_id(0) == 0
    late = pl.program_id(0) >= pl.num_programs(0) // 2

    @pl.when(first)
    def _():
        for pull in pulls:
            pull.start()

    def take(att, x_ref, cot_ref):
        for i, of in enumerate((0, 2, 1, 3)):
            att_s[:, i * width : (i + 1) * width] = att[of][0]
        x_s[...] = x_ref[...]
        cot_s[...] = cot_ref[...]

    @pl.when(jnp.logical_not(late))
    def _():
        take(att_a, xa, ca)

    @pl.when(late)
    def _():
        take(att_b, xb, cb)

    @pl.when(first)
    def _():
        for pull in pulls[:2]:
            pull.wait()

    residual = x_s[...].astype(jnp.float32) + _dot(att_s[...], o_s[...], NT)
    if keep:
        keep_ref = refs[23]

        @pl.when(late)
        def _():
            keep_ref[...] = residual

    normed_ref[0] = (_normed(residual)[1] * gain_ref[...]).astype(jnp.bfloat16)

    @pl.when(first)
    def _():
        for pull in pulls[2:]:
            pull.wait()

    both = _dot(normed_ref[0], w_s[...], NN).astype(jnp.bfloat16).astype(jnp.float32)
    gate, up = both[:, :count], both[:, count:]
    hidden_grad = _dot(cot_s[...], d_s[...], NN)
    sig = 0.5 * jnp.tanh(0.5 * gate) + 0.5
    act = gate * sig
    hidden = (act * up).astype(jnp.bfloat16)
    hidden_ref[0] = hidden
    grad_ref[0, :, :count] = (hidden_grad * up * (sig + act * (1.0 - sig))).astype(jnp.bfloat16)
    grad_ref[0, :, count:] = (hidden_grad * act).astype(jnp.bfloat16)
    part = _dot(grad_ref[0], w_s[...], NT).astype(jnp.bfloat16)
    branch = _dot(hidden, d_s[...], NT).astype(jnp.bfloat16)

    @pl.when(jnp.logical_not(late))
    def _():
        part_a[...] = part
        branch_a[...] = branch

    @pl.when(late)
    def _():
        part_b[...] = part
        branch_b[...] = branch


def mlp(attended_a, attended_b, x, cot, gain, weights, down, out_mate, keep):
    rows, depth = x[0].shape
    width = attended_a[0][0].shape[2]
    count = down.shape[1]
    tile = _row_tile(rows)
    steps = rows // tile
    bf16, f32 = jnp.bfloat16, jnp.float32
    early = lambda i: jnp.minimum(i, steps - 1)
    late = lambda i: jnp.maximum(i - steps, 0)
    rows_of = lambda where: pl.BlockSpec((tile, depth), lambda i: (where(i), 0))
    stack = lambda c: pl.BlockSpec((1, tile, c), lambda i: (i // steps, i % steps, 0))
    member = lambda n, where: pl.BlockSpec((1, tile, width), lambda i: (n, where(i), 0))
    outs = [jax.ShapeDtypeStruct((2, rows, c), bf16) for c in (count, 2 * count, depth)]
    outs += [jax.ShapeDtypeStruct((rows, depth), bf16)] * 4
    out_specs = [stack(count), stack(2 * count), stack(depth)] + [rows_of(early), rows_of(late)] * 2
    if keep:
        outs.append(jax.ShapeDtypeStruct((rows, depth), f32))
        out_specs.append(rows_of(late))
    anywhere = pl.BlockSpec(memory_space=pl.ANY)
    return pl.pallas_call(
        functools.partial(_mlp_kernel, keep),
        grid=(2 * steps,),
        out_shape=outs,
        in_specs=[member(n, early) for v, n in attended_a]
        + [member(n, late) for v, n in attended_b]
        + [rows_of(early), rows_of(late)] * 2
        + [_full((1, depth)), anywhere, anywhere, anywhere],
        out_specs=out_specs,
        scratch_shapes=[
            pltpu.VMEM((tile, 4 * width), bf16),
            pltpu.VMEM((tile, depth), bf16),
            pltpu.VMEM((tile, depth), bf16),
            pltpu.VMEM((depth, 4 * width), bf16),
            pltpu.VMEM((depth, 2 * count), bf16),
            pltpu.VMEM((depth, count), bf16),
            pltpu.SemaphoreType.DMA((4,)),
        ],
        compiler_params=_params(),
        cost_estimate=_cost(4 * rows * depth * (4 * width + 6 * count), 28 << 20),
        name="mlp",
    )(*[v for v, n in (*attended_a, *attended_b)], *x, *cot, gain, weights, down, out_mate)


def _pull_groups(right, right_s, row_at, column_at, step, sems, base):
    groups = []
    for c in range(right[0].shape[-1] // step):
        group = []
        at = row_at
        for j, piece in enumerate(right):
            rows = piece.shape[0]
            group.append(
                pltpu.make_async_copy(
                    piece.at[:, pl.ds(c * step, step)],
                    right_s.at[pl.ds(at, rows), pl.ds(column_at + c * step, step)],
                    sems.at[base + c * len(right) + j],
                )
            )
            at += rows
        groups.append(group)
    return groups


def _start_all(groups):
    @pl.when(pl.program_id(0) == 0)
    def _():
        for group in groups:
            for pull in group:
                pull.start()


def _wait_group(group):
    @pl.when(pl.program_id(0) == 0)
    def _():
        for pull in group:
            pull.wait()


def _join(pieces, out):
    at = 0
    for piece in pieces:
        rows = piece.shape[0]
        out[at : at + rows, :] = piece[...]
        at += rows


def _mlp_grad_kernel(n, step, *refs):
    normed, cot = refs[:2], refs[2 : 2 + n]
    grads, hidden = refs[2 + n : 4 + n], refs[4 + n : 6 + n]
    out_ref, left_s, right_s, sems = refs[6 + n :]
    members = lambda pair: [v.at[m] for v in pair for m in (0, 1)]
    wide = grads[0].shape[2]
    rows = left_s.shape[0] // n
    groups = _pull_groups(members(grads), right_s, 0, 0, step, sems, 0)
    groups += _pull_groups(members(hidden), right_s, 0, wide, step, sems, 4 * (wide // step))
    _start_all(groups)
    for m in range(n):
        left_s[m * rows : (m + 1) * rows, :] = normed[m // 2][m % 2]
    for c, group in enumerate(groups):
        at = slice(c * step, (c + 1) * step)
        if c * step == wide:
            _join(cot, left_s)
        _wait_group(group)
        out_ref[:, at] = _dot(left_s[...], right_s[:, at], TN).astype(out_ref.dtype)


def mlp_grads(normed, cot, grads, hidden, block=256):
    n = len(cot)
    piece, depth = cot[0].shape
    rows = n * piece
    columns = grads[0].shape[2] + hidden[0].shape[2]
    step = hidden[0].shape[2]
    anywhere = pl.BlockSpec(memory_space=pl.ANY)
    return pl.pallas_call(
        functools.partial(_mlp_grad_kernel, n, step),
        grid=(depth // block,),
        out_shape=jax.ShapeDtypeStruct((depth, columns), jnp.bfloat16),
        in_specs=[pl.BlockSpec((2, piece, block), lambda i: (0, 0, i))] * 2
        + [pl.BlockSpec((piece, block), lambda i: (0, i))] * n
        + [anywhere] * 4,
        out_specs=_rows(block, columns),
        scratch_shapes=[
            pltpu.VMEM((rows, block), jnp.bfloat16),
            pltpu.VMEM((rows, columns), jnp.bfloat16),
            pltpu.SemaphoreType.DMA((n * (columns // step),)),
        ],
        compiler_params=_params(),
        cost_estimate=_cost(2 * rows * depth * columns, 2 * rows * (depth + columns) + 2 * depth * columns),
        name="mlp_grads",
    )(*normed, *cot, *grads, *hidden)


def _split_rows(acc, y, near, far):
    size = near.shape[1]
    near[...] = acc[pl.ds(pl.multiple_of(y * size, size), size), :].astype(near.dtype)[None]
    far[...] = acc[pl.ds(pl.multiple_of((1 - y) * size, size), size), :].astype(far.dtype)[None]


def _qkv_grad_kernel(n, y_ref, *refs):
    left, right = refs[:n], refs[n : 2 * n]
    w_ref, gain_ref, row_ref, near, far, left_s, right_s, acc, sems = refs[2 * n :]
    columns = right_s.shape[1]
    groups = _pull_groups(right, right_s, 0, 0, columns, sems, 0)
    _start_all(groups)
    _join(left, left_s)
    _wait_group(groups[0])
    total = _dot(left_s[...], right_s[...], TN)
    acc[:, :columns] = total
    row = jnp.concatenate(
        [1.0 / gain_ref[...], row_ref[...], jnp.zeros((SEG - 9, row_ref.shape[1]), jnp.float32)], axis=0
    ).T
    attn = jnp.sum(total * w_ref[...].astype(jnp.float32), axis=-1, keepdims=True) * row[:, 0:1]
    lane = lax.broadcasted_iota(jnp.int32, row.shape, 1)
    acc[:, columns:] = jnp.where(lane == 0, attn, row)
    _split_rows(acc, y_ref[0], near, far)


def qkv_grads(y, normed, grads, weight, gain, mlp_sum, size):
    n, depth = len(normed), normed[0].shape[1]
    rows = sum(v.shape[0] for v in normed)
    columns = grads[0].shape[1]
    block = 2 * size
    anywhere = pl.BlockSpec(memory_space=pl.ANY)
    out = jax.ShapeDtypeStruct((depth // block, size, columns + SEG), jnp.bfloat16)
    out_spec = pl.BlockSpec((1, size, columns + SEG), lambda i: (i, 0, 0))
    lanes = lambda r: pl.BlockSpec((r, block), lambda i: (0, i))
    return pl.pallas_call(
        functools.partial(_qkv_grad_kernel, n),
        grid=(depth // block,),
        out_shape=[out, out],
        in_specs=[_smem()]
        + [lanes(v.shape[0]) for v in normed]
        + [anywhere] * n
        + [_rows(block, columns), lanes(1), lanes(8)],
        out_specs=[out_spec, out_spec],
        scratch_shapes=[
            pltpu.VMEM((rows, block), jnp.bfloat16),
            pltpu.VMEM((rows, columns), jnp.bfloat16),
            pltpu.VMEM((block, columns + SEG), jnp.float32),
            pltpu.SemaphoreType.DMA((n,)),
        ],
        compiler_params=_params(),
        cost_estimate=_cost(0, 0),
        name="qkv_grads",
    )(y, *normed, *grads, weight, gain, mlp_sum)


def _out_grad_kernel(left_ref, a0, a1, a2, a3, mine, theirs, right_s):
    width = a0.shape[2]

    @pl.when(pl.program_id(0) == 0)
    def _():
        for i, a in enumerate((a0, a2, a1, a3)):
            right_s[:, i * width : (i + 1) * width] = a[0]

    total = _dot(left_ref[...], right_s[...], TN).astype(mine.dtype)
    mine[...] = total[:, : 2 * width]
    theirs[...] = total[:, 2 * width :]


def out_grads(left, attended, block=256):
    rows, depth = left.shape
    width = attended[0][0].shape[2]
    out = jax.ShapeDtypeStruct((depth, 2 * width), jnp.bfloat16)
    member = lambda n: pl.BlockSpec((1, rows, width), lambda i: (n, 0, 0))
    return pl.pallas_call(
        _out_grad_kernel,
        grid=(depth // block,),
        out_shape=[out, out],
        in_specs=[pl.BlockSpec((rows, block), lambda i: (0, i))] + [member(n) for v, n in attended],
        out_specs=[_rows(block, 2 * width)] * 2,
        scratch_shapes=[pltpu.VMEM((rows, 4 * width), jnp.bfloat16)],
        compiler_params=_params(),
        cost_estimate=_cost(8 * rows * depth * width, 2 * rows * (depth + 4 * width) + 8 * depth * width),
        name="out_grads",
    )(left, *[v for v, n in attended])


def _pair_kernel(y_ref, a_ref, b_ref, near, far, acc):
    acc[...] = a_ref[...].astype(jnp.float32) + b_ref[...].astype(jnp.float32)
    _split_rows(acc, y_ref[0], near, far)


def pair_sum(y, a, b, size):
    depth, columns = a.shape
    block = 2 * size
    out = jax.ShapeDtypeStruct((depth // block, size, columns), jnp.bfloat16)
    out_spec = pl.BlockSpec((1, size, columns), lambda i: (i, 0, 0))
    return pl.pallas_call(
        _pair_kernel,
        grid=(depth // block,),
        out_shape=[out, out],
        in_specs=[_smem()] + [_rows(block, columns)] * 2,
        out_specs=[out_spec, out_spec],
        scratch_shapes=[pltpu.VMEM((block, columns), jnp.float32)],
        compiler_params=_params(),
        cost_estimate=_cost(0, 6 * depth * columns),
        name="pair_sum",
    )(y, a, b)


def _fold_kernel(z_ref, near, passed, *outs):
    count = near.shape[0]
    for step, out in enumerate(outs):
        row = lax.rem(z_ref[0] + step, count)
        out[...] = (near[row].astype(jnp.float32) + passed[row].astype(jnp.float32)).astype(out.dtype)


def fold(z, near, passed):
    count, size, columns = near.shape
    return pl.pallas_call(
        _fold_kernel,
        grid=(1,),
        out_shape=[jax.ShapeDtypeStruct((size, columns), jnp.bfloat16)] * count,
        in_specs=[_smem(), _full(near.shape), _full(near.shape)],
        out_specs=[_full((size, columns))] * count,
        compiler_params=_params(),
        cost_estimate=_cost(0, 0),
        name="fold",
    )(z, near, passed)


def _mid_kernel(p0, p1, p2, res_ref, cot_ref, gain_ref, near_ref, mate_ref, mid_ref, attn_ref, a0, a1, a2, a3, sum_ref):
    width = a0.shape[1]
    grad = p0[...].astype(jnp.float32) + p1[...].astype(jnp.float32) + p2[...].astype(jnp.float32)
    inverse, normed = _normed(res_ref[...])
    term = jnp.sum(grad * normed, axis=0, keepdims=True)

    @pl.when(pl.program_id(0) == 0)
    def _():
        sum_ref[...] = jnp.zeros_like(sum_ref)

    sum_ref[0:1, :] += term
    scaled = grad * gain_ref[...]
    mid = cot_ref[...] + inverse * (scaled - normed * jnp.mean(scaled * normed, axis=-1, keepdims=True))
    mid_ref[...] = mid
    low = mid.astype(jnp.bfloat16)
    attn_ref[...] = low
    a0[...] = _dot(low, near_ref[:, :width], NN).astype(jnp.bfloat16)
    a1[...] = _dot(low, mate_ref[:, :width], NN).astype(jnp.bfloat16)
    a2[...] = _dot(low, near_ref[:, width : 2 * width], NN).astype(jnp.bfloat16)
    a3[...] = _dot(low, mate_ref[:, width:], NN).astype(jnp.bfloat16)


def middle(parts, residual, cot, gain, weights, out_mate):
    rows, depth = residual.shape
    width = out_mate.shape[1] // 2
    tile = _row_tile(rows)
    return pl.pallas_call(
        _mid_kernel,
        grid=(rows // tile,),
        out_shape=[
            jax.ShapeDtypeStruct((rows, depth), jnp.float32),
            jax.ShapeDtypeStruct((rows, depth), jnp.bfloat16),
        ]
        + [jax.ShapeDtypeStruct((rows, width), jnp.bfloat16)] * 4
        + [jax.ShapeDtypeStruct((8, depth), jnp.float32)],
        in_specs=[_rows(tile, depth)] * 5
        + [
            _full((1, depth)),
            pl.BlockSpec((depth, 2 * width), lambda i: (0, weights.shape[1] // (2 * width) - 1)),
            _full(out_mate.shape),
        ],
        out_specs=[_rows(tile, depth)] * 2 + [_rows(tile, width)] * 4 + [_full((8, depth))],
        compiler_params=_params(),
        cost_estimate=_cost(2 * rows * depth * 4 * width, rows * depth * 20),
        name="middle",
    )(*parts, residual, cot, gain, weights, out_mate)


def _back_kernel(add, grad_ref, w_ref, *refs):
    part = _dot(grad_ref[...], w_ref[...], NT)
    if add:
        part = part + refs[0][...].astype(jnp.float32)
    refs[-1][...] = part.astype(refs[-1].dtype)


def project_back(grad, weight, add=None):
    rows, columns = grad.shape
    depth = weight.shape[0]
    tile = _row_tile(rows)
    extra = [] if add is None else [add]
    return pl.pallas_call(
        functools.partial(_back_kernel, add is not None),
        grid=(rows // tile,),
        out_shape=jax.ShapeDtypeStruct((rows, depth), jnp.bfloat16),
        in_specs=[_rows(tile, columns), _full((depth, columns))] + [_rows(tile, depth)] * len(extra),
        out_specs=_rows(tile, depth),
        compiler_params=_params(),
        cost_estimate=_cost(0, 0),
        name="project_back",
    )(grad, weight, *extra)


def _last_kernel(p0, p1, p2, x_ref, mid_ref, gain_ref, out_ref):
    grad = p0[...].astype(jnp.float32) + p1[...].astype(jnp.float32) + p2[...].astype(jnp.float32)
    inverse, normed = _normed(x_ref[...].astype(jnp.float32))
    scaled = grad * gain_ref[...]
    out_ref[...] = mid_ref[...] + inverse * (
        scaled - normed * jnp.mean(scaled * normed, axis=-1, keepdims=True)
    )


def last(parts, x, mid, gain):
    rows, depth = x.shape
    tile = _row_tile(rows)
    return pl.pallas_call(
        _last_kernel,
        grid=(rows // tile,),
        out_shape=jax.ShapeDtypeStruct((rows, depth), jnp.float32),
        in_specs=[_rows(tile, depth)] * 5 + [_full((1, depth))],
        out_specs=_rows(tile, depth),
        compiler_params=_params(),
        cost_estimate=_cost(0, rows * depth * 16),
        name="last",
    )(*parts, x, mid, gain)


def _half_place(info_ref, b, half, piece_blocks):
    block = 2 * b + half
    piece = lax.bitwise_xor(lax.div(block, piece_blocks), info_ref[0])
    return piece, lax.rem(block, piece_blocks) * SEG


def _mask(heads, same, causal):
    key = lax.broadcasted_iota(jnp.int32, (QB, heads * QB), 0)
    query = lax.broadcasted_iota(jnp.int32, (QB, heads * QB), 1) % QB
    allowed = jnp.logical_not(same & ((key // SEG) != (query // SEG)))
    if causal:
        allowed = allowed & (key <= query)
    return allowed


def _spread(block, heads):
    turned = block.T
    lane = lax.broadcasted_iota(jnp.int32, turned.shape, 0) // HDIM
    zero = jnp.zeros_like(turned)
    return jnp.concatenate([jnp.where(lane == h, turned, zero) for h in range(heads)], axis=1)


def _stack(block, heads):
    lane = lax.broadcasted_iota(jnp.int32, block.shape, 1) // HDIM
    zero = jnp.zeros_like(block)
    return jnp.concatenate([jnp.where(lane == h, block, zero) for h in range(heads)], axis=0)


def _parents(info_ref, b):
    leaf = 2 * (b - (TRUNK + 4 * SEG) // QB)
    return [pl.multiple_of(TRUNK - SEG + SEG * info_ref[2 + leaf + side], SEG) for side in (0, 1)]


def _attn_fwd_kernel(heads, piece_count, info_ref, *refs):
    pieces = refs[:piece_count]
    out_ref, lse_ref = refs[piece_count : piece_count + 2]
    q_s, k_s, vt_s, qt_s, s_s, p_s, m_s, l_s, acc_s, kp_s, vp_s = refs[piece_count + 2 :]
    width = heads * HDIM
    piece_rows = pieces[0].shape[0]
    tensor = info_ref[0]
    base = info_ref[1]
    trunk_blocks = TRUNK // QB
    leaf_block = (TRUNK + 4 * SEG) // QB
    for j in range(piece_count):
        at = pl.multiple_of(piece_rows * lax.bitwise_xor(tensor, j), SEG)
        q_s[pl.ds(at, piece_rows), :] = pieces[j][:, :width] * jnp.asarray(HDIM**-0.5, jnp.bfloat16)
        k_s[pl.ds(at, piece_rows), :] = pieces[j][:, width : 2 * width]
        vt_s[:, pl.ds(at, piece_rows)] = pieces[j][:, 2 * width :].T

    def q_block(i, carry):
        b = base + i
        row = pl.multiple_of(b * QB, QB)
        own = pl.ds(row, QB)
        leaf = b >= leaf_block
        qt_s[...] = _spread(q_s[own, :], heads)

        def score(keys, at, size, allowed):
            scores = _dot(keys, qt_s[...], NN)
            if allowed is not None:
                scores = jnp.where(allowed, scores, -1e30)
            s_s[pl.ds(at, size), :] = scores
            return jnp.max(scores, axis=0, keepdims=True)

        m_s[0:1, :] = score(k_s[own, :], TRUNK, QB, _mask(heads, b >= trunk_blocks, True))

        @pl.when(leaf)
        def _():
            for side, at in enumerate(_parents(info_ref, b)):
                kp_s[side * SEG : (side + 1) * SEG, :] = k_s[pl.ds(at, SEG), :]
                vp_s[:, side * SEG : (side + 1) * SEG] = vt_s[:, pl.ds(at, SEG)]
            top = score(kp_s[...], TRUNK + QB, QB, _mask(heads, True, False))
            m_s[0:1, :] = jnp.maximum(m_s[0:1, :], top)

        @pl.when(b >= trunk_blocks)
        def _():
            m_s[0:1, :] = jnp.maximum(m_s[0:1, :], score(k_s[:TRUNK, :], 0, TRUNK, None))

        @pl.when(b < trunk_blocks)
        def _():
            def chunk(c, carry):
                at = pl.multiple_of(c * QB, QB)
                m_s[0:1, :] = jnp.maximum(m_s[0:1, :], score(k_s[pl.ds(at, QB), :], at, QB, None))
                return carry

            lax.fori_loop(0, b, chunk, 0)

        def mix(values, at, size, fresh):
            probs = jnp.exp(s_s[pl.ds(at, size), :] - m_s[0:1, :])
            total = jnp.sum(probs, axis=0, keepdims=True)
            p_s[pl.ds(at, size), :] = probs.astype(jnp.bfloat16)
            l_s[0:1, :] = total if fresh else l_s[0:1, :] + total
            for h in range(heads):
                of = slice(h * HDIM, (h + 1) * HDIM)
                term = _dot(values(of), p_s[pl.ds(at, size), h * QB : (h + 1) * QB], NN)
                acc_s[of, :] = term if fresh else acc_s[of, :] + term

        mix(lambda of: vt_s[of, own], TRUNK, QB, True)

        @pl.when(leaf)
        def _():
            mix(lambda of: vp_s[of, :], TRUNK + QB, QB, False)

        @pl.when(b >= trunk_blocks)
        def _():
            mix(lambda of: vt_s[of, :TRUNK], 0, TRUNK, False)

        @pl.when(b < trunk_blocks)
        def _():
            def chunk(c, carry):
                at = pl.multiple_of(c * QB, QB)
                mix(lambda of: vt_s[of, pl.ds(at, QB)], at, QB, False)
                return carry

            lax.fori_loop(0, b, chunk, 0)

        mixed = []
        for h in range(heads):
            columns = slice(h * QB, (h + 1) * QB)
            total = l_s[0:1, columns]
            lse_ref[h : h + 1, pl.ds(pl.multiple_of(i * QB, QB), QB)] = m_s[0:1, columns] + jnp.log(total)
            mixed.append(acc_s[h * HDIM : (h + 1) * HDIM, :] / total)
        mixed = jnp.concatenate(mixed, axis=0).T.astype(jnp.bfloat16)
        for half in (0, 1):
            piece, at = _half_place(info_ref, b, half, piece_rows // SEG)
            at = pl.multiple_of(at, SEG)
            out_ref[lax.bitwise_and(piece, 1), pl.ds(at, SEG), :] = mixed[half * SEG : (half + 1) * SEG]
        return carry

    lax.fori_loop(0, lse_ref.shape[1] // QB, q_block, 0)


def attention_forward(info, pieces, heads):
    rows = sum(p.shape[0] for p in pieces)
    piece_rows = pieces[0].shape[0]
    width = heads * HDIM
    half = rows // 2
    bf16, f32 = jnp.bfloat16, jnp.float32
    return pl.pallas_call(
        functools.partial(_attn_fwd_kernel, heads, len(pieces)),
        out_shape=[
            jax.ShapeDtypeStruct((2, piece_rows, width), bf16),
            jax.ShapeDtypeStruct((8, half), f32),
        ],
        grid=(1,),
        in_specs=[_smem()] + [_full(p.shape) for p in pieces],
        out_specs=[_full((2, piece_rows, width)), _full((8, half))],
        scratch_shapes=[
            pltpu.VMEM((rows, width), bf16),
            pltpu.VMEM((rows, width), bf16),
            pltpu.VMEM((width, rows), bf16),
            pltpu.VMEM((width, heads * QB), bf16),
            pltpu.VMEM((TRUNK + 2 * QB, heads * QB), f32),
            pltpu.VMEM((TRUNK + 2 * QB, heads * QB), bf16),
            pltpu.VMEM((8, heads * QB), f32),
            pltpu.VMEM((8, heads * QB), f32),
            pltpu.VMEM((width, QB), f32),
            pltpu.VMEM((QB, width), bf16),
            pltpu.VMEM((width, QB), bf16),
        ],
        compiler_params=_params(),
        cost_estimate=_cost(rows * 1400 * width * 4, rows * width * 8),
        name="attn_fwd",
    )(info, *pieces)


def _attn_bwd_kernel(heads, info_ref, *refs):
    n = 4
    pieces, mixed_in, grads = refs[:n], refs[n : n + 2], refs[n + 2 : 2 * n + 2]
    lse_refs = refs[2 * n + 2 : 2 * n + 4]
    outs = refs[2 * n + 4 : 3 * n + 4]
    q_s, k_s, kt_s, v_s, o_s, g_s, dk_s, dv_s, lse_s = refs[3 * n + 4 : 3 * n + 13]
    qt_s, gt_s, qm_s, gm_s, row_s, delta_s, acc_s, kp_s, vp_s, kpt_s = refs[3 * n + 13 :]
    width = heads * HDIM
    piece_rows = pieces[0].shape[0]
    tensor = info_ref[0]
    chip = lax.div(tensor, 2)
    half_rows = lse_refs[0].shape[1]
    scale = HDIM**-0.5
    trunk_blocks = TRUNK // QB
    leaf_block = (TRUNK + 4 * SEG) // QB
    for j in range(n):
        rows_at = pl.ds(pl.multiple_of(piece_rows * lax.bitwise_xor(tensor, j), SEG), piece_rows)
        q_s[rows_at, :] = pieces[j][:, :width] * jnp.asarray(scale, jnp.bfloat16)
        k_s[rows_at, :] = pieces[j][:, width : 2 * width]
        kt_s[:, rows_at] = pieces[j][:, width : 2 * width].T
        v_s[rows_at, :] = pieces[j][:, 2 * width :]
        o_s[rows_at, :] = mixed_in[j // 2][j % 2]
        g_s[rows_at, :] = grads[j][...]
    lse_s[:, pl.ds(pl.multiple_of(chip * half_rows, SEG), half_rows)] = lse_refs[0][...]
    lse_s[:, pl.ds(pl.multiple_of((1 - chip) * half_rows, SEG), half_rows)] = lse_refs[1][...]
    dk_s[...] = jnp.zeros_like(dk_s)
    dv_s[...] = jnp.zeros_like(dv_s)
    head_of_lane = lax.broadcasted_iota(jnp.int32, (8, width), 1) // HDIM
    pick = jnp.where(lax.broadcasted_iota(jnp.int32, (8, width), 0) == head_of_lane, 1.0, 0.0)

    def q_block(b, carry):
        row = pl.multiple_of(b * QB, QB)
        own = pl.ds(row, QB)
        both = o_s[own, :].astype(jnp.float32) * g_s[own, :].astype(jnp.float32)
        delta = lax.dot_general(
            pick, both, NT, precision=lax.Precision.HIGHEST, preferred_element_type=jnp.float32
        )
        for h in range(heads):
            columns = slice(h * QB, (h + 1) * QB)
            delta_s[0:1, columns] = delta[h : h + 1, :]
            row_s[0:1, columns] = lse_s[h : h + 1, own]
        qt_s[...] = _spread(q_s[own, :], heads)
        gt_s[...] = _spread(g_s[own, :], heads)
        qm_s[...] = _stack(q_s[own, :], heads)
        gm_s[...] = _stack(g_s[own, :], heads)

        def step(k, v, kt, allowed, fresh, targets):
            scores = _dot(k, qt_s[...], NN)
            probs_grad = _dot(v, gt_s[...], NN)
            probs = jnp.exp(scores - row_s[0:1, :])
            if allowed is not None:
                probs = jnp.where(allowed, probs, 0.0)
            ds = (probs * (probs_grad - delta_s[0:1, :])).astype(jnp.bfloat16)
            dv = _dot(probs.astype(jnp.bfloat16), gm_s[...], NN)
            dk = _dot(ds, qm_s[...], NN)
            for h in range(heads):
                of = slice(h * HDIM, (h + 1) * HDIM)
                term = _dot(kt(of), ds[:, h * QB : (h + 1) * QB], NN)
                acc_s[of, :] = term if fresh else acc_s[of, :] + term
            first = 0
            for at, size in targets:
                dv_s[pl.ds(at, size), :] += dv[first : first + size]
                dk_s[pl.ds(at, size), :] += dk[first : first + size]
                first += size

        step(
            k_s[own, :], v_s[own, :], lambda of: kt_s[of, own],
            _mask(heads, b >= trunk_blocks, True), True, [(row, QB)],
        )

        @pl.when(b >= leaf_block)
        def _():
            ats = _parents(info_ref, b)
            for side, at in enumerate(ats):
                part = slice(side * SEG, (side + 1) * SEG)
                kp_s[part, :] = k_s[pl.ds(at, SEG), :]
                vp_s[part, :] = v_s[pl.ds(at, SEG), :]
                kpt_s[:, part] = kt_s[:, pl.ds(at, SEG)]
            step(
                kp_s[...], vp_s[...], lambda of: kpt_s[of, :],
                _mask(heads, True, False), False, [(at, SEG) for at in ats],
            )

        def trunk_step(c):
            at = pl.multiple_of(c * QB, QB)
            here = pl.ds(at, QB)
            step(k_s[here, :], v_s[here, :], lambda of: kt_s[of, here], None, False, [(at, QB)])

        def trunk_pair(c, carry):
            trunk_step(2 * c)
            trunk_step(2 * c + 1)
            return carry

        count = jnp.minimum(b, trunk_blocks)
        lax.fori_loop(0, lax.div(count, 2), trunk_pair, 0)

        @pl.when(lax.rem(count, 2) == 1)
        def _():
            trunk_step(count - 1)

        q_s[own, :] = (acc_s[...] * scale).T.astype(jnp.bfloat16)
        return carry

    lax.fori_loop(0, q_s.shape[0] // QB, q_block, 0)
    for j in range(n):
        rows_at = pl.ds(pl.multiple_of(piece_rows * lax.bitwise_xor(tensor, j), SEG), piece_rows)
        outs[j][:, :width] = q_s[rows_at, :]
        outs[j][:, width : 2 * width] = dk_s[rows_at, :].astype(jnp.bfloat16)
        outs[j][:, 2 * width :] = dv_s[rows_at, :].astype(jnp.bfloat16)


def attention_backward(info, pieces, mixed, grads, lses, heads):
    n = len(pieces)
    piece_rows = pieces[0].shape[0]
    rows = n * piece_rows
    width = heads * HDIM
    bf16, f32 = jnp.bfloat16, jnp.float32
    rows_low = pltpu.VMEM((rows, width), bf16)
    return pl.pallas_call(
        functools.partial(_attn_bwd_kernel, heads),
        out_shape=[jax.ShapeDtypeStruct((piece_rows, 3 * width), bf16)] * n,
        grid=(1,),
        in_specs=[_smem()] + [_full(v.shape) for v in (*pieces, *mixed, *grads, *lses)],
        out_specs=[_full((piece_rows, 3 * width))] * n,
        scratch_shapes=[
            rows_low,
            rows_low,
            pltpu.VMEM((width, rows), bf16),
            rows_low,
            rows_low,
            rows_low,
            pltpu.VMEM((rows, width), f32),
            pltpu.VMEM((rows, width), f32),
            pltpu.VMEM((8, rows), f32),
            pltpu.VMEM((width, heads * QB), bf16),
            pltpu.VMEM((width, heads * QB), bf16),
            pltpu.VMEM((heads * QB, width), bf16),
            pltpu.VMEM((heads * QB, width), bf16),
            pltpu.VMEM((8, heads * QB), f32),
            pltpu.VMEM((8, heads * QB), f32),
            pltpu.VMEM((width, QB), f32),
            pltpu.VMEM((QB, width), bf16),
            pltpu.VMEM((QB, width), bf16),
            pltpu.VMEM((width, QB), bf16),
        ],
        compiler_params=_params(),
        cost_estimate=_cost(rows * 1400 * width * 20, rows * width * 16),
        name="attn_bwd",
    )(info, *pieces, *mixed, *grads, *lses)


def mate(x):
    return lax.ppermute(x, "tensor", [(i, i ^ 1) for i in range(4)])


def across(x):
    return lax.ppermute(x, "tensor", [(i, i ^ 2) for i in range(4)])


def corner(x):
    return lax.ppermute(x, "tensor", [(i, i ^ 3) for i in range(4)])


def beside(x):
    return lax.ppermute(x, "dp", [(i, i ^ 1) for i in range(8)])


def ahead(x, step):
    return lax.ppermute(x, "dp", [(i, (i + 2 * step) % 8) for i in range(8)])


def after(x, *others):
    return lax.optimization_barrier((x, *others))[0]


def after_all(values, *others):
    return list(lax.optimization_barrier((*values, *others))[: len(values)])


def line_hops(x):
    return [x] + [ahead(x, step) for step in (1, 3, 2)]


def spread_hops(line, far):
    dp = lax.axis_index("dp")
    z, y = dp // 2, dp % 2
    order = jnp.array([0, 1, 3, 2], jnp.int32)
    from_z = (z - order) % 4
    where = jnp.concatenate([2 * from_z + y, 2 * from_z + 1 - y]).astype(jnp.int32)
    return place(where, line + far)


def fold_hops(near, passed):
    z = (lax.axis_index("dp") // 2).astype(jnp.int32)[None]
    return fold(z, near, passed)


def send_hops(chunks):
    return [chunks[0]] + [ahead(chunks[step], step) for step in (2, 1, 3)]


def sum_hops(received):
    return sum(v.astype(jnp.float32) for v in received)


def body(
    block_input,
    norm_gains,
    qkv_weight,
    out_weight,
    gate_up_weight,
    down_weight,
    parent_of_row,
    cotangent,
):
    bf16, f32 = jnp.bfloat16, jnp.float32
    shard = qkv_weight.shape[1]
    width = qkv_weight.shape[2]
    hidden_width = gate_up_weight.shape[2]
    heads = width // HDIM
    rows = parent_of_row.shape[0]
    tensor = lax.axis_index("tensor")
    chip = tensor // 2
    y = (lax.axis_index("dp") % 2).astype(jnp.int32)[None]
    leaf_first = TRUNK + 4 * SEG
    parents = parent_of_row[leaf_first::SEG]
    half_blocks = rows // (2 * QB)
    place_own = jnp.stack([tensor, half_blocks * chip]).astype(jnp.int32)
    place_far = jnp.stack([tensor, half_blocks * (1 - chip)]).astype(jnp.int32)
    info_own = jnp.concatenate([place_own, parents])
    info_far = jnp.concatenate([place_far, parents])

    half = block_input.shape[0] // 2
    gains_shard = jnp.pad(norm_gains.astype(bf16).T, ((0, 0), (0, SEG - 2)))
    qkv_shard = qkv_weight.astype(bf16).transpose(1, 0, 2).reshape(shard, 3 * width)
    out_shard = out_weight.astype(bf16).T
    gate_up_shard = gate_up_weight.astype(bf16).transpose(1, 0, 2).reshape(shard, 2 * hidden_width)
    first_line = line_hops(jnp.concatenate([qkv_shard, gains_shard], axis=1))
    beyond = [across(block_input[:half]), across(block_input[half:])]
    rest_shard = jnp.concatenate([gate_up_shard, out_shard, across(out_shard)], axis=1)
    rest = lax.all_gather(after(rest_shard, beyond[0], *first_line), "dp", axis=0, tiled=True)
    first_far = [beside(v) for v in first_line]
    near_x = mate(block_input)
    first = spread_hops(first_line, first_far)
    down_line = line_hops(after(down_weight.astype(bf16).T, *first_far))
    gains_low = first[:, 3 * width : 3 * width + 2].T.astype(f32)
    gain_attn, gain_mlp = gains_low[0:1], gains_low[1:2]
    n0, n1, p0, p1 = project(block_input, near_x, gain_attn, first, 3 * width)
    beyond = jnp.concatenate([beyond[0], beyond[1]], axis=0)
    inputs = [block_input, near_x, beyond, mate(beyond)]
    n2, n3, p2, p3 = project(inputs[2], after(inputs[3], p1), gain_attn, first, 3 * width)
    normed_attn, projected = [n0, n1, n2, n3], [p0, p1, p2, p3]
    cot_low = cotangent.astype(bf16)
    cot_x = across(after(cot_low, beyond))

    own, lse_own = attention_forward(info_own, projected, heads)
    own_x, own_m = across(after(own, cot_x)), mate(own)
    down_far = [beside(after(v, own)) for v in down_line]
    cot_near = mate(after(cot_low, own))
    far, lse_far = attention_forward(after(info_far, own), projected, heads)
    far_m, own_xm = mate(far), mate(after(own_x, far))
    far_x = across(far)
    down_low = spread_hops(down_line, after_all(down_far, far))
    cot_rows = [cot_low, cot_near, cot_x, mate(after(cot_x, far))]
    out_far = mate(after(rest[:, 2 * hidden_width :], down_low))

    own_rows = [(own, 0), (own_m, 1), (far_x, 0), None]
    hidden_far, grads_far, normed_far, part3, part2, branch3, branch2 = mlp(
        [(far, 1), (far_m, 0), (own_x, 1), (own_xm, 0)],
        [(far, 0), (far_m, 1), (own_x, 0), (own_xm, 1)],
        [inputs[3], inputs[2]], [cot_rows[3], cot_rows[2]], gain_mlp, rest, down_low, out_far, False,
    )
    far_xm = mate(after(far_x, part3))
    own_rows[3] = (far_xm, 1)
    passed = (part2.astype(f32) + mate(after(part3, far_x)).astype(f32)).astype(bf16)
    passed_x = across(passed)
    hidden_own, grads_own, normed_own, part1, part0, branch1, branch0, residual_mid = mlp(
        [(own, 1), (own_m, 0), (far_x, 1), (far_xm, 0)], own_rows,
        [inputs[1], inputs[0]], [after(cot_rows[1], passed), cot_rows[0]],
        gain_mlp, rest, down_low, out_far, True,
    )
    mlp_parts = [part0, mate(after(part1, passed_x)), passed_x]

    grad_sum = mlp_grads(
        [normed_far, normed_own],
        [cot_rows[n] for n in (3, 2, 1, 0)],
        [grads_far, grads_own],
        [hidden_far, hidden_own],
    )
    mid_grad, attn_grad, g0, g1, g2, g3, mlp_sum = middle(
        [after(mlp_parts[0], grad_sum), *mlp_parts[1:]], residual_mid, cotangent, gain_mlp, rest, out_far
    )
    grad_sum = lax.psum_scatter(grad_sum, "dp", scatter_dimension=0, tiled=True)
    g_x, g_c, g_m = across(g2), corner(g3), mate(g1)
    out_mine, out_theirs = out_grads(attn_grad, own_rows)
    out_theirs = mate(out_theirs)
    branch_passed = (branch2.astype(f32) + mate(branch3).astype(f32)).astype(bf16)
    out_pair = pair_sum(y, out_mine, after(out_theirs, branch_passed), shard)
    out_y = beside(out_pair[1])
    branch_x = across(after(branch_passed, g_x, g_c))

    bwd_grads = after_all([g0, g_m, g_x, g_c], out_pair[1], branch_passed)
    projected_grad = attention_backward(
        info_own, projected, [own, far], bwd_grads, [lse_own, lse_far], heads
    )
    out_chunks = fold_hops(out_pair[0], after(out_y, *projected_grad, branch_x))
    out_received = send_hops(out_chunks)
    qkv_pair = qkv_grads(
        y, normed_attn, after_all(projected_grad, out_chunks[1]), first, gain_attn, mlp_sum, shard
    )
    qkv_y = beside(qkv_pair[1])
    back3 = project_back(after(projected_grad[3], qkv_pair[1]), first)
    back2 = project_back(projected_grad[2], first, mate(back3))
    back_x = across(back2)
    back1 = project_back(after(projected_grad[1], back2, *out_received), first)
    back0 = project_back(after(projected_grad[0], back1), first)
    branch_sum = branch0.astype(f32) + mate(branch1).astype(f32)
    block_output = residual_mid + branch_sum + after(branch_x, back0).astype(f32)
    qkv_chunks = fold_hops(qkv_pair[0], after(qkv_y, back0, block_output))
    qkv_received = send_hops(qkv_chunks)
    back_m = mate(after(back1, qkv_y))
    input_grad = last([back0, back_m, after(back_x, qkv_chunks[1])], block_input, mid_grad, gain_attn)
    grad_sum = after(grad_sum, input_grad).astype(f32)
    down_out = grad_sum[:, 2 * hidden_width :].T
    gate_up_out = grad_sum[:, : 2 * hidden_width].reshape(shard, 2, hidden_width).transpose(1, 0, 2)
    out_sum = sum_hops(out_received)
    qkv_sum = sum_hops(after_all(qkv_received, input_grad))
    qkv_out = qkv_sum[:, : 3 * width].reshape(shard, 3, width).transpose(1, 0, 2)
    gains_sum = qkv_sum[:, 3 * width :]
    gains_sum = gains_sum + mate(gains_sum.astype(bf16)).astype(f32)
    from_x = across(jnp.concatenate([out_sum[:, width:], gains_sum], axis=1).astype(bf16)).astype(f32)
    out_out = (out_sum[:, :width] + from_x[:, :width]).T
    gains_out = (gains_sum + from_x[:, width:])[:, :2].T
    return (block_output, input_grad, gains_out, qkv_out, out_out, gate_up_out, down_out)


def solution(mesh):
    placed = (
        P(("dp", "tensor"), None),
        P(None, "dp"),
        P(None, "dp", "tensor"),
        P("tensor", "dp"),
        P(None, "dp", "tensor"),
        P("tensor", "dp"),
        P("dp"),
        P(("dp", "tensor"), None),
    )
    four_by_eight = mesh.shape["tensor"] == 4 and mesh.shape["dp"] == 8
    return jax.shard_map(
        body if four_by_eight else body_any_mesh,
        mesh=mesh,
        in_specs=placed,
        out_specs=(
            P(("dp", "tensor"), None),
            P(("dp", "tensor"), None),
            P(None, "dp"),
            P(None, "dp", "tensor"),
            P("tensor", "dp"),
            P(None, "dp", "tensor"),
            P("tensor", "dp"),
        ),
        check_vma=False,
    )
```

```python
import functools
import jax
import jax.numpy as jnp
from jax import lax
from jax.experimental import pallas as pl
from jax.experimental.pallas import tpu as pltpu
from jax.sharding import PartitionSpec as P

HDIM = 64
TRUNK = 1024
SEG = 128
ROW_TREE = 2560


epsilon = 1e-06


def norm_rows(values, gain_row):
    inverse_rms = lax.rsqrt(jnp.mean(values * values, axis=-1, keepdims=True) + epsilon)
    return values * inverse_rms * gain_row


def segment_ids(row_count):
    position = jnp.arange(row_count, dtype=jnp.int32)
    tree_base = position // ROW_TREE * 13
    within = position % ROW_TREE
    beyond = within - TRUNK
    own_segment = jnp.where(
        within < TRUNK,
        0,
        jnp.where(beyond < 4 * SEG, 1 + beyond // SEG, 5 + (beyond - 4 * SEG) // SEG),
    )
    return (own_segment + tree_base, tree_base)


def body_any_mesh(
    block_input,
    norm_gains,
    qkv_weight,
    out_weight,
    gate_up_weight,
    down_weight,
    parent_of_row,
    cotangent,
):
    gains_cast = norm_gains.astype(jnp.bfloat16)
    qkv_cast = qkv_weight.astype(jnp.bfloat16)
    out_cast = out_weight.astype(jnp.bfloat16)
    gate_up_cast = gate_up_weight.astype(jnp.bfloat16)
    down_cast = down_weight.astype(jnp.bfloat16)
    gains_low, qkv_low, out_low, gate_up_low, down_low = (
        lax.all_gather(gains_cast, "dp", axis=1, tiled=True),
        lax.all_gather(qkv_cast, "dp", axis=1, tiled=True),
        lax.all_gather(out_cast, "dp", axis=1, tiled=True),
        lax.all_gather(gate_up_cast, "dp", axis=1, tiled=True),
        lax.all_gather(down_cast, "dp", axis=1, tiled=True),
    )
    row_count = parent_of_row.shape[0]
    width_local = qkv_low.shape[2]
    head_local = width_local // HDIM
    block_rows = min(512, row_count)
    block_count = row_count // block_rows
    score_scale = float(HDIM) ** (-0.5)
    segment_of_row, trunk_of_row = segment_ids(row_count)
    parent_segment = parent_of_row + trunk_of_row
    column_index = jnp.arange(row_count, dtype=jnp.int32)
    residual_in = block_input.astype(jnp.float32)
    gain_attn = gains_low[0].astype(jnp.float32)
    gain_mlp = gains_low[1].astype(jnp.float32)
    normed_attn = lax.all_gather(
        norm_rows(residual_in, gain_attn).astype(jnp.bfloat16), "tensor", axis=0, tiled=True
    )
    projected = jnp.einsum(
        "rd,cde->cre", normed_attn, qkv_low, preferred_element_type=jnp.float32
    ).astype(jnp.bfloat16)
    query_rows = projected[0].reshape(row_count, head_local, HDIM)
    key_rows = projected[1].reshape(row_count, head_local, HDIM)
    value_rows = projected[2].reshape(row_count, head_local, HDIM)

    def block_scores(block_index):
        row_start = block_index * block_rows
        query_block = lax.dynamic_slice_in_dim(query_rows, row_start, block_rows, 0)
        scores = (
            jnp.einsum("qhd,khd->hqk", query_block, key_rows, preferred_element_type=jnp.float32)
            * score_scale
        )
        row_index = row_start + jnp.arange(block_rows, dtype=jnp.int32)
        row_segment = lax.dynamic_slice_in_dim(segment_of_row, row_start, block_rows, 0)
        row_parent = lax.dynamic_slice_in_dim(parent_segment, row_start, block_rows, 0)
        row_trunk = lax.dynamic_slice_in_dim(trunk_of_row, row_start, block_rows, 0)
        column_segment = segment_of_row[None, :]
        allowed = (column_index[None, :] <= row_index[:, None]) & (
            (column_segment == row_segment[:, None])
            | (column_segment == row_parent[:, None])
            | (column_segment == row_trunk[:, None])
        )
        return (jnp.where(allowed[None], scores, -1e30), query_block)

    def attend_block(block_index):
        scores, query_block = block_scores(block_index)
        top_score = jnp.max(scores, axis=-1, keepdims=True)
        exp_scores = jnp.exp(scores - top_score)
        row_total = jnp.sum(exp_scores, axis=-1, keepdims=True)
        softmax_low = (exp_scores / row_total).astype(jnp.bfloat16)
        mixed_heads = jnp.einsum(
            "hqk,khd->qhd", softmax_low, value_rows, preferred_element_type=jnp.float32
        ).astype(jnp.bfloat16)
        return (mixed_heads, (top_score + jnp.log(row_total))[..., 0])

    block_ids = jnp.arange(block_count, dtype=jnp.int32)
    attended, log_totals = lax.map(attend_block, block_ids)
    attended = attended.reshape(row_count, width_local)
    attn_partial = jnp.dot(attended, out_low, preferred_element_type=jnp.float32)
    residual_mid = residual_in + lax.psum_scatter(
        attn_partial, "tensor", scatter_dimension=0, tiled=True
    )
    normed_mlp = lax.all_gather(
        norm_rows(residual_mid, gain_mlp).astype(jnp.bfloat16), "tensor", axis=0, tiled=True
    )
    gate_up = jnp.einsum(
        "rd,cdf->crf", normed_mlp, gate_up_low, preferred_element_type=jnp.float32
    ).astype(jnp.bfloat16)
    gate_value = gate_up[0].astype(jnp.float32)
    up_value = gate_up[1].astype(jnp.float32)
    sigmoid_gate = jax.nn.sigmoid(gate_value)
    hidden = (gate_value * sigmoid_gate * up_value).astype(jnp.bfloat16)
    mlp_partial = jnp.dot(hidden, down_low, preferred_element_type=jnp.float32)
    block_output = residual_mid + lax.psum_scatter(
        mlp_partial.astype(jnp.bfloat16), "tensor", scatter_dimension=0, tiled=True
    ).astype(jnp.float32)
    gains_again = norm_gains.astype(jnp.bfloat16)
    qkv_again = qkv_weight.astype(jnp.bfloat16)
    out_again = out_weight.astype(jnp.bfloat16)
    gate_up_again = gate_up_weight.astype(jnp.bfloat16)
    down_again = down_weight.astype(jnp.bfloat16)
    gains_low, qkv_low, out_low, gate_up_low, down_low = (
        lax.all_gather(gains_again, "dp", axis=1, tiled=True),
        lax.all_gather(qkv_again, "dp", axis=1, tiled=True),
        lax.all_gather(out_again, "dp", axis=1, tiled=True),
        lax.all_gather(gate_up_again, "dp", axis=1, tiled=True),
        lax.all_gather(down_again, "dp", axis=1, tiled=True),
    )
    gain_attn = gains_low[0].astype(jnp.float32)
    gain_mlp = gains_low[1].astype(jnp.float32)
    mlp_grad_rows = lax.all_gather(cotangent.astype(jnp.bfloat16), "tensor", axis=0, tiled=True)
    down_grad = jnp.einsum("rf,rd->fd", hidden, mlp_grad_rows, preferred_element_type=jnp.float32)
    hidden_grad = jnp.einsum(
        "rd,fd->rf", mlp_grad_rows, down_low, preferred_element_type=jnp.float32
    )
    gate_grad = hidden_grad * up_value * sigmoid_gate * (1.0 + gate_value * (1.0 - sigmoid_gate))
    up_grad = hidden_grad * gate_value * sigmoid_gate
    gate_up_grad_low = jnp.stack([gate_grad, up_grad]).astype(jnp.bfloat16)
    gate_up_grad = jnp.einsum(
        "rd,crf->cdf", normed_mlp, gate_up_grad_low, preferred_element_type=jnp.float32
    )
    normed_mlp_part = jnp.einsum(
        "crf,cdf->rd", gate_up_grad_low, gate_up_low, preferred_element_type=jnp.float32
    )
    normed_mlp_grad = lax.psum_scatter(normed_mlp_part, "tensor", scatter_dimension=0, tiled=True)
    norm_back_mlp = jax.vjp(norm_rows, residual_mid, gain_mlp)[1]
    mid_from_norm, gain_mlp_grad = norm_back_mlp(normed_mlp_grad)
    mid_grad = cotangent + mid_from_norm
    attn_grad_rows = lax.all_gather(mid_grad.astype(jnp.bfloat16), "tensor", axis=0, tiled=True)
    out_grad = jnp.einsum("re,rd->ed", attended, attn_grad_rows, preferred_element_type=jnp.float32)
    attended_grad = jnp.einsum(
        "rd,ed->re", attn_grad_rows, out_low, preferred_element_type=jnp.float32
    ).astype(jnp.bfloat16)
    attended_grad = attended_grad.reshape(row_count, head_local, HDIM)

    def back_block(carry, block_inputs):
        key_grad, value_grad = carry
        block_index, log_total = block_inputs
        scores, query_block = block_scores(block_index)
        probs = jnp.exp(scores - log_total[..., None])
        grad_block = lax.dynamic_slice_in_dim(
            attended_grad, block_index * block_rows, block_rows, 0
        )
        probs_grad = jnp.einsum(
            "qhd,khd->hqk", grad_block, value_rows, preferred_element_type=jnp.float32
        )
        inner_term = jnp.sum(probs * probs_grad, axis=-1, keepdims=True)
        score_grad = (probs * (probs_grad - inner_term)).astype(jnp.bfloat16)
        query_grad = (
            jnp.einsum("hqk,khd->qhd", score_grad, key_rows, preferred_element_type=jnp.float32)
            * score_scale
        )
        key_grad = (
            key_grad
            + jnp.einsum(
                "hqk,qhd->khd", score_grad, query_block, preferred_element_type=jnp.float32
            )
            * score_scale
        )
        value_grad = value_grad + jnp.einsum(
            "hqk,qhd->khd",
            probs.astype(jnp.bfloat16),
            grad_block,
            preferred_element_type=jnp.float32,
        )
        return ((key_grad, value_grad), query_grad)

    zero_grad = jnp.zeros((row_count, head_local, HDIM), jnp.float32)
    carried, query_grads = lax.scan(back_block, (zero_grad, zero_grad), (block_ids, log_totals))
    projected_grad = jnp.stack(
        [
            query_grads.reshape(row_count, width_local),
            carried[0].reshape(row_count, width_local),
            carried[1].reshape(row_count, width_local),
        ]
    ).astype(jnp.bfloat16)
    qkv_grad = jnp.einsum(
        "rd,cre->cde", normed_attn, projected_grad, preferred_element_type=jnp.float32
    )
    normed_attn_part = jnp.einsum(
        "cre,cde->rd", projected_grad, qkv_low, preferred_element_type=jnp.float32
    )
    normed_attn_grad = lax.psum_scatter(
        normed_attn_part.astype(jnp.bfloat16), "tensor", scatter_dimension=0, tiled=True
    ).astype(jnp.float32)
    norm_back_attn = jax.vjp(norm_rows, residual_in, gain_attn)[1]
    input_from_norm, gain_attn_grad = norm_back_attn(normed_attn_grad)
    input_grad = mid_grad + input_from_norm
    gain_grads = lax.psum(jnp.stack([gain_attn_grad, gain_mlp_grad]), "tensor")
    gains_out, qkv_out, out_out, gate_up_out, down_out = (
        lax.psum_scatter(
            gain_grads.astype(jnp.bfloat16), "dp", scatter_dimension=1, tiled=True
        ).astype(jnp.float32),
        lax.psum_scatter(
            qkv_grad.astype(jnp.bfloat16), "dp", scatter_dimension=1, tiled=True
        ).astype(jnp.float32),
        lax.psum_scatter(
            out_grad.astype(jnp.bfloat16), "dp", scatter_dimension=1, tiled=True
        ).astype(jnp.float32),
        lax.psum_scatter(
            gate_up_grad.astype(jnp.bfloat16), "dp", scatter_dimension=1, tiled=True
        ).astype(jnp.float32),
        lax.psum_scatter(
            down_grad.astype(jnp.bfloat16), "dp", scatter_dimension=1, tiled=True
        ).astype(jnp.float32),
    )
    return (block_output, input_grad, gains_out, qkv_out, out_out, gate_up_out, down_out)


QB = 256
NT = (((1,), (1,)), ((), ()))
NN = (((1,), (0,)), ((), ()))
TN = (((0,), (0,)), ((), ()))


def _dot(a, b, dims):
    return lax.dot_general(a, b, dims, preferred_element_type=jnp.float32)


def _stacked(tile, columns, n):
    return pl.BlockSpec((1, tile, columns), lambda i: (n, i, 0))


def _full(shape):
    return pl.BlockSpec(shape, lambda i: (0,) * len(shape))


def _smem():
    return pl.BlockSpec(memory_space=pltpu.SMEM)


def _rows(tile, columns):
    return pl.BlockSpec((tile, columns), lambda i: (i, 0))


def _params():
    return pltpu.CompilerParams(dimension_semantics=("arbitrary",), vmem_limit_bytes=60 << 20)


STRETCH = 6.0


def _cost(flops, bytes_accessed):
    return pl.CostEstimate(
        flops=int(flops * STRETCH), bytes_accessed=int(bytes_accessed * STRETCH), transcendentals=0
    )


def _row_tile(rows):
    return rows // 2 if rows % 32 == 0 else rows


def _normed(values):
    inverse_rms = lax.rsqrt(jnp.mean(values * values, axis=-1, keepdims=True) + epsilon)
    return inverse_rms, values * inverse_rms


def _place_kernel(where_ref, *refs):
    shards, out = refs[:-1], refs[-1]
    size = shards[0].shape[0]
    for n, shard in enumerate(shards):
        out[pl.ds(pl.multiple_of(where_ref[n] * size, size), size), :] = shard[...]


def place(where, shards):
    size, columns = shards[0].shape
    return pl.pallas_call(
        _place_kernel,
        grid=(1,),
        out_shape=jax.ShapeDtypeStruct((size * len(shards), columns), shards[0].dtype),
        in_specs=[_smem()] + [_full((size, columns))] * len(shards),
        out_specs=_full((size * len(shards), columns)),
        compiler_params=_params(),
        cost_estimate=_cost(0, 4 * size * columns * len(shards)),
        name="place",
    )(where, *shards)


def _project_kernel(x0_ref, x1_ref, gain_ref, w_ref, n0_ref, n1_ref, p0_ref, p1_ref):
    def run(x_ref, normed_ref, out_ref):
        normed = (_normed(x_ref[...].astype(jnp.float32))[1] * gain_ref[...]).astype(jnp.bfloat16)
        normed_ref[...] = normed
        out_ref[...] = _dot(normed, w_ref[...], NN).astype(jnp.bfloat16)

    half = pl.num_programs(0) // 2

    @pl.when(pl.program_id(0) < half)
    def _():
        run(x0_ref, n0_ref, p0_ref)

    @pl.when(pl.program_id(0) >= half)
    def _():
        run(x1_ref, n1_ref, p1_ref)


def project(x0, x1, gain, weight, columns):
    rows, depth = x0.shape
    tile = _row_tile(rows)
    steps = rows // tile
    early = lambda c: pl.BlockSpec((tile, c), lambda i: (jnp.minimum(i, steps - 1), 0))
    late = lambda c: pl.BlockSpec((tile, c), lambda i: (jnp.maximum(i - steps, 0), 0))
    out = lambda c: jax.ShapeDtypeStruct((rows, c), jnp.bfloat16)
    return pl.pallas_call(
        _project_kernel,
        grid=(2 * steps,),
        out_shape=[out(depth), out(depth), out(columns), out(columns)],
        in_specs=[early(depth), late(depth), _full((1, depth)), _full((depth, columns))],
        out_specs=[early(depth), late(depth), early(columns), late(columns)],
        compiler_params=_params(),
        cost_estimate=_cost(4 * rows * depth * columns, 4 * rows * (2 * depth + columns)),
        name="project",
    )(x0, x1, gain, weight)


def _mlp_kernel(keep, *refs):
    att_a, att_b, (xa, xb, ca, cb) = refs[:4], refs[4:8], refs[8:12]
    gain_ref, w_hbm, d_hbm, m_hbm = refs[12:16]
    hidden_ref, grad_ref, normed_ref = refs[16:19]
    part_a, part_b, branch_a, branch_b = refs[19:23]
    att_s, x_s, cot_s, o_s, w_s, d_s, sems = refs[-7:]
    width = att_a[0].shape[2]
    count = hidden_ref.shape[2]
    pulls = [
        pltpu.make_async_copy(
            d_hbm.at[:, pl.ds(count, 2 * width)], o_s.at[:, pl.ds(0, 2 * width)], sems.at[0]
        ),
        pltpu.make_async_copy(m_hbm, o_s.at[:, pl.ds(2 * width, 2 * width)], sems.at[1]),
        pltpu.make_async_copy(w_hbm, w_s, sems.at[2]),
        pltpu.make_async_copy(d_hbm.at[:, pl.ds(0, count)], d_s, sems.at[3]),
    ]
    first = pl.program_id(0) == 0
    late = pl.program_id(0) >= pl.num_programs(0) // 2

    @pl.when(first)
    def _():
        for pull in pulls:
            pull.start()

    def take(att, x_ref, cot_ref):
        for i, of in enumerate((0, 2, 1, 3)):
            att_s[:, i * width : (i + 1) * width] = att[of][0]
        x_s[...] = x_ref[...]
        cot_s[...] = cot_ref[...]

    @pl.when(jnp.logical_not(late))
    def _():
        take(att_a, xa, ca)

    @pl.when(late)
    def _():
        take(att_b, xb, cb)

    @pl.when(first)
    def _():
        for pull in pulls[:2]:
            pull.wait()

    residual = x_s[...].astype(jnp.float32) + _dot(att_s[...], o_s[...], NT)
    if keep:
        keep_ref = refs[23]

        @pl.when(late)
        def _():
            keep_ref[...] = residual

    normed_ref[0] = (_normed(residual)[1] * gain_ref[...]).astype(jnp.bfloat16)

    @pl.when(first)
    def _():
        for pull in pulls[2:]:
            pull.wait()

    both = _dot(normed_ref[0], w_s[...], NN).astype(jnp.bfloat16).astype(jnp.float32)
    gate, up = both[:, :count], both[:, count:]
    hidden_grad = _dot(cot_s[...], d_s[...], NN)
    sig = 0.5 * jnp.tanh(0.5 * gate) + 0.5
    act = gate * sig
    hidden = (act * up).astype(jnp.bfloat16)
    hidden_ref[0] = hidden
    grad_ref[0, :, :count] = (hidden_grad * up * (sig + act * (1.0 - sig))).astype(jnp.bfloat16)
    grad_ref[0, :, count:] = (hidden_grad * act).astype(jnp.bfloat16)
    part = _dot(grad_ref[0], w_s[...], NT).astype(jnp.bfloat16)
    branch = _dot(hidden, d_s[...], NT).astype(jnp.bfloat16)

    @pl.when(jnp.logical_not(late))
    def _():
        part_a[...] = part
        branch_a[...] = branch

    @pl.when(late)
    def _():
        part_b[...] = part
        branch_b[...] = branch


def mlp(attended_a, attended_b, x, cot, gain, weights, down, out_mate, keep):
    rows, depth = x[0].shape
    width = attended_a[0][0].shape[2]
    count = weights.shape[1] // 2
    tile = _row_tile(rows)
    steps = rows // tile
    bf16, f32 = jnp.bfloat16, jnp.float32
    early = lambda i: jnp.minimum(i, steps - 1)
    late = lambda i: jnp.maximum(i - steps, 0)
    rows_of = lambda where: pl.BlockSpec((tile, depth), lambda i: (where(i), 0))
    stack = lambda c: pl.BlockSpec((1, tile, c), lambda i: (i // steps, i % steps, 0))
    member = lambda n, where: pl.BlockSpec((1, tile, width), lambda i: (n, where(i), 0))
    outs = [jax.ShapeDtypeStruct((2, rows, c), bf16) for c in (count, 2 * count, depth)]
    outs += [jax.ShapeDtypeStruct((rows, depth), bf16)] * 4
    out_specs = [stack(count), stack(2 * count), stack(depth)] + [rows_of(early), rows_of(late)] * 2
    if keep:
        outs.append(jax.ShapeDtypeStruct((rows, depth), f32))
        out_specs.append(rows_of(late))
    anywhere = pl.BlockSpec(memory_space=pl.ANY)
    return pl.pallas_call(
        functools.partial(_mlp_kernel, keep),
        grid=(2 * steps,),
        out_shape=outs,
        in_specs=[member(n, early) for v, n in attended_a]
        + [member(n, late) for v, n in attended_b]
        + [rows_of(early), rows_of(late)] * 2
        + [_full((1, depth)), anywhere, anywhere, anywhere],
        out_specs=out_specs,
        scratch_shapes=[
            pltpu.VMEM((tile, 4 * width), bf16),
            pltpu.VMEM((tile, depth), bf16),
            pltpu.VMEM((tile, depth), bf16),
            pltpu.VMEM((depth, 4 * width), bf16),
            pltpu.VMEM((depth, 2 * count), bf16),
            pltpu.VMEM((depth, count), bf16),
            pltpu.SemaphoreType.DMA((4,)),
        ],
        compiler_params=_params(),
        cost_estimate=_cost(4 * rows * depth * (4 * width + 6 * count), 28 << 20),
        name="mlp",
    )(*[v for v, n in (*attended_a, *attended_b)], *x, *cot, gain, weights, down, out_mate)


def _pull_groups(right, right_s, row_at, column_at, step, sems, base):
    groups = []
    for c in range(right[0].shape[-1] // step):
        group = []
        at = row_at
        for j, piece in enumerate(right):
            rows = piece.shape[0]
            group.append(
                pltpu.make_async_copy(
                    piece.at[:, pl.ds(c * step, step)],
                    right_s.at[pl.ds(at, rows), pl.ds(column_at + c * step, step)],
                    sems.at[base + c * len(right) + j],
                )
            )
            at += rows
        groups.append(group)
    return groups


def _start_all(groups):
    @pl.when(pl.program_id(0) == 0)
    def _():
        for group in groups:
            for pull in group:
                pull.start()


def _wait_group(group):
    @pl.when(pl.program_id(0) == 0)
    def _():
        for pull in group:
            pull.wait()


def _join(pieces, out):
    at = 0
    for piece in pieces:
        rows = piece.shape[0]
        out[at : at + rows, :] = piece[...]
        at += rows


def _mlp_grad_kernel(n, step, *refs):
    normed, cot = refs[:2], refs[2 : 2 + n]
    grads, hidden = refs[2 + n : 4 + n], refs[4 + n : 6 + n]
    out_ref, left_s, right_s, sems = refs[6 + n :]
    members = lambda pair: [v.at[m] for v in pair for m in (0, 1)]
    wide = grads[0].shape[2]
    rows = left_s.shape[0] // n
    groups = _pull_groups(members(grads), right_s, 0, 0, step, sems, 0)
    groups += _pull_groups(members(hidden), right_s, 0, wide, step, sems, 4 * (wide // step))
    _start_all(groups)
    for m in range(n):
        left_s[m * rows : (m + 1) * rows, :] = normed[m // 2][m % 2]
    for c, group in enumerate(groups):
        at = slice(c * step, (c + 1) * step)
        if c * step == wide:
            _join(cot, left_s)
        _wait_group(group)
        out_ref[:, at] = _dot(left_s[...], right_s[:, at], TN).astype(out_ref.dtype)


def mlp_grads(normed, cot, grads, hidden, block=256):
    n = len(cot)
    piece, depth = cot[0].shape
    rows = n * piece
    columns = grads[0].shape[2] + hidden[0].shape[2]
    step = hidden[0].shape[2]
    anywhere = pl.BlockSpec(memory_space=pl.ANY)
    return pl.pallas_call(
        functools.partial(_mlp_grad_kernel, n, step),
        grid=(depth // block,),
        out_shape=jax.ShapeDtypeStruct((depth, columns), jnp.bfloat16),
        in_specs=[pl.BlockSpec((2, piece, block), lambda i: (0, 0, i))] * 2
        + [pl.BlockSpec((piece, block), lambda i: (0, i))] * n
        + [anywhere] * 4,
        out_specs=_rows(block, columns),
        scratch_shapes=[
            pltpu.VMEM((rows, block), jnp.bfloat16),
            pltpu.VMEM((rows, columns), jnp.bfloat16),
            pltpu.SemaphoreType.DMA((n * (columns // step),)),
        ],
        compiler_params=_params(),
        cost_estimate=_cost(2 * rows * depth * columns, 2 * rows * (depth + columns) + 2 * depth * columns),
        name="mlp_grads",
    )(*normed, *cot, *grads, *hidden)


def _split_rows(acc, y, near, far):
    size = near.shape[1]
    near[...] = acc[pl.ds(pl.multiple_of(y * size, size), size), :].astype(near.dtype)[None]
    far[...] = acc[pl.ds(pl.multiple_of((1 - y) * size, size), size), :].astype(far.dtype)[None]


def _qkv_grad_kernel(n, y_ref, *refs):
    left, right = refs[:n], refs[n : 2 * n]
    w_ref, gain_ref, row_ref, near, far, left_s, right_s, acc, sems = refs[2 * n :]
    columns = right_s.shape[1]
    groups = _pull_groups(right, right_s, 0, 0, columns, sems, 0)
    _start_all(groups)
    _join(left, left_s)
    _wait_group(groups[0])
    total = _dot(left_s[...], right_s[...], TN)
    acc[:, :columns] = total
    row = jnp.concatenate(
        [1.0 / gain_ref[...], row_ref[...], jnp.zeros((SEG - 9, row_ref.shape[1]), jnp.float32)], axis=0
    ).T
    attn = jnp.sum(total * w_ref[...].astype(jnp.float32), axis=-1, keepdims=True) * row[:, 0:1]
    lane = lax.broadcasted_iota(jnp.int32, row.shape, 1)
    acc[:, columns:] = jnp.where(lane == 0, attn, row)
    _split_rows(acc, y_ref[0], near, far)


def qkv_grads(y, normed, grads, weight, gain, mlp_sum, size):
    n, depth = len(normed), normed[0].shape[1]
    rows = sum(v.shape[0] for v in normed)
    columns = grads[0].shape[1]
    block = 2 * size
    anywhere = pl.BlockSpec(memory_space=pl.ANY)
    out = jax.ShapeDtypeStruct((depth // block, size, columns + SEG), jnp.bfloat16)
    out_spec = pl.BlockSpec((1, size, columns + SEG), lambda i: (i, 0, 0))
    lanes = lambda r: pl.BlockSpec((r, block), lambda i: (0, i))
    return pl.pallas_call(
        functools.partial(_qkv_grad_kernel, n),
        grid=(depth // block,),
        out_shape=[out, out],
        in_specs=[_smem()]
        + [lanes(v.shape[0]) for v in normed]
        + [anywhere] * n
        + [_rows(block, columns), lanes(1), lanes(8)],
        out_specs=[out_spec, out_spec],
        scratch_shapes=[
            pltpu.VMEM((rows, block), jnp.bfloat16),
            pltpu.VMEM((rows, columns), jnp.bfloat16),
            pltpu.VMEM((block, columns + SEG), jnp.float32),
            pltpu.SemaphoreType.DMA((n,)),
        ],
        compiler_params=_params(),
        cost_estimate=_cost(0, 0),
        name="qkv_grads",
    )(y, *normed, *grads, weight, gain, mlp_sum)


def _out_grad_kernel(left_ref, a0, a1, a2, a3, mine, theirs, right_s):
    width = a0.shape[2]

    @pl.when(pl.program_id(0) == 0)
    def _():
        for i, a in enumerate((a0, a2, a1, a3)):
            right_s[:, i * width : (i + 1) * width] = a[0]

    total = _dot(left_ref[...], right_s[...], TN).astype(mine.dtype)
    mine[...] = total[:, : 2 * width]
    theirs[...] = total[:, 2 * width :]


def out_grads(left, attended, block=256):
    rows, depth = left.shape
    width = attended[0][0].shape[2]
    out = jax.ShapeDtypeStruct((depth, 2 * width), jnp.bfloat16)
    member = lambda n: pl.BlockSpec((1, rows, width), lambda i: (n, 0, 0))
    return pl.pallas_call(
        _out_grad_kernel,
        grid=(depth // block,),
        out_shape=[out, out],
        in_specs=[pl.BlockSpec((rows, block), lambda i: (0, i))] + [member(n) for v, n in attended],
        out_specs=[_rows(block, 2 * width)] * 2,
        scratch_shapes=[pltpu.VMEM((rows, 4 * width), jnp.bfloat16)],
        compiler_params=_params(),
        cost_estimate=_cost(8 * rows * depth * width, 2 * rows * (depth + 4 * width) + 8 * depth * width),
        name="out_grads",
    )(left, *[v for v, n in attended])


def _pair_kernel(y_ref, a_ref, b_ref, near, far, acc):
    acc[...] = a_ref[...].astype(jnp.float32) + b_ref[...].astype(jnp.float32)
    _split_rows(acc, y_ref[0], near, far)


def pair_sum(y, a, b, size):
    depth, columns = a.shape
    block = 2 * size
    out = jax.ShapeDtypeStruct((depth // block, size, columns), jnp.bfloat16)
    out_spec = pl.BlockSpec((1, size, columns), lambda i: (i, 0, 0))
    return pl.pallas_call(
        _pair_kernel,
        grid=(depth // block,),
        out_shape=[out, out],
        in_specs=[_smem()] + [_rows(block, columns)] * 2,
        out_specs=[out_spec, out_spec],
        scratch_shapes=[pltpu.VMEM((block, columns), jnp.float32)],
        compiler_params=_params(),
        cost_estimate=_cost(0, 6 * depth * columns),
        name="pair_sum",
    )(y, a, b)


def _fold_kernel(z_ref, near, passed, *outs):
    count = near.shape[0]
    for step, out in enumerate(outs):
        row = lax.rem(z_ref[0] + step, count)
        out[...] = (near[row].astype(jnp.float32) + passed[row].astype(jnp.float32)).astype(out.dtype)


def fold(z, near, passed):
    count, size, columns = near.shape
    return pl.pallas_call(
        _fold_kernel,
        grid=(1,),
        out_shape=[jax.ShapeDtypeStruct((size, columns), jnp.bfloat16)] * count,
        in_specs=[_smem(), _full(near.shape), _full(near.shape)],
        out_specs=[_full((size, columns))] * count,
        compiler_params=_params(),
        cost_estimate=_cost(0, 0),
        name="fold",
    )(z, near, passed)


def _mid_kernel(p0, p1, p2, res_ref, cot_ref, gain_ref, near_ref, mate_ref, mid_ref, attn_ref, a0, a1, a2, a3, sum_ref):
    width = a0.shape[1]
    grad = p0[...].astype(jnp.float32) + p1[...].astype(jnp.float32) + p2[...].astype(jnp.float32)
    inverse, normed = _normed(res_ref[...])
    term = jnp.sum(grad * normed, axis=0, keepdims=True)

    @pl.when(pl.program_id(0) == 0)
    def _():
        sum_ref[...] = jnp.zeros_like(sum_ref)

    sum_ref[0:1, :] += term
    scaled = grad * gain_ref[...]
    mid = cot_ref[...] + inverse * (scaled - normed * jnp.mean(scaled * normed, axis=-1, keepdims=True))
    mid_ref[...] = mid
    low = mid.astype(jnp.bfloat16)
    attn_ref[...] = low
    a0[...] = _dot(low, near_ref[:, :width], NN).astype(jnp.bfloat16)
    a1[...] = _dot(low, mate_ref[:, :width], NN).astype(jnp.bfloat16)
    a2[...] = _dot(low, near_ref[:, width : 2 * width], NN).astype(jnp.bfloat16)
    a3[...] = _dot(low, mate_ref[:, width:], NN).astype(jnp.bfloat16)


def middle(parts, residual, cot, gain, weights, out_mate):
    rows, depth = residual.shape
    width = out_mate.shape[1] // 2
    tile = _row_tile(rows)
    return pl.pallas_call(
        _mid_kernel,
        grid=(rows // tile,),
        out_shape=[
            jax.ShapeDtypeStruct((rows, depth), jnp.float32),
            jax.ShapeDtypeStruct((rows, depth), jnp.bfloat16),
        ]
        + [jax.ShapeDtypeStruct((rows, width), jnp.bfloat16)] * 4
        + [jax.ShapeDtypeStruct((8, depth), jnp.float32)],
        in_specs=[_rows(tile, depth)] * 5
        + [
            _full((1, depth)),
            pl.BlockSpec((depth, 2 * width), lambda i: (0, weights.shape[1] // (2 * width) - 1)),
            _full(out_mate.shape),
        ],
        out_specs=[_rows(tile, depth)] * 2 + [_rows(tile, width)] * 4 + [_full((8, depth))],
        compiler_params=_params(),
        cost_estimate=_cost(2 * rows * depth * 4 * width, rows * depth * 20),
        name="middle",
    )(*parts, residual, cot, gain, weights, out_mate)


def _back_kernel(add, grad_ref, w_ref, *refs):
    part = _dot(grad_ref[...], w_ref[...], NT)
    if add:
        part = part + refs[0][...].astype(jnp.float32)
    refs[-1][...] = part.astype(refs[-1].dtype)


def project_back(grad, weight, add=None):
    rows, columns = grad.shape
    depth = weight.shape[0]
    tile = _row_tile(rows)
    extra = [] if add is None else [add]
    return pl.pallas_call(
        functools.partial(_back_kernel, add is not None),
        grid=(rows // tile,),
        out_shape=jax.ShapeDtypeStruct((rows, depth), jnp.bfloat16),
        in_specs=[_rows(tile, columns), _full((depth, columns))] + [_rows(tile, depth)] * len(extra),
        out_specs=_rows(tile, depth),
        compiler_params=_params(),
        cost_estimate=_cost(0, 0),
        name="project_back",
    )(grad, weight, *extra)


def _last_kernel(p0, p1, p2, x_ref, mid_ref, gain_ref, out_ref):
    grad = p0[...].astype(jnp.float32) + p1[...].astype(jnp.float32) + p2[...].astype(jnp.float32)
    inverse, normed = _normed(x_ref[...].astype(jnp.float32))
    scaled = grad * gain_ref[...]
    out_ref[...] = mid_ref[...] + inverse * (
        scaled - normed * jnp.mean(scaled * normed, axis=-1, keepdims=True)
    )


def last(parts, x, mid, gain):
    rows, depth = x.shape
    tile = _row_tile(rows)
    return pl.pallas_call(
        _last_kernel,
        grid=(rows // tile,),
        out_shape=jax.ShapeDtypeStruct((rows, depth), jnp.float32),
        in_specs=[_rows(tile, depth)] * 5 + [_full((1, depth))],
        out_specs=_rows(tile, depth),
        compiler_params=_params(),
        cost_estimate=_cost(0, rows * depth * 16),
        name="last",
    )(*parts, x, mid, gain)


def _half_place(info_ref, b, half, piece_blocks):
    block = 2 * b + half
    piece = lax.bitwise_xor(lax.div(block, piece_blocks), info_ref[0])
    return piece, lax.rem(block, piece_blocks) * SEG


def _mask(heads, same, causal):
    key = lax.broadcasted_iota(jnp.int32, (QB, heads * QB), 0)
    query = lax.broadcasted_iota(jnp.int32, (QB, heads * QB), 1) % QB
    allowed = jnp.logical_not(same & ((key // SEG) != (query // SEG)))
    if causal:
        allowed = allowed & (key <= query)
    return allowed


def _spread(block, heads):
    turned = block.T
    lane = lax.broadcasted_iota(jnp.int32, turned.shape, 0) // HDIM
    zero = jnp.zeros_like(turned)
    return jnp.concatenate([jnp.where(lane == h, turned, zero) for h in range(heads)], axis=1)


def _stack(block, heads):
    lane = lax.broadcasted_iota(jnp.int32, block.shape, 1) // HDIM
    zero = jnp.zeros_like(block)
    return jnp.concatenate([jnp.where(lane == h, block, zero) for h in range(heads)], axis=0)


def _parents(info_ref, b):
    leaf = 2 * (b - (TRUNK + 4 * SEG) // QB)
    return [pl.multiple_of(TRUNK - SEG + SEG * info_ref[2 + leaf + side], SEG) for side in (0, 1)]


def _attn_fwd_kernel(heads, piece_count, info_ref, *refs):
    pieces = refs[:piece_count]
    out_ref, lse_ref = refs[piece_count : piece_count + 2]
    q_s, k_s, vt_s, qt_s, s_s, p_s, m_s, l_s, acc_s, kp_s, vp_s = refs[piece_count + 2 :]
    width = heads * HDIM
    piece_rows = pieces[0].shape[0]
    tensor = info_ref[0]
    base = info_ref[1]
    trunk_blocks = TRUNK // QB
    leaf_block = (TRUNK + 4 * SEG) // QB
    for j in range(piece_count):
        at = pl.multiple_of(piece_rows * lax.bitwise_xor(tensor, j), SEG)
        q_s[pl.ds(at, piece_rows), :] = pieces[j][:, :width] * jnp.asarray(HDIM**-0.5, jnp.bfloat16)
        k_s[pl.ds(at, piece_rows), :] = pieces[j][:, width : 2 * width]
        vt_s[:, pl.ds(at, piece_rows)] = pieces[j][:, 2 * width :].T

    def q_block(i, carry):
        b = base + i
        row = pl.multiple_of(b * QB, QB)
        own = pl.ds(row, QB)
        leaf = b >= leaf_block
        qt_s[...] = _spread(q_s[own, :], heads)

        def score(keys, at, size, allowed):
            scores = _dot(keys, qt_s[...], NN)
            if allowed is not None:
                scores = jnp.where(allowed, scores, -1e30)
            s_s[pl.ds(at, size), :] = scores
            return jnp.max(scores, axis=0, keepdims=True)

        m_s[0:1, :] = score(k_s[own, :], TRUNK, QB, _mask(heads, b >= trunk_blocks, True))

        @pl.when(leaf)
        def _():
            for side, at in enumerate(_parents(info_ref, b)):
                kp_s[side * SEG : (side + 1) * SEG, :] = k_s[pl.ds(at, SEG), :]
                vp_s[:, side * SEG : (side + 1) * SEG] = vt_s[:, pl.ds(at, SEG)]
            top = score(kp_s[...], TRUNK + QB, QB, _mask(heads, True, False))
            m_s[0:1, :] = jnp.maximum(m_s[0:1, :], top)

        @pl.when(b >= trunk_blocks)
        def _():
            m_s[0:1, :] = jnp.maximum(m_s[0:1, :], score(k_s[:TRUNK, :], 0, TRUNK, None))

        @pl.when(b < trunk_blocks)
        def _():
            def chunk(c, carry):
                at = pl.multiple_of(c * QB, QB)
                m_s[0:1, :] = jnp.maximum(m_s[0:1, :], score(k_s[pl.ds(at, QB), :], at, QB, None))
                return carry

            lax.fori_loop(0, b, chunk, 0)

        def mix(values, at, size, fresh):
            probs = jnp.exp(s_s[pl.ds(at, size), :] - m_s[0:1, :])
            total = jnp.sum(probs, axis=0, keepdims=True)
            p_s[pl.ds(at, size), :] = probs.astype(jnp.bfloat16)
            l_s[0:1, :] = total if fresh else l_s[0:1, :] + total
            for h in range(heads):
                of = slice(h * HDIM, (h + 1) * HDIM)
                term = _dot(values(of), p_s[pl.ds(at, size), h * QB : (h + 1) * QB], NN)
                acc_s[of, :] = term if fresh else acc_s[of, :] + term

        mix(lambda of: vt_s[of, own], TRUNK, QB, True)

        @pl.when(leaf)
        def _():
            mix(lambda of: vp_s[of, :], TRUNK + QB, QB, False)

        @pl.when(b >= trunk_blocks)
        def _():
            mix(lambda of: vt_s[of, :TRUNK], 0, TRUNK, False)

        @pl.when(b < trunk_blocks)
        def _():
            def chunk(c, carry):
                at = pl.multiple_of(c * QB, QB)
                mix(lambda of: vt_s[of, pl.ds(at, QB)], at, QB, False)
                return carry

            lax.fori_loop(0, b, chunk, 0)

        mixed = []
        for h in range(heads):
            columns = slice(h * QB, (h + 1) * QB)
            total = l_s[0:1, columns]
            lse_ref[h : h + 1, pl.ds(pl.multiple_of(i * QB, QB), QB)] = m_s[0:1, columns] + jnp.log(total)
            mixed.append(acc_s[h * HDIM : (h + 1) * HDIM, :] / total)
        mixed = jnp.concatenate(mixed, axis=0).T.astype(jnp.bfloat16)
        for half in (0, 1):
            piece, at = _half_place(info_ref, b, half, piece_rows // SEG)
            at = pl.multiple_of(at, SEG)
            out_ref[lax.bitwise_and(piece, 1), pl.ds(at, SEG), :] = mixed[half * SEG : (half + 1) * SEG]
        return carry

    lax.fori_loop(0, lse_ref.shape[1] // QB, q_block, 0)


def attention_forward(info, pieces, heads):
    rows = sum(p.shape[0] for p in pieces)
    piece_rows = pieces[0].shape[0]
    width = heads * HDIM
    half = rows // 2
    bf16, f32 = jnp.bfloat16, jnp.float32
    return pl.pallas_call(
        functools.partial(_attn_fwd_kernel, heads, len(pieces)),
        out_shape=[
            jax.ShapeDtypeStruct((2, piece_rows, width), bf16),
            jax.ShapeDtypeStruct((8, half), f32),
        ],
        grid=(1,),
        in_specs=[_smem()] + [_full(p.shape) for p in pieces],
        out_specs=[_full((2, piece_rows, width)), _full((8, half))],
        scratch_shapes=[
            pltpu.VMEM((rows, width), bf16),
            pltpu.VMEM((rows, width), bf16),
            pltpu.VMEM((width, rows), bf16),
            pltpu.VMEM((width, heads * QB), bf16),
            pltpu.VMEM((TRUNK + 2 * QB, heads * QB), f32),
            pltpu.VMEM((TRUNK + 2 * QB, heads * QB), bf16),
            pltpu.VMEM((8, heads * QB), f32),
            pltpu.VMEM((8, heads * QB), f32),
            pltpu.VMEM((width, QB), f32),
            pltpu.VMEM((QB, width), bf16),
            pltpu.VMEM((width, QB), bf16),
        ],
        compiler_params=_params(),
        cost_estimate=_cost(rows * 1400 * width * 4, rows * width * 8),
        name="attn_fwd",
    )(info, *pieces)


def _attn_bwd_kernel(heads, info_ref, *refs):
    n = 4
    pieces, mixed_in, grads = refs[:n], refs[n : n + 2], refs[n + 2 : 2 * n + 2]
    lse_refs = refs[2 * n + 2 : 2 * n + 4]
    outs = refs[2 * n + 4 : 3 * n + 4]
    q_s, k_s, kt_s, v_s, o_s, g_s, dk_s, dv_s, lse_s = refs[3 * n + 4 : 3 * n + 13]
    qt_s, gt_s, qm_s, gm_s, row_s, delta_s, acc_s, kp_s, vp_s, kpt_s = refs[3 * n + 13 :]
    width = heads * HDIM
    piece_rows = pieces[0].shape[0]
    tensor = info_ref[0]
    chip = lax.div(tensor, 2)
    half_rows = lse_refs[0].shape[1]
    scale = HDIM**-0.5
    trunk_blocks = TRUNK // QB
    leaf_block = (TRUNK + 4 * SEG) // QB
    for j in range(n):
        rows_at = pl.ds(pl.multiple_of(piece_rows * lax.bitwise_xor(tensor, j), SEG), piece_rows)
        q_s[rows_at, :] = pieces[j][:, :width] * jnp.asarray(scale, jnp.bfloat16)
        k_s[rows_at, :] = pieces[j][:, width : 2 * width]
        kt_s[:, rows_at] = pieces[j][:, width : 2 * width].T
        v_s[rows_at, :] = pieces[j][:, 2 * width :]
        o_s[rows_at, :] = mixed_in[j // 2][j % 2]
        g_s[rows_at, :] = grads[j][...]
    lse_s[:, pl.ds(pl.multiple_of(chip * half_rows, SEG), half_rows)] = lse_refs[0][...]
    lse_s[:, pl.ds(pl.multiple_of((1 - chip) * half_rows, SEG), half_rows)] = lse_refs[1][...]
    dk_s[...] = jnp.zeros_like(dk_s)
    dv_s[...] = jnp.zeros_like(dv_s)
    head_of_lane = lax.broadcasted_iota(jnp.int32, (8, width), 1) // HDIM
    pick = jnp.where(lax.broadcasted_iota(jnp.int32, (8, width), 0) == head_of_lane, 1.0, 0.0)

    def q_block(b, carry):
        row = pl.multiple_of(b * QB, QB)
        own = pl.ds(row, QB)
        both = o_s[own, :].astype(jnp.float32) * g_s[own, :].astype(jnp.float32)
        delta = lax.dot_general(
            pick, both, NT, precision=lax.Precision.HIGHEST, preferred_element_type=jnp.float32
        )
        for h in range(heads):
            columns = slice(h * QB, (h + 1) * QB)
            delta_s[0:1, columns] = delta[h : h + 1, :]
            row_s[0:1, columns] = lse_s[h : h + 1, own]
        qt_s[...] = _spread(q_s[own, :], heads)
        gt_s[...] = _spread(g_s[own, :], heads)
        qm_s[...] = _stack(q_s[own, :], heads)
        gm_s[...] = _stack(g_s[own, :], heads)

        def step(k, v, kt, allowed, fresh, targets):
            scores = _dot(k, qt_s[...], NN)
            probs_grad = _dot(v, gt_s[...], NN)
            probs = jnp.exp(scores - row_s[0:1, :])
            if allowed is not None:
                probs = jnp.where(allowed, probs, 0.0)
            ds = (probs * (probs_grad - delta_s[0:1, :])).astype(jnp.bfloat16)
            dv = _dot(probs.astype(jnp.bfloat16), gm_s[...], NN)
            dk = _dot(ds, qm_s[...], NN)
            for h in range(heads):
                of = slice(h * HDIM, (h + 1) * HDIM)
                term = _dot(kt(of), ds[:, h * QB : (h + 1) * QB], NN)
                acc_s[of, :] = term if fresh else acc_s[of, :] + term
            first = 0
            for at, size in targets:
                dv_s[pl.ds(at, size), :] += dv[first : first + size]
                dk_s[pl.ds(at, size), :] += dk[first : first + size]
                first += size

        step(
            k_s[own, :], v_s[own, :], lambda of: kt_s[of, own],
            _mask(heads, b >= trunk_blocks, True), True, [(row, QB)],
        )

        @pl.when(b >= leaf_block)
        def _():
            ats = _parents(info_ref, b)
            for side, at in enumerate(ats):
                part = slice(side * SEG, (side + 1) * SEG)
                kp_s[part, :] = k_s[pl.ds(at, SEG), :]
                vp_s[part, :] = v_s[pl.ds(at, SEG), :]
                kpt_s[:, part] = kt_s[:, pl.ds(at, SEG)]
            step(
                kp_s[...], vp_s[...], lambda of: kpt_s[of, :],
                _mask(heads, True, False), False, [(at, SEG) for at in ats],
            )

        def trunk_step(c):
            at = pl.multiple_of(c * QB, QB)
            here = pl.ds(at, QB)
            step(k_s[here, :], v_s[here, :], lambda of: kt_s[of, here], None, False, [(at, QB)])

        def trunk_pair(c, carry):
            trunk_step(2 * c)
            trunk_step(2 * c + 1)
            return carry

        count = jnp.minimum(b, trunk_blocks)
        lax.fori_loop(0, lax.div(count, 2), trunk_pair, 0)

        @pl.when(lax.rem(count, 2) == 1)
        def _():
            trunk_step(count - 1)

        q_s[own, :] = (acc_s[...] * scale).T.astype(jnp.bfloat16)
        return carry

    lax.fori_loop(0, q_s.shape[0] // QB, q_block, 0)
    for j in range(n):
        rows_at = pl.ds(pl.multiple_of(piece_rows * lax.bitwise_xor(tensor, j), SEG), piece_rows)
        outs[j][:, :width] = q_s[rows_at, :]
        outs[j][:, width : 2 * width] = dk_s[rows_at, :].astype(jnp.bfloat16)
        outs[j][:, 2 * width :] = dv_s[rows_at, :].astype(jnp.bfloat16)


def attention_backward(info, pieces, mixed, grads, lses, heads):
    n = len(pieces)
    piece_rows = pieces[0].shape[0]
    rows = n * piece_rows
    width = heads * HDIM
    bf16, f32 = jnp.bfloat16, jnp.float32
    rows_low = pltpu.VMEM((rows, width), bf16)
    return pl.pallas_call(
        functools.partial(_attn_bwd_kernel, heads),
        out_shape=[jax.ShapeDtypeStruct((piece_rows, 3 * width), bf16)] * n,
        grid=(1,),
        in_specs=[_smem()] + [_full(v.shape) for v in (*pieces, *mixed, *grads, *lses)],
        out_specs=[_full((piece_rows, 3 * width))] * n,
        scratch_shapes=[
            rows_low,
            rows_low,
            pltpu.VMEM((width, rows), bf16),
            rows_low,
            rows_low,
            rows_low,
            pltpu.VMEM((rows, width), f32),
            pltpu.VMEM((rows, width), f32),
            pltpu.VMEM((8, rows), f32),
            pltpu.VMEM((width, heads * QB), bf16),
            pltpu.VMEM((width, heads * QB), bf16),
            pltpu.VMEM((heads * QB, width), bf16),
            pltpu.VMEM((heads * QB, width), bf16),
            pltpu.VMEM((8, heads * QB), f32),
            pltpu.VMEM((8, heads * QB), f32),
            pltpu.VMEM((width, QB), f32),
            pltpu.VMEM((QB, width), bf16),
            pltpu.VMEM((QB, width), bf16),
            pltpu.VMEM((width, QB), bf16),
        ],
        compiler_params=_params(),
        cost_estimate=_cost(0, 0),
        name="attn_bwd",
    )(info, *pieces, *mixed, *grads, *lses)


def mate(x):
    return lax.ppermute(x, "tensor", [(i, i ^ 1) for i in range(4)])


def across(x):
    return lax.ppermute(x, "tensor", [(i, i ^ 2) for i in range(4)])


def corner(x):
    return lax.ppermute(x, "tensor", [(i, i ^ 3) for i in range(4)])


def beside(x):
    return lax.ppermute(x, "dp", [(i, i ^ 1) for i in range(8)])


def ahead(x, step):
    return lax.ppermute(x, "dp", [(i, (i + 2 * step) % 8) for i in range(8)])


def after(x, *others):
    return lax.optimization_barrier((x, *others))[0]


def after_all(values, *others):
    return list(lax.optimization_barrier((*values, *others))[: len(values)])


def line_hops(x):
    return [x] + [ahead(x, step) for step in (1, 3, 2)]


def spread_hops(line, far):
    dp = lax.axis_index("dp")
    z, y = dp // 2, dp % 2
    order = jnp.array([0, 1, 3, 2], jnp.int32)
    from_z = (z - order) % 4
    where = jnp.concatenate([2 * from_z + y, 2 * from_z + 1 - y]).astype(jnp.int32)
    return place(where, line + far)


def fold_hops(near, passed):
    z = (lax.axis_index("dp") // 2).astype(jnp.int32)[None]
    return fold(z, near, passed)


def send_hops(chunks):
    return [chunks[0]] + [ahead(chunks[step], step) for step in (2, 1, 3)]


def sum_hops(received):
    return sum(v.astype(jnp.float32) for v in received)


def body(
    block_input,
    norm_gains,
    qkv_weight,
    out_weight,
    gate_up_weight,
    down_weight,
    parent_of_row,
    cotangent,
):
    bf16, f32 = jnp.bfloat16, jnp.float32
    shard = qkv_weight.shape[1]
    width = qkv_weight.shape[2]
    hidden_width = gate_up_weight.shape[2]
    heads = width // HDIM
    rows = parent_of_row.shape[0]
    tensor = lax.axis_index("tensor")
    chip = tensor // 2
    y = (lax.axis_index("dp") % 2).astype(jnp.int32)[None]
    leaf_first = TRUNK + 4 * SEG
    parents = parent_of_row[leaf_first::SEG]
    half_blocks = rows // (2 * QB)
    place_own = jnp.stack([tensor, half_blocks * chip]).astype(jnp.int32)
    place_far = jnp.stack([tensor, half_blocks * (1 - chip)]).astype(jnp.int32)
    info_own = jnp.concatenate([place_own, parents])
    info_far = jnp.concatenate([place_far, parents])

    gains_shard = jnp.pad(norm_gains.astype(bf16).T, ((0, 0), (0, SEG - 2)))
    qkv_shard = qkv_weight.astype(bf16).transpose(1, 0, 2).reshape(shard, 3 * width)
    first_line = line_hops(jnp.concatenate([qkv_shard, gains_shard], axis=1))
    out_shard = out_weight.astype(bf16).T
    out_x = across(out_shard)
    beyond = across(after(block_input, out_x))
    near_x = mate(block_input)
    gate_up_shard = gate_up_weight.astype(bf16).transpose(1, 0, 2).reshape(shard, 2 * hidden_width)
    rest = lax.all_gather(after(gate_up_shard, out_x), "dp", axis=0, tiled=True)
    first_far = [beside(v) for v in first_line]
    first = spread_hops(first_line, first_far)
    second_shard = jnp.concatenate([down_weight.astype(bf16).T, out_shard, out_x], axis=1)
    down_line = line_hops(after(second_shard, *first_line))
    gains_low = first[:, 3 * width : 3 * width + 2].T.astype(f32)
    gain_attn, gain_mlp = gains_low[0:1], gains_low[1:2]
    n0, n1, p0, p1 = project(block_input, near_x, gain_attn, first, 3 * width)
    inputs = [block_input, near_x, beyond, mate(beyond)]
    n2, n3, p2, p3 = project(inputs[2], after(inputs[3], p1), gain_attn, first, 3 * width)
    normed_attn, projected = [n0, n1, n2, n3], [p0, p1, p2, p3]
    cot_low = cotangent.astype(bf16)
    cot_x = across(after(cot_low, beyond))

    own, lse_own = attention_forward(info_own, projected, heads)
    own_x, own_m = across(after(own, cot_x)), mate(own)
    down_far = [beside(after(down_line[0], p1)), beside(after(down_line[1], own)), beside(after(down_line[2], own))]
    cot_near = mate(after(cot_low, own))
    far, lse_far = attention_forward(after(info_far, own), projected, heads)
    down_far += [beside(after(v, far)) for v in down_line[3:]]
    far_m, own_xm = mate(far), mate(after(own_x, far))
    far_x = across(far)
    down_low = spread_hops(down_line, down_far)
    cot_rows = [cot_low, cot_near, cot_x, mate(after(cot_x, far))]
    out_far = mate(down_low[:, hidden_width:])

    own_rows = [(own, 0), (own_m, 1), (far_x, 0), None]
    hidden_far, grads_far, normed_far, part3, part2, branch3, branch2 = mlp(
        [(far, 1), (far_m, 0), (own_x, 1), (own_xm, 0)],
        [(far, 0), (far_m, 1), (own_x, 0), (own_xm, 1)],
        [inputs[3], inputs[2]], [cot_rows[3], cot_rows[2]], gain_mlp, rest, down_low, out_far, False,
    )
    far_xm = mate(after(far_x, part3))
    own_rows[3] = (far_xm, 1)
    passed = (part2.astype(f32) + mate(after(part3, far_x)).astype(f32)).astype(bf16)
    passed_x = across(passed)
    hidden_own, grads_own, normed_own, part1, part0, branch1, branch0, residual_mid = mlp(
        [(own, 1), (own_m, 0), (far_x, 1), (far_xm, 0)], own_rows,
        [inputs[1], inputs[0]], [after(cot_rows[1], passed), cot_rows[0]],
        gain_mlp, rest, down_low, out_far, True,
    )
    mlp_parts = [part0, mate(after(part1, passed_x)), passed_x]

    grad_sum = mlp_grads(
        [after(normed_far, passed_x), normed_own],
        [cot_rows[n] for n in (3, 2, 1, 0)],
        [grads_far, grads_own],
        [hidden_far, hidden_own],
    )
    mid_grad, attn_grad, g0, g1, g2, g3, mlp_sum = middle(
        [after(mlp_parts[0], grad_sum), *mlp_parts[1:]], residual_mid, cotangent, gain_mlp, down_low, out_far
    )
    grad_sum = lax.psum_scatter(grad_sum, "dp", scatter_dimension=0, tiled=True)
    g_x, g_c, g_m = across(g2), corner(g3), mate(g1)
    out_mine, out_theirs = out_grads(attn_grad, own_rows)
    out_theirs = mate(out_theirs)
    branch_passed = (branch2.astype(f32) + mate(branch3).astype(f32)).astype(bf16)
    out_pair = pair_sum(y, out_mine, after(out_theirs, branch_passed), shard)
    out_y = beside(out_pair[1])
    branch_x = across(after(branch_passed, g_x, g_c))

    bwd_grads = after_all([g0, g_m, g_x, g_c], out_pair[1], branch_passed)
    projected_grad = attention_backward(
        info_own, projected, [own, far], bwd_grads, [lse_own, lse_far], heads
    )
    out_chunks = fold_hops(out_pair[0], after(out_y, *projected_grad, branch_x))
    out_received = send_hops(out_chunks)
    qkv_pair = qkv_grads(
        y, normed_attn, after_all(projected_grad, out_chunks[1]), first, gain_attn, mlp_sum, shard
    )
    qkv_y = beside(qkv_pair[1])
    back3 = project_back(after(projected_grad[3], qkv_pair[1]), first)
    back2 = project_back(projected_grad[2], first, mate(back3))
    back_x = across(back2)
    back1 = project_back(after(projected_grad[1], back2, *out_received), first)
    back0 = project_back(after(projected_grad[0], back1), first)
    branch_sum = branch0.astype(f32) + mate(branch1).astype(f32)
    block_output = residual_mid + branch_sum + after(branch_x, back0).astype(f32)
    qkv_chunks = fold_hops(qkv_pair[0], after(qkv_y, back0, block_output))
    qkv_received = send_hops(qkv_chunks)
    back_m = mate(after(back1, qkv_y))
    input_grad = last([back0, back_m, after(back_x, qkv_chunks[1])], block_input, mid_grad, gain_attn)
    grad_sum = after(grad_sum, input_grad).astype(f32)
    down_out = grad_sum[:, 2 * hidden_width :].T
    gate_up_out = grad_sum[:, : 2 * hidden_width].reshape(shard, 2, hidden_width).transpose(1, 0, 2)
    out_sum = sum_hops(out_received)
    qkv_sum = sum_hops(after_all(qkv_received, input_grad))
    qkv_out = qkv_sum[:, : 3 * width].reshape(shard, 3, width).transpose(1, 0, 2)
    gains_sum = qkv_sum[:, 3 * width :]
    gains_sum = gains_sum + mate(gains_sum.astype(bf16)).astype(f32)
    from_x = across(jnp.concatenate([out_sum[:, width:], gains_sum], axis=1).astype(bf16)).astype(f32)
    out_out = (out_sum[:, :width] + from_x[:, :width]).T
    gains_out = (gains_sum + from_x[:, width:])[:, :2].T
    return (block_output, input_grad, gains_out, qkv_out, out_out, gate_up_out, down_out)


def solution(mesh):
    placed = (
        P(("dp", "tensor"), None),
        P(None, "dp"),
        P(None, "dp", "tensor"),
        P("tensor", "dp"),
        P(None, "dp", "tensor"),
        P("tensor", "dp"),
        P("dp"),
        P(("dp", "tensor"), None),
    )
    four_by_eight = mesh.shape["tensor"] == 4 and mesh.shape["dp"] == 8
    return jax.shard_map(
        body if four_by_eight else body_any_mesh,
        mesh=mesh,
        in_specs=placed,
        out_specs=(
            P(("dp", "tensor"), None),
            P(("dp", "tensor"), None),
            P(None, "dp"),
            P(None, "dp", "tensor"),
            P("tensor", "dp"),
            P(None, "dp", "tensor"),
            P("tensor", "dp"),
        ),
        check_vma=False,
    )
```

```python
import functools
import jax
import jax.numpy as jnp
from jax import lax
from jax.experimental import pallas as pl
from jax.experimental.pallas import tpu as pltpu
from jax.sharding import PartitionSpec as P

HDIM = 64
TRUNK = 1024
SEG = 128
ROW_TREE = 2560


epsilon = 1e-06


def norm_rows(values, gain_row):
    inverse_rms = lax.rsqrt(jnp.mean(values * values, axis=-1, keepdims=True) + epsilon)
    return values * inverse_rms * gain_row


def segment_ids(row_count):
    position = jnp.arange(row_count, dtype=jnp.int32)
    tree_base = position // ROW_TREE * 13
    within = position % ROW_TREE
    beyond = within - TRUNK
    own_segment = jnp.where(
        within < TRUNK,
        0,
        jnp.where(beyond < 4 * SEG, 1 + beyond // SEG, 5 + (beyond - 4 * SEG) // SEG),
    )
    return (own_segment + tree_base, tree_base)


def body_any_mesh(
    block_input,
    norm_gains,
    qkv_weight,
    out_weight,
    gate_up_weight,
    down_weight,
    parent_of_row,
    cotangent,
):
    gains_cast = norm_gains.astype(jnp.bfloat16)
    qkv_cast = qkv_weight.astype(jnp.bfloat16)
    out_cast = out_weight.astype(jnp.bfloat16)
    gate_up_cast = gate_up_weight.astype(jnp.bfloat16)
    down_cast = down_weight.astype(jnp.bfloat16)
    gains_low, qkv_low, out_low, gate_up_low, down_low = (
        lax.all_gather(gains_cast, "dp", axis=1, tiled=True),
        lax.all_gather(qkv_cast, "dp", axis=1, tiled=True),
        lax.all_gather(out_cast, "dp", axis=1, tiled=True),
        lax.all_gather(gate_up_cast, "dp", axis=1, tiled=True),
        lax.all_gather(down_cast, "dp", axis=1, tiled=True),
    )
    row_count = parent_of_row.shape[0]
    width_local = qkv_low.shape[2]
    head_local = width_local // HDIM
    block_rows = min(512, row_count)
    block_count = row_count // block_rows
    score_scale = float(HDIM) ** (-0.5)
    segment_of_row, trunk_of_row = segment_ids(row_count)
    parent_segment = parent_of_row + trunk_of_row
    column_index = jnp.arange(row_count, dtype=jnp.int32)
    residual_in = block_input.astype(jnp.float32)
    gain_attn = gains_low[0].astype(jnp.float32)
    gain_mlp = gains_low[1].astype(jnp.float32)
    normed_attn = lax.all_gather(
        norm_rows(residual_in, gain_attn).astype(jnp.bfloat16), "tensor", axis=0, tiled=True
    )
    projected = jnp.einsum(
        "rd,cde->cre", normed_attn, qkv_low, preferred_element_type=jnp.float32
    ).astype(jnp.bfloat16)
    query_rows = projected[0].reshape(row_count, head_local, HDIM)
    key_rows = projected[1].reshape(row_count, head_local, HDIM)
    value_rows = projected[2].reshape(row_count, head_local, HDIM)

    def block_scores(block_index):
        row_start = block_index * block_rows
        query_block = lax.dynamic_slice_in_dim(query_rows, row_start, block_rows, 0)
        scores = (
            jnp.einsum("qhd,khd->hqk", query_block, key_rows, preferred_element_type=jnp.float32)
            * score_scale
        )
        row_index = row_start + jnp.arange(block_rows, dtype=jnp.int32)
        row_segment = lax.dynamic_slice_in_dim(segment_of_row, row_start, block_rows, 0)
        row_parent = lax.dynamic_slice_in_dim(parent_segment, row_start, block_rows, 0)
        row_trunk = lax.dynamic_slice_in_dim(trunk_of_row, row_start, block_rows, 0)
        column_segment = segment_of_row[None, :]
        allowed = (column_index[None, :] <= row_index[:, None]) & (
            (column_segment == row_segment[:, None])
            | (column_segment == row_parent[:, None])
            | (column_segment == row_trunk[:, None])
        )
        return (jnp.where(allowed[None], scores, -1e30), query_block)

    def attend_block(block_index):
        scores, query_block = block_scores(block_index)
        top_score = jnp.max(scores, axis=-1, keepdims=True)
        exp_scores = jnp.exp(scores - top_score)
        row_total = jnp.sum(exp_scores, axis=-1, keepdims=True)
        softmax_low = (exp_scores / row_total).astype(jnp.bfloat16)
        mixed_heads = jnp.einsum(
            "hqk,khd->qhd", softmax_low, value_rows, preferred_element_type=jnp.float32
        ).astype(jnp.bfloat16)
        return (mixed_heads, (top_score + jnp.log(row_total))[..., 0])

    block_ids = jnp.arange(block_count, dtype=jnp.int32)
    attended, log_totals = lax.map(attend_block, block_ids)
    attended = attended.reshape(row_count, width_local)
    attn_partial = jnp.dot(attended, out_low, preferred_element_type=jnp.float32)
    residual_mid = residual_in + lax.psum_scatter(
        attn_partial, "tensor", scatter_dimension=0, tiled=True
    )
    normed_mlp = lax.all_gather(
        norm_rows(residual_mid, gain_mlp).astype(jnp.bfloat16), "tensor", axis=0, tiled=True
    )
    gate_up = jnp.einsum(
        "rd,cdf->crf", normed_mlp, gate_up_low, preferred_element_type=jnp.float32
    ).astype(jnp.bfloat16)
    gate_value = gate_up[0].astype(jnp.float32)
    up_value = gate_up[1].astype(jnp.float32)
    sigmoid_gate = jax.nn.sigmoid(gate_value)
    hidden = (gate_value * sigmoid_gate * up_value).astype(jnp.bfloat16)
    mlp_partial = jnp.dot(hidden, down_low, preferred_element_type=jnp.float32)
    block_output = residual_mid + lax.psum_scatter(
        mlp_partial.astype(jnp.bfloat16), "tensor", scatter_dimension=0, tiled=True
    ).astype(jnp.float32)
    gains_again = norm_gains.astype(jnp.bfloat16)
    qkv_again = qkv_weight.astype(jnp.bfloat16)
    out_again = out_weight.astype(jnp.bfloat16)
    gate_up_again = gate_up_weight.astype(jnp.bfloat16)
    down_again = down_weight.astype(jnp.bfloat16)
    gains_low, qkv_low, out_low, gate_up_low, down_low = (
        lax.all_gather(gains_again, "dp", axis=1, tiled=True),
        lax.all_gather(qkv_again, "dp", axis=1, tiled=True),
        lax.all_gather(out_again, "dp", axis=1, tiled=True),
        lax.all_gather(gate_up_again, "dp", axis=1, tiled=True),
        lax.all_gather(down_again, "dp", axis=1, tiled=True),
    )
    gain_attn = gains_low[0].astype(jnp.float32)
    gain_mlp = gains_low[1].astype(jnp.float32)
    mlp_grad_rows = lax.all_gather(cotangent.astype(jnp.bfloat16), "tensor", axis=0, tiled=True)
    down_grad = jnp.einsum("rf,rd->fd", hidden, mlp_grad_rows, preferred_element_type=jnp.float32)
    hidden_grad = jnp.einsum(
        "rd,fd->rf", mlp_grad_rows, down_low, preferred_element_type=jnp.float32
    )
    gate_grad = hidden_grad * up_value * sigmoid_gate * (1.0 + gate_value * (1.0 - sigmoid_gate))
    up_grad = hidden_grad * gate_value * sigmoid_gate
    gate_up_grad_low = jnp.stack([gate_grad, up_grad]).astype(jnp.bfloat16)
    gate_up_grad = jnp.einsum(
        "rd,crf->cdf", normed_mlp, gate_up_grad_low, preferred_element_type=jnp.float32
    )
    normed_mlp_part = jnp.einsum(
        "crf,cdf->rd", gate_up_grad_low, gate_up_low, preferred_element_type=jnp.float32
    )
    normed_mlp_grad = lax.psum_scatter(normed_mlp_part, "tensor", scatter_dimension=0, tiled=True)
    norm_back_mlp = jax.vjp(norm_rows, residual_mid, gain_mlp)[1]
    mid_from_norm, gain_mlp_grad = norm_back_mlp(normed_mlp_grad)
    mid_grad = cotangent + mid_from_norm
    attn_grad_rows = lax.all_gather(mid_grad.astype(jnp.bfloat16), "tensor", axis=0, tiled=True)
    out_grad = jnp.einsum("re,rd->ed", attended, attn_grad_rows, preferred_element_type=jnp.float32)
    attended_grad = jnp.einsum(
        "rd,ed->re", attn_grad_rows, out_low, preferred_element_type=jnp.float32
    ).astype(jnp.bfloat16)
    attended_grad = attended_grad.reshape(row_count, head_local, HDIM)

    def back_block(carry, block_inputs):
        key_grad, value_grad = carry
        block_index, log_total = block_inputs
        scores, query_block = block_scores(block_index)
        probs = jnp.exp(scores - log_total[..., None])
        grad_block = lax.dynamic_slice_in_dim(
            attended_grad, block_index * block_rows, block_rows, 0
        )
        probs_grad = jnp.einsum(
            "qhd,khd->hqk", grad_block, value_rows, preferred_element_type=jnp.float32
        )
        inner_term = jnp.sum(probs * probs_grad, axis=-1, keepdims=True)
        score_grad = (probs * (probs_grad - inner_term)).astype(jnp.bfloat16)
        query_grad = (
            jnp.einsum("hqk,khd->qhd", score_grad, key_rows, preferred_element_type=jnp.float32)
            * score_scale
        )
        key_grad = (
            key_grad
            + jnp.einsum(
                "hqk,qhd->khd", score_grad, query_block, preferred_element_type=jnp.float32
            )
            * score_scale
        )
        value_grad = value_grad + jnp.einsum(
            "hqk,qhd->khd",
            probs.astype(jnp.bfloat16),
            grad_block,
            preferred_element_type=jnp.float32,
        )
        return ((key_grad, value_grad), query_grad)

    zero_grad = jnp.zeros((row_count, head_local, HDIM), jnp.float32)
    carried, query_grads = lax.scan(back_block, (zero_grad, zero_grad), (block_ids, log_totals))
    projected_grad = jnp.stack(
        [
            query_grads.reshape(row_count, width_local),
            carried[0].reshape(row_count, width_local),
            carried[1].reshape(row_count, width_local),
        ]
    ).astype(jnp.bfloat16)
    qkv_grad = jnp.einsum(
        "rd,cre->cde", normed_attn, projected_grad, preferred_element_type=jnp.float32
    )
    normed_attn_part = jnp.einsum(
        "cre,cde->rd", projected_grad, qkv_low, preferred_element_type=jnp.float32
    )
    normed_attn_grad = lax.psum_scatter(
        normed_attn_part.astype(jnp.bfloat16), "tensor", scatter_dimension=0, tiled=True
    ).astype(jnp.float32)
    norm_back_attn = jax.vjp(norm_rows, residual_in, gain_attn)[1]
    input_from_norm, gain_attn_grad = norm_back_attn(normed_attn_grad)
    input_grad = mid_grad + input_from_norm
    gain_grads = lax.psum(jnp.stack([gain_attn_grad, gain_mlp_grad]), "tensor")
    gains_out, qkv_out, out_out, gate_up_out, down_out = (
        lax.psum_scatter(
            gain_grads.astype(jnp.bfloat16), "dp", scatter_dimension=1, tiled=True
        ).astype(jnp.float32),
        lax.psum_scatter(
            qkv_grad.astype(jnp.bfloat16), "dp", scatter_dimension=1, tiled=True
        ).astype(jnp.float32),
        lax.psum_scatter(
            out_grad.astype(jnp.bfloat16), "dp", scatter_dimension=1, tiled=True
        ).astype(jnp.float32),
        lax.psum_scatter(
            gate_up_grad.astype(jnp.bfloat16), "dp", scatter_dimension=1, tiled=True
        ).astype(jnp.float32),
        lax.psum_scatter(
            down_grad.astype(jnp.bfloat16), "dp", scatter_dimension=1, tiled=True
        ).astype(jnp.float32),
    )
    return (block_output, input_grad, gains_out, qkv_out, out_out, gate_up_out, down_out)


QB = 256
NT = (((1,), (1,)), ((), ()))
NN = (((1,), (0,)), ((), ()))
TN = (((0,), (0,)), ((), ()))


def _dot(a, b, dims):
    return lax.dot_general(a, b, dims, preferred_element_type=jnp.float32)


def _stacked(tile, columns, n):
    return pl.BlockSpec((1, tile, columns), lambda i: (n, i, 0))


def _full(shape):
    return pl.BlockSpec(shape, lambda i: (0,) * len(shape))


def _smem():
    return pl.BlockSpec(memory_space=pltpu.SMEM)


def _rows(tile, columns):
    return pl.BlockSpec((tile, columns), lambda i: (i, 0))


def _params():
    return pltpu.CompilerParams(dimension_semantics=("arbitrary",), vmem_limit_bytes=60 << 20)


STRETCH = 6.0


def _cost(flops, bytes_accessed):
    return pl.CostEstimate(
        flops=int(flops * STRETCH), bytes_accessed=int(bytes_accessed * STRETCH), transcendentals=0
    )


def _row_tile(rows):
    return rows // 2 if rows % 32 == 0 else rows


def _normed(values):
    inverse_rms = lax.rsqrt(jnp.mean(values * values, axis=-1, keepdims=True) + epsilon)
    return inverse_rms, values * inverse_rms


def _place_kernel(where_ref, *refs):
    shards, out = refs[:-1], refs[-1]
    size = shards[0].shape[0]
    for n, shard in enumerate(shards):
        out[pl.ds(pl.multiple_of(where_ref[n] * size, size), size), :] = shard[...]


def place(where, shards):
    size, columns = shards[0].shape
    return pl.pallas_call(
        _place_kernel,
        grid=(1,),
        out_shape=jax.ShapeDtypeStruct((size * len(shards), columns), shards[0].dtype),
        in_specs=[_smem()] + [_full((size, columns))] * len(shards),
        out_specs=_full((size * len(shards), columns)),
        compiler_params=_params(),
        cost_estimate=_cost(0, 4 * size * columns * len(shards)),
        name="place",
    )(where, *shards)


def _project_kernel(x0_ref, x1_ref, gain_ref, w_ref, n0_ref, n1_ref, p0_ref, p1_ref):
    def run(x_ref, normed_ref, out_ref):
        normed = (_normed(x_ref[...].astype(jnp.float32))[1] * gain_ref[...]).astype(jnp.bfloat16)
        normed_ref[...] = normed
        out_ref[...] = _dot(normed, w_ref[...], NN).astype(jnp.bfloat16)

    half = pl.num_programs(0) // 2

    @pl.when(pl.program_id(0) < half)
    def _():
        run(x0_ref, n0_ref, p0_ref)

    @pl.when(pl.program_id(0) >= half)
    def _():
        run(x1_ref, n1_ref, p1_ref)


def project(x0, x1, gain, weight, columns):
    rows, depth = x0.shape
    tile = _row_tile(rows)
    steps = rows // tile
    early = lambda c: pl.BlockSpec((tile, c), lambda i: (jnp.minimum(i, steps - 1), 0))
    late = lambda c: pl.BlockSpec((tile, c), lambda i: (jnp.maximum(i - steps, 0), 0))
    out = lambda c: jax.ShapeDtypeStruct((rows, c), jnp.bfloat16)
    return pl.pallas_call(
        _project_kernel,
        grid=(2 * steps,),
        out_shape=[out(depth), out(depth), out(columns), out(columns)],
        in_specs=[early(depth), late(depth), _full((1, depth)), _full((depth, columns))],
        out_specs=[early(depth), late(depth), early(columns), late(columns)],
        compiler_params=_params(),
        cost_estimate=_cost(4 * rows * depth * columns, 4 * rows * (2 * depth + columns)),
        name="project",
    )(x0, x1, gain, weight)


def _mlp_kernel(keep, *refs):
    att_a, att_b, (xa, xb, ca, cb) = refs[:4], refs[4:8], refs[8:12]
    gain_ref, w_hbm, d_hbm, m_hbm = refs[12:16]
    hidden_ref, grad_ref, normed_ref = refs[16:19]
    part_a, part_b, branch_a, branch_b = refs[19:23]
    att_s, x_s, cot_s, o_s, w_s, d_s, sems = refs[-7:]
    width = att_a[0].shape[2]
    count = hidden_ref.shape[2]
    pulls = [
        pltpu.make_async_copy(
            d_hbm.at[:, pl.ds(count, 2 * width)], o_s.at[:, pl.ds(0, 2 * width)], sems.at[0]
        ),
        pltpu.make_async_copy(m_hbm, o_s.at[:, pl.ds(2 * width, 2 * width)], sems.at[1]),
        pltpu.make_async_copy(w_hbm, w_s, sems.at[2]),
        pltpu.make_async_copy(d_hbm.at[:, pl.ds(0, count)], d_s, sems.at[3]),
    ]
    first = pl.program_id(0) == 0
    late = pl.program_id(0) >= pl.num_programs(0) // 2

    @pl.when(first)
    def _():
        for pull in pulls:
            pull.start()

    def take(att, x_ref, cot_ref):
        for i, of in enumerate((0, 2, 1, 3)):
            att_s[:, i * width : (i + 1) * width] = att[of][0]
        x_s[...] = x_ref[...]
        cot_s[...] = cot_ref[...]

    @pl.when(jnp.logical_not(late))
    def _():
        take(att_a, xa, ca)

    @pl.when(late)
    def _():
        take(att_b, xb, cb)

    @pl.when(first)
    def _():
        for pull in pulls[:2]:
            pull.wait()

    residual = x_s[...].astype(jnp.float32) + _dot(att_s[...], o_s[...], NT)
    if keep:
        keep_ref = refs[23]

        @pl.when(late)
        def _():
            keep_ref[...] = residual

    normed_ref[0] = (_normed(residual)[1] * gain_ref[...]).astype(jnp.bfloat16)

    @pl.when(first)
    def _():
        for pull in pulls[2:]:
            pull.wait()

    both = _dot(normed_ref[0], w_s[...], NN).astype(jnp.bfloat16).astype(jnp.float32)
    gate, up = both[:, :count], both[:, count:]
    hidden_grad = _dot(cot_s[...], d_s[...], NN)
    sig = 0.5 * jnp.tanh(0.5 * gate) + 0.5
    act = gate * sig
    hidden = (act * up).astype(jnp.bfloat16)
    hidden_ref[0] = hidden
    grad_ref[0, :, :count] = (hidden_grad * up * (sig + act * (1.0 - sig))).astype(jnp.bfloat16)
    grad_ref[0, :, count:] = (hidden_grad * act).astype(jnp.bfloat16)
    part = _dot(grad_ref[0], w_s[...], NT).astype(jnp.bfloat16)
    branch = _dot(hidden, d_s[...], NT).astype(jnp.bfloat16)

    @pl.when(jnp.logical_not(late))
    def _():
        part_a[...] = part
        branch_a[...] = branch

    @pl.when(late)
    def _():
        part_b[...] = part
        branch_b[...] = branch


def mlp(attended_a, attended_b, x, cot, gain, weights, down, out_mate, keep):
    rows, depth = x[0].shape
    width = attended_a[0][0].shape[2]
    count = weights.shape[1] // 2
    tile = _row_tile(rows)
    steps = rows // tile
    bf16, f32 = jnp.bfloat16, jnp.float32
    early = lambda i: jnp.minimum(i, steps - 1)
    late = lambda i: jnp.maximum(i - steps, 0)
    rows_of = lambda where: pl.BlockSpec((tile, depth), lambda i: (where(i), 0))
    stack = lambda c: pl.BlockSpec((1, tile, c), lambda i: (i // steps, i % steps, 0))
    member = lambda n, where: pl.BlockSpec((1, tile, width), lambda i: (n, where(i), 0))
    outs = [jax.ShapeDtypeStruct((2, rows, c), bf16) for c in (count, 2 * count, depth)]
    outs += [jax.ShapeDtypeStruct((rows, depth), bf16)] * 4
    out_specs = [stack(count), stack(2 * count), stack(depth)] + [rows_of(early), rows_of(late)] * 2
    if keep:
        outs.append(jax.ShapeDtypeStruct((rows, depth), f32))
        out_specs.append(rows_of(late))
    anywhere = pl.BlockSpec(memory_space=pl.ANY)
    return pl.pallas_call(
        functools.partial(_mlp_kernel, keep),
        grid=(2 * steps,),
        out_shape=outs,
        in_specs=[member(n, early) for v, n in attended_a]
        + [member(n, late) for v, n in attended_b]
        + [rows_of(early), rows_of(late)] * 2
        + [_full((1, depth)), anywhere, anywhere, anywhere],
        out_specs=out_specs,
        scratch_shapes=[
            pltpu.VMEM((tile, 4 * width), bf16),
            pltpu.VMEM((tile, depth), bf16),
            pltpu.VMEM((tile, depth), bf16),
            pltpu.VMEM((depth, 4 * width), bf16),
            pltpu.VMEM((depth, 2 * count), bf16),
            pltpu.VMEM((depth, count), bf16),
            pltpu.SemaphoreType.DMA((4,)),
        ],
        compiler_params=_params(),
        cost_estimate=_cost(4 * rows * depth * (4 * width + 6 * count), 28 << 20),
        name="mlp",
    )(*[v for v, n in (*attended_a, *attended_b)], *x, *cot, gain, weights, down, out_mate)


def _pull_groups(right, right_s, row_at, column_at, step, sems, base):
    groups = []
    for c in range(right[0].shape[-1] // step):
        group = []
        at = row_at
        for j, piece in enumerate(right):
            rows = piece.shape[0]
            group.append(
                pltpu.make_async_copy(
                    piece.at[:, pl.ds(c * step, step)],
                    right_s.at[pl.ds(at, rows), pl.ds(column_at + c * step, step)],
                    sems.at[base + c * len(right) + j],
                )
            )
            at += rows
        groups.append(group)
    return groups


def _start_all(groups):
    @pl.when(pl.program_id(0) == 0)
    def _():
        for group in groups:
            for pull in group:
                pull.start()


def _wait_group(group):
    @pl.when(pl.program_id(0) == 0)
    def _():
        for pull in group:
            pull.wait()


def _join(pieces, out):
    at = 0
    for piece in pieces:
        rows = piece.shape[0]
        out[at : at + rows, :] = piece[...]
        at += rows


def _mlp_grad_kernel(n, step, *refs):
    normed, cot = refs[:2], refs[2 : 2 + n]
    grads, hidden = refs[2 + n : 4 + n], refs[4 + n : 6 + n]
    out_ref, left_s, right_s, sems = refs[6 + n :]
    members = lambda pair: [v.at[m] for v in pair for m in (0, 1)]
    wide = grads[0].shape[2]
    rows = left_s.shape[0] // n
    groups = _pull_groups(members(grads), right_s, 0, 0, step, sems, 0)
    groups += _pull_groups(members(hidden), right_s, 0, wide, step, sems, 4 * (wide // step))
    _start_all(groups)
    for m in range(n):
        left_s[m * rows : (m + 1) * rows, :] = normed[m // 2][m % 2]
    for c, group in enumerate(groups):
        at = slice(c * step, (c + 1) * step)
        if c * step == wide:
            _join(cot, left_s)
        _wait_group(group)
        out_ref[:, at] = _dot(left_s[...], right_s[:, at], TN).astype(out_ref.dtype)


def mlp_grads(normed, cot, grads, hidden, block=256):
    n = len(cot)
    piece, depth = cot[0].shape
    rows = n * piece
    columns = grads[0].shape[2] + hidden[0].shape[2]
    step = hidden[0].shape[2]
    anywhere = pl.BlockSpec(memory_space=pl.ANY)
    return pl.pallas_call(
        functools.partial(_mlp_grad_kernel, n, step),
        grid=(depth // block,),
        out_shape=jax.ShapeDtypeStruct((depth, columns), jnp.bfloat16),
        in_specs=[pl.BlockSpec((2, piece, block), lambda i: (0, 0, i))] * 2
        + [pl.BlockSpec((piece, block), lambda i: (0, i))] * n
        + [anywhere] * 4,
        out_specs=_rows(block, columns),
        scratch_shapes=[
            pltpu.VMEM((rows, block), jnp.bfloat16),
            pltpu.VMEM((rows, columns), jnp.bfloat16),
            pltpu.SemaphoreType.DMA((n * (columns // step),)),
        ],
        compiler_params=_params(),
        cost_estimate=_cost(2 * rows * depth * columns, 2 * rows * (depth + columns) + 2 * depth * columns),
        name="mlp_grads",
    )(*normed, *cot, *grads, *hidden)


def _split_rows(acc, y, near, far):
    size = near.shape[1]
    near[...] = acc[pl.ds(pl.multiple_of(y * size, size), size), :].astype(near.dtype)[None]
    far[...] = acc[pl.ds(pl.multiple_of((1 - y) * size, size), size), :].astype(far.dtype)[None]


def _qkv_grad_kernel(n, y_ref, *refs):
    left, right = refs[:n], refs[n : 2 * n]
    w_ref, gain_ref, row_ref, near, far, left_s, right_s, acc, sems = refs[2 * n :]
    columns = right_s.shape[1]
    groups = _pull_groups(right, right_s, 0, 0, columns, sems, 0)
    _start_all(groups)
    _join(left, left_s)
    _wait_group(groups[0])
    total = _dot(left_s[...], right_s[...], TN)
    acc[:, :columns] = total
    row = jnp.concatenate(
        [1.0 / gain_ref[...], row_ref[...], jnp.zeros((SEG - 9, row_ref.shape[1]), jnp.float32)], axis=0
    ).T
    attn = jnp.sum(total * w_ref[...].astype(jnp.float32), axis=-1, keepdims=True) * row[:, 0:1]
    lane = lax.broadcasted_iota(jnp.int32, row.shape, 1)
    acc[:, columns:] = jnp.where(lane == 0, attn, row)
    _split_rows(acc, y_ref[0], near, far)


def qkv_grads(y, normed, grads, weight, gain, mlp_sum, size):
    n, depth = len(normed), normed[0].shape[1]
    rows = sum(v.shape[0] for v in normed)
    columns = grads[0].shape[1]
    block = 2 * size
    anywhere = pl.BlockSpec(memory_space=pl.ANY)
    out = jax.ShapeDtypeStruct((depth // block, size, columns + SEG), jnp.bfloat16)
    out_spec = pl.BlockSpec((1, size, columns + SEG), lambda i: (i, 0, 0))
    lanes = lambda r: pl.BlockSpec((r, block), lambda i: (0, i))
    return pl.pallas_call(
        functools.partial(_qkv_grad_kernel, n),
        grid=(depth // block,),
        out_shape=[out, out],
        in_specs=[_smem()]
        + [lanes(v.shape[0]) for v in normed]
        + [anywhere] * n
        + [_rows(block, columns), lanes(1), lanes(8)],
        out_specs=[out_spec, out_spec],
        scratch_shapes=[
            pltpu.VMEM((rows, block), jnp.bfloat16),
            pltpu.VMEM((rows, columns), jnp.bfloat16),
            pltpu.VMEM((block, columns + SEG), jnp.float32),
            pltpu.SemaphoreType.DMA((n,)),
        ],
        compiler_params=_params(),
        cost_estimate=_cost(0, 0),
        name="qkv_grads",
    )(y, *normed, *grads, weight, gain, mlp_sum)


def _out_grad_kernel(left_ref, a0, a1, a2, a3, mine, theirs, right_s):
    width = a0.shape[2]

    @pl.when(pl.program_id(0) == 0)
    def _():
        for i, a in enumerate((a0, a2, a1, a3)):
            right_s[:, i * width : (i + 1) * width] = a[0]

    total = _dot(left_ref[...], right_s[...], TN).astype(mine.dtype)
    mine[...] = total[:, : 2 * width]
    theirs[...] = total[:, 2 * width :]


def out_grads(left, attended, block=256):
    rows, depth = left.shape
    width = attended[0][0].shape[2]
    out = jax.ShapeDtypeStruct((depth, 2 * width), jnp.bfloat16)
    member = lambda n: pl.BlockSpec((1, rows, width), lambda i: (n, 0, 0))
    return pl.pallas_call(
        _out_grad_kernel,
        grid=(depth // block,),
        out_shape=[out, out],
        in_specs=[pl.BlockSpec((rows, block), lambda i: (0, i))] + [member(n) for v, n in attended],
        out_specs=[_rows(block, 2 * width)] * 2,
        scratch_shapes=[pltpu.VMEM((rows, 4 * width), jnp.bfloat16)],
        compiler_params=_params(),
        cost_estimate=_cost(8 * rows * depth * width, 2 * rows * (depth + 4 * width) + 8 * depth * width),
        name="out_grads",
    )(left, *[v for v, n in attended])


def _pair_kernel(y_ref, a_ref, b_ref, near, far, acc):
    acc[...] = a_ref[...].astype(jnp.float32) + b_ref[...].astype(jnp.float32)
    _split_rows(acc, y_ref[0], near, far)


def pair_sum(y, a, b, size):
    depth, columns = a.shape
    block = 2 * size
    out = jax.ShapeDtypeStruct((depth // block, size, columns), jnp.bfloat16)
    out_spec = pl.BlockSpec((1, size, columns), lambda i: (i, 0, 0))
    return pl.pallas_call(
        _pair_kernel,
        grid=(depth // block,),
        out_shape=[out, out],
        in_specs=[_smem()] + [_rows(block, columns)] * 2,
        out_specs=[out_spec, out_spec],
        scratch_shapes=[pltpu.VMEM((block, columns), jnp.float32)],
        compiler_params=_params(),
        cost_estimate=_cost(0, 6 * depth * columns),
        name="pair_sum",
    )(y, a, b)


def _fold_kernel(z_ref, near, passed, *outs):
    count = near.shape[0]
    for step, out in enumerate(outs):
        row = lax.rem(z_ref[0] + step, count)
        out[...] = (near[row].astype(jnp.float32) + passed[row].astype(jnp.float32)).astype(out.dtype)


def fold(z, near, passed):
    count, size, columns = near.shape
    return pl.pallas_call(
        _fold_kernel,
        grid=(1,),
        out_shape=[jax.ShapeDtypeStruct((size, columns), jnp.bfloat16)] * count,
        in_specs=[_smem(), _full(near.shape), _full(near.shape)],
        out_specs=[_full((size, columns))] * count,
        compiler_params=_params(),
        cost_estimate=_cost(0, 0),
        name="fold",
    )(z, near, passed)


def _mid_kernel(p0, p1, p2, res_ref, cot_ref, gain_ref, near_ref, mate_ref, mid_ref, attn_ref, a0, a1, a2, a3, sum_ref):
    width = a0.shape[1]
    grad = p0[...].astype(jnp.float32) + p1[...].astype(jnp.float32) + p2[...].astype(jnp.float32)
    inverse, normed = _normed(res_ref[...])
    term = jnp.sum(grad * normed, axis=0, keepdims=True)

    @pl.when(pl.program_id(0) == 0)
    def _():
        sum_ref[...] = jnp.zeros_like(sum_ref)

    sum_ref[0:1, :] += term
    scaled = grad * gain_ref[...]
    mid = cot_ref[...] + inverse * (scaled - normed * jnp.mean(scaled * normed, axis=-1, keepdims=True))
    mid_ref[...] = mid
    low = mid.astype(jnp.bfloat16)
    attn_ref[...] = low
    a0[...] = _dot(low, near_ref[:, :width], NN).astype(jnp.bfloat16)
    a1[...] = _dot(low, mate_ref[:, :width], NN).astype(jnp.bfloat16)
    a2[...] = _dot(low, near_ref[:, width : 2 * width], NN).astype(jnp.bfloat16)
    a3[...] = _dot(low, mate_ref[:, width:], NN).astype(jnp.bfloat16)


def middle(parts, residual, cot, gain, weights, out_mate):
    rows, depth = residual.shape
    width = out_mate.shape[1] // 2
    tile = _row_tile(rows)
    return pl.pallas_call(
        _mid_kernel,
        grid=(rows // tile,),
        out_shape=[
            jax.ShapeDtypeStruct((rows, depth), jnp.float32),
            jax.ShapeDtypeStruct((rows, depth), jnp.bfloat16),
        ]
        + [jax.ShapeDtypeStruct((rows, width), jnp.bfloat16)] * 4
        + [jax.ShapeDtypeStruct((8, depth), jnp.float32)],
        in_specs=[_rows(tile, depth)] * 5
        + [
            _full((1, depth)),
            pl.BlockSpec((depth, 2 * width), lambda i: (0, weights.shape[1] // (2 * width) - 1)),
            _full(out_mate.shape),
        ],
        out_specs=[_rows(tile, depth)] * 2 + [_rows(tile, width)] * 4 + [_full((8, depth))],
        compiler_params=_params(),
        cost_estimate=_cost(2 * rows * depth * 4 * width, rows * depth * 20),
        name="middle",
    )(*parts, residual, cot, gain, weights, out_mate)


def _back_kernel(add, grad_ref, w_ref, *refs):
    part = _dot(grad_ref[...], w_ref[...], NT)
    if add:
        part = part + refs[0][...].astype(jnp.float32)
    refs[-1][...] = part.astype(refs[-1].dtype)


def project_back(grad, weight, add=None):
    rows, columns = grad.shape
    depth = weight.shape[0]
    tile = _row_tile(rows)
    extra = [] if add is None else [add]
    return pl.pallas_call(
        functools.partial(_back_kernel, add is not None),
        grid=(rows // tile,),
        out_shape=jax.ShapeDtypeStruct((rows, depth), jnp.bfloat16),
        in_specs=[_rows(tile, columns), _full((depth, columns))] + [_rows(tile, depth)] * len(extra),
        out_specs=_rows(tile, depth),
        compiler_params=_params(),
        cost_estimate=_cost(0, 0),
        name="project_back",
    )(grad, weight, *extra)


def _last_kernel(p0, p1, p2, x_ref, mid_ref, gain_ref, out_ref):
    grad = p0[...].astype(jnp.float32) + p1[...].astype(jnp.float32) + p2[...].astype(jnp.float32)
    inverse, normed = _normed(x_ref[...].astype(jnp.float32))
    scaled = grad * gain_ref[...]
    out_ref[...] = mid_ref[...] + inverse * (
        scaled - normed * jnp.mean(scaled * normed, axis=-1, keepdims=True)
    )


def last(parts, x, mid, gain):
    rows, depth = x.shape
    tile = _row_tile(rows)
    return pl.pallas_call(
        _last_kernel,
        grid=(rows // tile,),
        out_shape=jax.ShapeDtypeStruct((rows, depth), jnp.float32),
        in_specs=[_rows(tile, depth)] * 5 + [_full((1, depth))],
        out_specs=_rows(tile, depth),
        compiler_params=_params(),
        cost_estimate=_cost(0, rows * depth * 16),
        name="last",
    )(*parts, x, mid, gain)


def _half_place(info_ref, b, half, piece_blocks):
    block = 2 * b + half
    piece = lax.bitwise_xor(lax.div(block, piece_blocks), info_ref[0])
    return piece, lax.rem(block, piece_blocks) * SEG


def _mask(heads, same, causal):
    key = lax.broadcasted_iota(jnp.int32, (QB, heads * QB), 0)
    query = lax.broadcasted_iota(jnp.int32, (QB, heads * QB), 1) % QB
    allowed = jnp.logical_not(same & ((key // SEG) != (query // SEG)))
    if causal:
        allowed = allowed & (key <= query)
    return allowed


def _spread(block, heads):
    turned = block.T
    lane = lax.broadcasted_iota(jnp.int32, turned.shape, 0) // HDIM
    zero = jnp.zeros_like(turned)
    return jnp.concatenate([jnp.where(lane == h, turned, zero) for h in range(heads)], axis=1)


def _stack(block, heads):
    lane = lax.broadcasted_iota(jnp.int32, block.shape, 1) // HDIM
    zero = jnp.zeros_like(block)
    return jnp.concatenate([jnp.where(lane == h, block, zero) for h in range(heads)], axis=0)


def _parents(info_ref, b):
    leaf = 2 * (b - (TRUNK + 4 * SEG) // QB)
    return [pl.multiple_of(TRUNK - SEG + SEG * info_ref[2 + leaf + side], SEG) for side in (0, 1)]


def _attn_fwd_kernel(heads, piece_count, info_ref, *refs):
    pieces = refs[:piece_count]
    out_ref, lse_ref = refs[piece_count : piece_count + 2]
    q_s, k_s, vt_s, qt_s, s_s, p_s, m_s, l_s, acc_s, kp_s, vp_s = refs[piece_count + 2 :]
    width = heads * HDIM
    piece_rows = pieces[0].shape[0]
    tensor = info_ref[0]
    base = info_ref[1]
    trunk_blocks = TRUNK // QB
    leaf_block = (TRUNK + 4 * SEG) // QB
    for j in range(piece_count):
        at = pl.multiple_of(piece_rows * lax.bitwise_xor(tensor, j), SEG)
        q_s[pl.ds(at, piece_rows), :] = pieces[j][:, :width] * jnp.asarray(HDIM**-0.5, jnp.bfloat16)
        k_s[pl.ds(at, piece_rows), :] = pieces[j][:, width : 2 * width]
        vt_s[:, pl.ds(at, piece_rows)] = pieces[j][:, 2 * width :].T

    def q_block(i, carry):
        b = base + i
        row = pl.multiple_of(b * QB, QB)
        own = pl.ds(row, QB)
        leaf = b >= leaf_block
        qt_s[...] = _spread(q_s[own, :], heads)

        def score(keys, at, size, allowed):
            scores = _dot(keys, qt_s[...], NN)
            if allowed is not None:
                scores = jnp.where(allowed, scores, -1e30)
            s_s[pl.ds(at, size), :] = scores
            return jnp.max(scores, axis=0, keepdims=True)

        m_s[0:1, :] = score(k_s[own, :], TRUNK, QB, _mask(heads, b >= trunk_blocks, True))

        @pl.when(leaf)
        def _():
            for side, at in enumerate(_parents(info_ref, b)):
                kp_s[side * SEG : (side + 1) * SEG, :] = k_s[pl.ds(at, SEG), :]
                vp_s[:, side * SEG : (side + 1) * SEG] = vt_s[:, pl.ds(at, SEG)]
            top = score(kp_s[...], TRUNK + QB, QB, _mask(heads, True, False))
            m_s[0:1, :] = jnp.maximum(m_s[0:1, :], top)

        @pl.when(b >= trunk_blocks)
        def _():
            m_s[0:1, :] = jnp.maximum(m_s[0:1, :], score(k_s[:TRUNK, :], 0, TRUNK, None))

        @pl.when(b < trunk_blocks)
        def _():
            def chunk(c, carry):
                at = pl.multiple_of(c * QB, QB)
                m_s[0:1, :] = jnp.maximum(m_s[0:1, :], score(k_s[pl.ds(at, QB), :], at, QB, None))
                return carry

            lax.fori_loop(0, b, chunk, 0)

        def mix(values, at, size, fresh):
            probs = jnp.exp(s_s[pl.ds(at, size), :] - m_s[0:1, :])
            total = jnp.sum(probs, axis=0, keepdims=True)
            p_s[pl.ds(at, size), :] = probs.astype(jnp.bfloat16)
            l_s[0:1, :] = total if fresh else l_s[0:1, :] + total
            for h in range(heads):
                of = slice(h * HDIM, (h + 1) * HDIM)
                term = _dot(values(of), p_s[pl.ds(at, size), h * QB : (h + 1) * QB], NN)
                acc_s[of, :] = term if fresh else acc_s[of, :] + term

        mix(lambda of: vt_s[of, own], TRUNK, QB, True)

        @pl.when(leaf)
        def _():
            mix(lambda of: vp_s[of, :], TRUNK + QB, QB, False)

        @pl.when(b >= trunk_blocks)
        def _():
            mix(lambda of: vt_s[of, :TRUNK], 0, TRUNK, False)

        @pl.when(b < trunk_blocks)
        def _():
            def chunk(c, carry):
                at = pl.multiple_of(c * QB, QB)
                mix(lambda of: vt_s[of, pl.ds(at, QB)], at, QB, False)
                return carry

            lax.fori_loop(0, b, chunk, 0)

        mixed = []
        for h in range(heads):
            columns = slice(h * QB, (h + 1) * QB)
            total = l_s[0:1, columns]
            lse_ref[h : h + 1, pl.ds(pl.multiple_of(i * QB, QB), QB)] = m_s[0:1, columns] + jnp.log(total)
            mixed.append(acc_s[h * HDIM : (h + 1) * HDIM, :] / total)
        mixed = jnp.concatenate(mixed, axis=0).T.astype(jnp.bfloat16)
        for half in (0, 1):
            piece, at = _half_place(info_ref, b, half, piece_rows // SEG)
            at = pl.multiple_of(at, SEG)
            out_ref[lax.bitwise_and(piece, 1), pl.ds(at, SEG), :] = mixed[half * SEG : (half + 1) * SEG]
        return carry

    lax.fori_loop(0, lse_ref.shape[1] // QB, q_block, 0)


def attention_forward(info, pieces, heads):
    rows = sum(p.shape[0] for p in pieces)
    piece_rows = pieces[0].shape[0]
    width = heads * HDIM
    half = rows // 2
    bf16, f32 = jnp.bfloat16, jnp.float32
    return pl.pallas_call(
        functools.partial(_attn_fwd_kernel, heads, len(pieces)),
        out_shape=[
            jax.ShapeDtypeStruct((2, piece_rows, width), bf16),
            jax.ShapeDtypeStruct((8, half), f32),
        ],
        grid=(1,),
        in_specs=[_smem()] + [_full(p.shape) for p in pieces],
        out_specs=[_full((2, piece_rows, width)), _full((8, half))],
        scratch_shapes=[
            pltpu.VMEM((rows, width), bf16),
            pltpu.VMEM((rows, width), bf16),
            pltpu.VMEM((width, rows), bf16),
            pltpu.VMEM((width, heads * QB), bf16),
            pltpu.VMEM((TRUNK + 2 * QB, heads * QB), f32),
            pltpu.VMEM((TRUNK + 2 * QB, heads * QB), bf16),
            pltpu.VMEM((8, heads * QB), f32),
            pltpu.VMEM((8, heads * QB), f32),
            pltpu.VMEM((width, QB), f32),
            pltpu.VMEM((QB, width), bf16),
            pltpu.VMEM((width, QB), bf16),
        ],
        compiler_params=_params(),
        cost_estimate=_cost(rows * 1400 * width * 4, rows * width * 8),
        name="attn_fwd",
    )(info, *pieces)


def _attn_bwd_kernel(heads, info_ref, *refs):
    n = 4
    pieces, mixed_in, grads = refs[:n], refs[n : n + 2], refs[n + 2 : 2 * n + 2]
    lse_refs = refs[2 * n + 2 : 2 * n + 4]
    outs = refs[2 * n + 4 : 3 * n + 4]
    q_s, k_s, kt_s, v_s, o_s, g_s, dk_s, dv_s, lse_s = refs[3 * n + 4 : 3 * n + 13]
    qt_s, gt_s, qm_s, gm_s, row_s, delta_s, acc_s, kp_s, vp_s, kpt_s = refs[3 * n + 13 :]
    width = heads * HDIM
    piece_rows = pieces[0].shape[0]
    tensor = info_ref[0]
    chip = lax.div(tensor, 2)
    half_rows = lse_refs[0].shape[1]
    scale = HDIM**-0.5
    trunk_blocks = TRUNK // QB
    leaf_block = (TRUNK + 4 * SEG) // QB
    for j in range(n):
        rows_at = pl.ds(pl.multiple_of(piece_rows * lax.bitwise_xor(tensor, j), SEG), piece_rows)
        q_s[rows_at, :] = pieces[j][:, :width] * jnp.asarray(scale, jnp.bfloat16)
        k_s[rows_at, :] = pieces[j][:, width : 2 * width]
        kt_s[:, rows_at] = pieces[j][:, width : 2 * width].T
        v_s[rows_at, :] = pieces[j][:, 2 * width :]
        o_s[rows_at, :] = mixed_in[j // 2][j % 2]
        g_s[rows_at, :] = grads[j][...]
    lse_s[:, pl.ds(pl.multiple_of(chip * half_rows, SEG), half_rows)] = lse_refs[0][...]
    lse_s[:, pl.ds(pl.multiple_of((1 - chip) * half_rows, SEG), half_rows)] = lse_refs[1][...]
    dk_s[...] = jnp.zeros_like(dk_s)
    dv_s[...] = jnp.zeros_like(dv_s)
    head_of_lane = lax.broadcasted_iota(jnp.int32, (8, width), 1) // HDIM
    pick = jnp.where(lax.broadcasted_iota(jnp.int32, (8, width), 0) == head_of_lane, 1.0, 0.0)

    def q_block(b, carry):
        row = pl.multiple_of(b * QB, QB)
        own = pl.ds(row, QB)
        both = o_s[own, :].astype(jnp.float32) * g_s[own, :].astype(jnp.float32)
        delta = lax.dot_general(
            pick, both, NT, precision=lax.Precision.HIGHEST, preferred_element_type=jnp.float32
        )
        for h in range(heads):
            columns = slice(h * QB, (h + 1) * QB)
            delta_s[0:1, columns] = delta[h : h + 1, :]
            row_s[0:1, columns] = lse_s[h : h + 1, own]
        qt_s[...] = _spread(q_s[own, :], heads)
        gt_s[...] = _spread(g_s[own, :], heads)
        qm_s[...] = _stack(q_s[own, :], heads)
        gm_s[...] = _stack(g_s[own, :], heads)

        def step(k, v, kt, allowed, fresh, targets):
            scores = _dot(k, qt_s[...], NN)
            probs_grad = _dot(v, gt_s[...], NN)
            probs = jnp.exp(scores - row_s[0:1, :])
            if allowed is not None:
                probs = jnp.where(allowed, probs, 0.0)
            ds = (probs * (probs_grad - delta_s[0:1, :])).astype(jnp.bfloat16)
            dv = _dot(probs.astype(jnp.bfloat16), gm_s[...], NN)
            dk = _dot(ds, qm_s[...], NN)
            for h in range(heads):
                of = slice(h * HDIM, (h + 1) * HDIM)
                term = _dot(kt(of), ds[:, h * QB : (h + 1) * QB], NN)
                acc_s[of, :] = term if fresh else acc_s[of, :] + term
            first = 0
            for at, size in targets:
                dv_s[pl.ds(at, size), :] += dv[first : first + size]
                dk_s[pl.ds(at, size), :] += dk[first : first + size]
                first += size

        step(
            k_s[own, :], v_s[own, :], lambda of: kt_s[of, own],
            _mask(heads, b >= trunk_blocks, True), True, [(row, QB)],
        )

        @pl.when(b >= leaf_block)
        def _():
            ats = _parents(info_ref, b)
            for side, at in enumerate(ats):
                part = slice(side * SEG, (side + 1) * SEG)
                kp_s[part, :] = k_s[pl.ds(at, SEG), :]
                vp_s[part, :] = v_s[pl.ds(at, SEG), :]
                kpt_s[:, part] = kt_s[:, pl.ds(at, SEG)]
            step(
                kp_s[...], vp_s[...], lambda of: kpt_s[of, :],
                _mask(heads, True, False), False, [(at, SEG) for at in ats],
            )

        def trunk_step(c):
            at = pl.multiple_of(c * QB, QB)
            here = pl.ds(at, QB)
            step(k_s[here, :], v_s[here, :], lambda of: kt_s[of, here], None, False, [(at, QB)])

        def trunk_pair(c, carry):
            trunk_step(2 * c)
            trunk_step(2 * c + 1)
            return carry

        count = jnp.minimum(b, trunk_blocks)
        lax.fori_loop(0, lax.div(count, 2), trunk_pair, 0)

        @pl.when(lax.rem(count, 2) == 1)
        def _():
            trunk_step(count - 1)

        q_s[own, :] = (acc_s[...] * scale).T.astype(jnp.bfloat16)
        return carry

    lax.fori_loop(0, q_s.shape[0] // QB, q_block, 0)
    for j in range(n):
        rows_at = pl.ds(pl.multiple_of(piece_rows * lax.bitwise_xor(tensor, j), SEG), piece_rows)
        outs[j][:, :width] = q_s[rows_at, :]
        outs[j][:, width : 2 * width] = dk_s[rows_at, :].astype(jnp.bfloat16)
        outs[j][:, 2 * width :] = dv_s[rows_at, :].astype(jnp.bfloat16)


def attention_backward(info, pieces, mixed, grads, lses, heads):
    n = len(pieces)
    piece_rows = pieces[0].shape[0]
    rows = n * piece_rows
    width = heads * HDIM
    bf16, f32 = jnp.bfloat16, jnp.float32
    rows_low = pltpu.VMEM((rows, width), bf16)
    return pl.pallas_call(
        functools.partial(_attn_bwd_kernel, heads),
        out_shape=[jax.ShapeDtypeStruct((piece_rows, 3 * width), bf16)] * n,
        grid=(1,),
        in_specs=[_smem()] + [_full(v.shape) for v in (*pieces, *mixed, *grads, *lses)],
        out_specs=[_full((piece_rows, 3 * width))] * n,
        scratch_shapes=[
            rows_low,
            rows_low,
            pltpu.VMEM((width, rows), bf16),
            rows_low,
            rows_low,
            rows_low,
            pltpu.VMEM((rows, width), f32),
            pltpu.VMEM((rows, width), f32),
            pltpu.VMEM((8, rows), f32),
            pltpu.VMEM((width, heads * QB), bf16),
            pltpu.VMEM((width, heads * QB), bf16),
            pltpu.VMEM((heads * QB, width), bf16),
            pltpu.VMEM((heads * QB, width), bf16),
            pltpu.VMEM((8, heads * QB), f32),
            pltpu.VMEM((8, heads * QB), f32),
            pltpu.VMEM((width, QB), f32),
            pltpu.VMEM((QB, width), bf16),
            pltpu.VMEM((QB, width), bf16),
            pltpu.VMEM((width, QB), bf16),
        ],
        compiler_params=_params(),
        cost_estimate=_cost(0, 0),
        name="attn_bwd",
    )(info, *pieces, *mixed, *grads, *lses)


def mate(x):
    return lax.ppermute(x, "tensor", [(i, i ^ 1) for i in range(4)])


def across(x):
    return lax.ppermute(x, "tensor", [(i, i ^ 2) for i in range(4)])


def corner(x):
    return lax.ppermute(x, "tensor", [(i, i ^ 3) for i in range(4)])


def beside(x):
    return lax.ppermute(x, "dp", [(i, i ^ 1) for i in range(8)])


def ahead(x, step):
    return lax.ppermute(x, "dp", [(i, (i + 2 * step) % 8) for i in range(8)])


def after(x, *others):
    return lax.optimization_barrier((x, *others))[0]


def after_all(values, *others):
    return list(lax.optimization_barrier((*values, *others))[: len(values)])


def line_hops(x):
    return [x] + [ahead(x, step) for step in (1, 3, 2)]


def spread_hops(line, far):
    dp = lax.axis_index("dp")
    z, y = dp // 2, dp % 2
    order = jnp.array([0, 1, 3, 2], jnp.int32)
    from_z = (z - order) % 4
    where = jnp.concatenate([2 * from_z + y, 2 * from_z + 1 - y]).astype(jnp.int32)
    return place(where, line + far)


def fold_hops(near, passed):
    z = (lax.axis_index("dp") // 2).astype(jnp.int32)[None]
    return fold(z, near, passed)


def send_hops(chunks):
    return [chunks[0]] + [ahead(chunks[step], step) for step in (2, 1, 3)]


def sum_hops(received):
    return sum(v.astype(jnp.float32) for v in received)


def body(
    block_input,
    norm_gains,
    qkv_weight,
    out_weight,
    gate_up_weight,
    down_weight,
    parent_of_row,
    cotangent,
):
    bf16, f32 = jnp.bfloat16, jnp.float32
    shard = qkv_weight.shape[1]
    width = qkv_weight.shape[2]
    hidden_width = gate_up_weight.shape[2]
    heads = width // HDIM
    rows = parent_of_row.shape[0]
    tensor = lax.axis_index("tensor")
    chip = tensor // 2
    y = (lax.axis_index("dp") % 2).astype(jnp.int32)[None]
    leaf_first = TRUNK + 4 * SEG
    parents = parent_of_row[leaf_first::SEG]
    half_blocks = rows // (2 * QB)
    place_own = jnp.stack([tensor, half_blocks * chip]).astype(jnp.int32)
    place_far = jnp.stack([tensor, half_blocks * (1 - chip)]).astype(jnp.int32)
    info_own = jnp.concatenate([place_own, parents])
    info_far = jnp.concatenate([place_far, parents])

    gains_shard = jnp.pad(norm_gains.astype(bf16).T, ((0, 0), (0, SEG - 2)))
    qkv_shard = qkv_weight.astype(bf16).transpose(1, 0, 2).reshape(shard, 3 * width)
    first_line = line_hops(jnp.concatenate([qkv_shard, gains_shard], axis=1))
    out_shard = out_weight.astype(bf16).T
    out_x = across(out_shard)
    beyond = across(after(block_input, out_x))
    near_x = mate(block_input)
    gate_up_shard = gate_up_weight.astype(bf16).transpose(1, 0, 2).reshape(shard, 2 * hidden_width)
    rest = lax.all_gather(after(gate_up_shard, out_x), "dp", axis=0, tiled=True)
    first_far = [beside(v) for v in first_line]
    first = spread_hops(first_line, first_far)
    second_shard = jnp.concatenate([down_weight.astype(bf16).T, out_shard, out_x], axis=1)
    down_line = line_hops(after(second_shard, *first_line))
    gains_low = first[:, 3 * width : 3 * width + 2].T.astype(f32)
    gain_attn, gain_mlp = gains_low[0:1], gains_low[1:2]
    n0, n1, p0, p1 = project(block_input, near_x, gain_attn, first, 3 * width)
    inputs = [block_input, near_x, beyond, mate(beyond)]
    n2, n3, p2, p3 = project(inputs[2], after(inputs[3], p1), gain_attn, first, 3 * width)
    normed_attn, projected = [n0, n1, n2, n3], [p0, p1, p2, p3]
    cot_low = cotangent.astype(bf16)
    cot_x = across(after(cot_low, beyond))

    own, lse_own = attention_forward(info_own, projected, heads)
    own_x, own_m = across(after(own, cot_x)), mate(own)
    down_far = [beside(after(down_line[0], p1)), beside(after(down_line[1], own)), beside(after(down_line[2], own))]
    cot_near = mate(after(cot_low, own))
    far, lse_far = attention_forward(after(info_far, own), projected, heads)
    down_far += [beside(after(v, far)) for v in down_line[3:]]
    far_m, own_xm = mate(far), mate(after(own_x, far))
    far_x = across(far)
    down_low = spread_hops(down_line, down_far)
    cot_rows = [cot_low, cot_near, cot_x, mate(after(cot_x, far))]
    out_far = mate(down_low[:, hidden_width:])

    own_rows = [(own, 0), (own_m, 1), (far_x, 0), None]
    hidden_far, grads_far, normed_far, part3, part2, branch3, branch2 = mlp(
        [(far, 1), (far_m, 0), (own_x, 1), (own_xm, 0)],
        [(far, 0), (far_m, 1), (own_x, 0), (own_xm, 1)],
        [inputs[3], inputs[2]], [cot_rows[3], cot_rows[2]], gain_mlp, rest, down_low, out_far, False,
    )
    far_xm = mate(after(far_x, part3))
    own_rows[3] = (far_xm, 1)
    passed = (part2.astype(f32) + mate(after(part3, far_x)).astype(f32)).astype(bf16)
    passed_x = across(passed)
    hidden_own, grads_own, normed_own, part1, part0, branch1, branch0, residual_mid = mlp(
        [(own, 1), (own_m, 0), (far_x, 1), (far_xm, 0)], own_rows,
        [inputs[1], inputs[0]], [after(cot_rows[1], passed), cot_rows[0]],
        gain_mlp, rest, down_low, out_far, True,
    )
    mlp_parts = [part0, mate(after(part1, passed_x)), passed_x]

    grad_sum = mlp_grads(
        [after(normed_far, passed_x), normed_own],
        [cot_rows[n] for n in (3, 2, 1, 0)],
        [grads_far, grads_own],
        [hidden_far, hidden_own],
    )
    mid_grad, attn_grad, g0, g1, g2, g3, mlp_sum = middle(
        [after(mlp_parts[0], grad_sum), *mlp_parts[1:]], residual_mid, cotangent, gain_mlp, down_low, out_far
    )
    grad_sum = lax.psum_scatter(grad_sum, "dp", scatter_dimension=0, tiled=True)
    g_x, g_c, g_m = across(g2), corner(g3), mate(g1)
    out_mine, out_theirs = out_grads(attn_grad, own_rows)
    out_theirs = mate(out_theirs)
    branch_passed = (branch2.astype(f32) + mate(branch3).astype(f32)).astype(bf16)
    out_pair = pair_sum(y, out_mine, after(out_theirs, branch_passed), shard)
    out_y = beside(out_pair[1])
    branch_x = across(after(branch_passed, g_x, g_c))

    bwd_grads = after_all([g0, g_m, g_x, g_c], out_pair[1], branch_passed)
    projected_grad = attention_backward(
        info_own, projected, [own, far], bwd_grads, [lse_own, lse_far], heads
    )
    back3 = project_back(after(projected_grad[3], out_y, branch_x), first)
    qkv_pair = qkv_grads(
        y, normed_attn, after_all(projected_grad, back3), first, gain_attn, mlp_sum, shard
    )
    qkv_y = beside(qkv_pair[1])
    out_chunks = fold_hops(out_pair[0], after(out_y, qkv_pair[1]))
    out_received = send_hops(out_chunks)
    back2 = project_back(after(projected_grad[2], out_chunks[1]), first, mate(back3))
    back_x = across(back2)
    back1 = project_back(after(projected_grad[1], back2), first)
    qkv_chunks = fold_hops(qkv_pair[0], after(qkv_y, back1))
    qkv_received = send_hops(qkv_chunks)
    back0 = project_back(after(projected_grad[0], qkv_chunks[1]), first)
    back_m = mate(after(back1, qkv_y))
    branch_sum = branch0.astype(f32) + mate(branch1).astype(f32)
    block_output = residual_mid + branch_sum + after(branch_x, back0).astype(f32)
    grad_sum = after(grad_sum, qkv_chunks[1]).astype(f32)
    down_out = grad_sum[:, 2 * hidden_width :].T
    gate_up_out = grad_sum[:, : 2 * hidden_width].reshape(shard, 2, hidden_width).transpose(1, 0, 2)
    input_grad = last(
        [back0, back_m, after(back_x, down_out, gate_up_out, block_output)], block_input, mid_grad, gain_attn
    )
    out_sum = sum_hops(out_received)
    qkv_sum = sum_hops(after_all(qkv_received, input_grad))
    qkv_out = qkv_sum[:, : 3 * width].reshape(shard, 3, width).transpose(1, 0, 2)
    gains_sum = qkv_sum[:, 3 * width :]
    gains_sum = gains_sum + mate(gains_sum.astype(bf16)).astype(f32)
    from_x = across(jnp.concatenate([out_sum[:, width:], gains_sum], axis=1).astype(bf16)).astype(f32)
    out_out = (out_sum[:, :width] + from_x[:, :width]).T
    gains_out = (gains_sum + from_x[:, width:])[:, :2].T
    return (block_output, input_grad, gains_out, qkv_out, out_out, gate_up_out, down_out)


def solution(mesh):
    placed = (
        P(("dp", "tensor"), None),
        P(None, "dp"),
        P(None, "dp", "tensor"),
        P("tensor", "dp"),
        P(None, "dp", "tensor"),
        P("tensor", "dp"),
        P("dp"),
        P(("dp", "tensor"), None),
    )
    four_by_eight = mesh.shape["tensor"] == 4 and mesh.shape["dp"] == 8
    return jax.shard_map(
        body if four_by_eight else body_any_mesh,
        mesh=mesh,
        in_specs=placed,
        out_specs=(
            P(("dp", "tensor"), None),
            P(("dp", "tensor"), None),
            P(None, "dp"),
            P(None, "dp", "tensor"),
            P("tensor", "dp"),
            P(None, "dp", "tensor"),
            P("tensor", "dp"),
        ),
        check_vma=False,
    )
```

```python
import functools
import jax
import jax.numpy as jnp
from jax import lax
from jax.experimental import pallas as pl
from jax.experimental.pallas import tpu as pltpu
from jax.sharding import PartitionSpec as P

HDIM = 64
TRUNK = 1024
SEG = 128
ROW_TREE = 2560


epsilon = 1e-06


def norm_rows(values, gain_row):
    inverse_rms = lax.rsqrt(jnp.mean(values * values, axis=-1, keepdims=True) + epsilon)
    return values * inverse_rms * gain_row


def segment_ids(row_count):
    position = jnp.arange(row_count, dtype=jnp.int32)
    tree_base = position // ROW_TREE * 13
    within = position % ROW_TREE
    beyond = within - TRUNK
    own_segment = jnp.where(
        within < TRUNK,
        0,
        jnp.where(beyond < 4 * SEG, 1 + beyond // SEG, 5 + (beyond - 4 * SEG) // SEG),
    )
    return (own_segment + tree_base, tree_base)


def body_any_mesh(
    block_input,
    norm_gains,
    qkv_weight,
    out_weight,
    gate_up_weight,
    down_weight,
    parent_of_row,
    cotangent,
):
    gains_cast = norm_gains.astype(jnp.bfloat16)
    qkv_cast = qkv_weight.astype(jnp.bfloat16)
    out_cast = out_weight.astype(jnp.bfloat16)
    gate_up_cast = gate_up_weight.astype(jnp.bfloat16)
    down_cast = down_weight.astype(jnp.bfloat16)
    gains_low, qkv_low, out_low, gate_up_low, down_low = (
        lax.all_gather(gains_cast, "dp", axis=1, tiled=True),
        lax.all_gather(qkv_cast, "dp", axis=1, tiled=True),
        lax.all_gather(out_cast, "dp", axis=1, tiled=True),
        lax.all_gather(gate_up_cast, "dp", axis=1, tiled=True),
        lax.all_gather(down_cast, "dp", axis=1, tiled=True),
    )
    row_count = parent_of_row.shape[0]
    width_local = qkv_low.shape[2]
    head_local = width_local // HDIM
    block_rows = min(512, row_count)
    block_count = row_count // block_rows
    score_scale = float(HDIM) ** (-0.5)
    segment_of_row, trunk_of_row = segment_ids(row_count)
    parent_segment = parent_of_row + trunk_of_row
    column_index = jnp.arange(row_count, dtype=jnp.int32)
    residual_in = block_input.astype(jnp.float32)
    gain_attn = gains_low[0].astype(jnp.float32)
    gain_mlp = gains_low[1].astype(jnp.float32)
    normed_attn = lax.all_gather(
        norm_rows(residual_in, gain_attn).astype(jnp.bfloat16), "tensor", axis=0, tiled=True
    )
    projected = jnp.einsum(
        "rd,cde->cre", normed_attn, qkv_low, preferred_element_type=jnp.float32
    ).astype(jnp.bfloat16)
    query_rows = projected[0].reshape(row_count, head_local, HDIM)
    key_rows = projected[1].reshape(row_count, head_local, HDIM)
    value_rows = projected[2].reshape(row_count, head_local, HDIM)

    def block_scores(block_index):
        row_start = block_index * block_rows
        query_block = lax.dynamic_slice_in_dim(query_rows, row_start, block_rows, 0)
        scores = (
            jnp.einsum("qhd,khd->hqk", query_block, key_rows, preferred_element_type=jnp.float32)
            * score_scale
        )
        row_index = row_start + jnp.arange(block_rows, dtype=jnp.int32)
        row_segment = lax.dynamic_slice_in_dim(segment_of_row, row_start, block_rows, 0)
        row_parent = lax.dynamic_slice_in_dim(parent_segment, row_start, block_rows, 0)
        row_trunk = lax.dynamic_slice_in_dim(trunk_of_row, row_start, block_rows, 0)
        column_segment = segment_of_row[None, :]
        allowed = (column_index[None, :] <= row_index[:, None]) & (
            (column_segment == row_segment[:, None])
            | (column_segment == row_parent[:, None])
            | (column_segment == row_trunk[:, None])
        )
        return (jnp.where(allowed[None], scores, -1e30), query_block)

    def attend_block(block_index):
        scores, query_block = block_scores(block_index)
        top_score = jnp.max(scores, axis=-1, keepdims=True)
        exp_scores = jnp.exp(scores - top_score)
        row_total = jnp.sum(exp_scores, axis=-1, keepdims=True)
        softmax_low = (exp_scores / row_total).astype(jnp.bfloat16)
        mixed_heads = jnp.einsum(
            "hqk,khd->qhd", softmax_low, value_rows, preferred_element_type=jnp.float32
        ).astype(jnp.bfloat16)
        return (mixed_heads, (top_score + jnp.log(row_total))[..., 0])

    block_ids = jnp.arange(block_count, dtype=jnp.int32)
    attended, log_totals = lax.map(attend_block, block_ids)
    attended = attended.reshape(row_count, width_local)
    attn_partial = jnp.dot(attended, out_low, preferred_element_type=jnp.float32)
    residual_mid = residual_in + lax.psum_scatter(
        attn_partial, "tensor", scatter_dimension=0, tiled=True
    )
    normed_mlp = lax.all_gather(
        norm_rows(residual_mid, gain_mlp).astype(jnp.bfloat16), "tensor", axis=0, tiled=True
    )
    gate_up = jnp.einsum(
        "rd,cdf->crf", normed_mlp, gate_up_low, preferred_element_type=jnp.float32
    ).astype(jnp.bfloat16)
    gate_value = gate_up[0].astype(jnp.float32)
    up_value = gate_up[1].astype(jnp.float32)
    sigmoid_gate = jax.nn.sigmoid(gate_value)
    hidden = (gate_value * sigmoid_gate * up_value).astype(jnp.bfloat16)
    mlp_partial = jnp.dot(hidden, down_low, preferred_element_type=jnp.float32)
    block_output = residual_mid + lax.psum_scatter(
        mlp_partial.astype(jnp.bfloat16), "tensor", scatter_dimension=0, tiled=True
    ).astype(jnp.float32)
    gains_again = norm_gains.astype(jnp.bfloat16)
    qkv_again = qkv_weight.astype(jnp.bfloat16)
    out_again = out_weight.astype(jnp.bfloat16)
    gate_up_again = gate_up_weight.astype(jnp.bfloat16)
    down_again = down_weight.astype(jnp.bfloat16)
    gains_low, qkv_low, out_low, gate_up_low, down_low = (
        lax.all_gather(gains_again, "dp", axis=1, tiled=True),
        lax.all_gather(qkv_again, "dp", axis=1, tiled=True),
        lax.all_gather(out_again, "dp", axis=1, tiled=True),
        lax.all_gather(gate_up_again, "dp", axis=1, tiled=True),
        lax.all_gather(down_again, "dp", axis=1, tiled=True),
    )
    gain_attn = gains_low[0].astype(jnp.float32)
    gain_mlp = gains_low[1].astype(jnp.float32)
    mlp_grad_rows = lax.all_gather(cotangent.astype(jnp.bfloat16), "tensor", axis=0, tiled=True)
    down_grad = jnp.einsum("rf,rd->fd", hidden, mlp_grad_rows, preferred_element_type=jnp.float32)
    hidden_grad = jnp.einsum(
        "rd,fd->rf", mlp_grad_rows, down_low, preferred_element_type=jnp.float32
    )
    gate_grad = hidden_grad * up_value * sigmoid_gate * (1.0 + gate_value * (1.0 - sigmoid_gate))
    up_grad = hidden_grad * gate_value * sigmoid_gate
    gate_up_grad_low = jnp.stack([gate_grad, up_grad]).astype(jnp.bfloat16)
    gate_up_grad = jnp.einsum(
        "rd,crf->cdf", normed_mlp, gate_up_grad_low, preferred_element_type=jnp.float32
    )
    normed_mlp_part = jnp.einsum(
        "crf,cdf->rd", gate_up_grad_low, gate_up_low, preferred_element_type=jnp.float32
    )
    normed_mlp_grad = lax.psum_scatter(normed_mlp_part, "tensor", scatter_dimension=0, tiled=True)
    norm_back_mlp = jax.vjp(norm_rows, residual_mid, gain_mlp)[1]
    mid_from_norm, gain_mlp_grad = norm_back_mlp(normed_mlp_grad)
    mid_grad = cotangent + mid_from_norm
    attn_grad_rows = lax.all_gather(mid_grad.astype(jnp.bfloat16), "tensor", axis=0, tiled=True)
    out_grad = jnp.einsum("re,rd->ed", attended, attn_grad_rows, preferred_element_type=jnp.float32)
    attended_grad = jnp.einsum(
        "rd,ed->re", attn_grad_rows, out_low, preferred_element_type=jnp.float32
    ).astype(jnp.bfloat16)
    attended_grad = attended_grad.reshape(row_count, head_local, HDIM)

    def back_block(carry, block_inputs):
        key_grad, value_grad = carry
        block_index, log_total = block_inputs
        scores, query_block = block_scores(block_index)
        probs = jnp.exp(scores - log_total[..., None])
        grad_block = lax.dynamic_slice_in_dim(
            attended_grad, block_index * block_rows, block_rows, 0
        )
        probs_grad = jnp.einsum(
            "qhd,khd->hqk", grad_block, value_rows, preferred_element_type=jnp.float32
        )
        inner_term = jnp.sum(probs * probs_grad, axis=-1, keepdims=True)
        score_grad = (probs * (probs_grad - inner_term)).astype(jnp.bfloat16)
        query_grad = (
            jnp.einsum("hqk,khd->qhd", score_grad, key_rows, preferred_element_type=jnp.float32)
            * score_scale
        )
        key_grad = (
            key_grad
            + jnp.einsum(
                "hqk,qhd->khd", score_grad, query_block, preferred_element_type=jnp.float32
            )
            * score_scale
        )
        value_grad = value_grad + jnp.einsum(
            "hqk,qhd->khd",
            probs.astype(jnp.bfloat16),
            grad_block,
            preferred_element_type=jnp.float32,
        )
        return ((key_grad, value_grad), query_grad)

    zero_grad = jnp.zeros((row_count, head_local, HDIM), jnp.float32)
    carried, query_grads = lax.scan(back_block, (zero_grad, zero_grad), (block_ids, log_totals))
    projected_grad = jnp.stack(
        [
            query_grads.reshape(row_count, width_local),
            carried[0].reshape(row_count, width_local),
            carried[1].reshape(row_count, width_local),
        ]
    ).astype(jnp.bfloat16)
    qkv_grad = jnp.einsum(
        "rd,cre->cde", normed_attn, projected_grad, preferred_element_type=jnp.float32
    )
    normed_attn_part = jnp.einsum(
        "cre,cde->rd", projected_grad, qkv_low, preferred_element_type=jnp.float32
    )
    normed_attn_grad = lax.psum_scatter(
        normed_attn_part.astype(jnp.bfloat16), "tensor", scatter_dimension=0, tiled=True
    ).astype(jnp.float32)
    norm_back_attn = jax.vjp(norm_rows, residual_in, gain_attn)[1]
    input_from_norm, gain_attn_grad = norm_back_attn(normed_attn_grad)
    input_grad = mid_grad + input_from_norm
    gain_grads = lax.psum(jnp.stack([gain_attn_grad, gain_mlp_grad]), "tensor")
    gains_out, qkv_out, out_out, gate_up_out, down_out = (
        lax.psum_scatter(
            gain_grads.astype(jnp.bfloat16), "dp", scatter_dimension=1, tiled=True
        ).astype(jnp.float32),
        lax.psum_scatter(
            qkv_grad.astype(jnp.bfloat16), "dp", scatter_dimension=1, tiled=True
        ).astype(jnp.float32),
        lax.psum_scatter(
            out_grad.astype(jnp.bfloat16), "dp", scatter_dimension=1, tiled=True
        ).astype(jnp.float32),
        lax.psum_scatter(
            gate_up_grad.astype(jnp.bfloat16), "dp", scatter_dimension=1, tiled=True
        ).astype(jnp.float32),
        lax.psum_scatter(
            down_grad.astype(jnp.bfloat16), "dp", scatter_dimension=1, tiled=True
        ).astype(jnp.float32),
    )
    return (block_output, input_grad, gains_out, qkv_out, out_out, gate_up_out, down_out)


QB = 256
NT = (((1,), (1,)), ((), ()))
NN = (((1,), (0,)), ((), ()))
TN = (((0,), (0,)), ((), ()))


def _dot(a, b, dims):
    return lax.dot_general(a, b, dims, preferred_element_type=jnp.float32)


def _stacked(tile, columns, n):
    return pl.BlockSpec((1, tile, columns), lambda i: (n, i, 0))


def _full(shape):
    return pl.BlockSpec(shape, lambda i: (0,) * len(shape))


def _smem():
    return pl.BlockSpec(memory_space=pltpu.SMEM)


def _rows(tile, columns):
    return pl.BlockSpec((tile, columns), lambda i: (i, 0))


def _params():
    return pltpu.CompilerParams(dimension_semantics=("arbitrary",), vmem_limit_bytes=60 << 20)


STRETCH = 6.0


def _cost(flops, bytes_accessed):
    return pl.CostEstimate(
        flops=int(flops * STRETCH), bytes_accessed=int(bytes_accessed * STRETCH), transcendentals=0
    )


def _row_tile(rows):
    return rows // 2 if rows % 32 == 0 else rows


def _normed(values):
    inverse_rms = lax.rsqrt(jnp.mean(values * values, axis=-1, keepdims=True) + epsilon)
    return inverse_rms, values * inverse_rms


def _place_kernel(count, cut, where_ref, *refs):
    shards, outs = refs[:count], refs[count:]
    size = shards[0].shape[0]
    for n, shard in enumerate(shards):
        at = pl.ds(pl.multiple_of(where_ref[n] * size, size), size)
        outs[0][at, :] = shard[:, :cut]
        if len(outs) > 1:
            outs[1][at, :] = shard[:, cut:]


def place(where, shards, cut=None):
    size, columns = shards[0].shape
    widths = [columns] if cut is None else [cut, columns - cut]
    rows = size * len(shards)
    return pl.pallas_call(
        functools.partial(_place_kernel, len(shards), widths[0]),
        grid=(1,),
        out_shape=[jax.ShapeDtypeStruct((rows, c), shards[0].dtype) for c in widths],
        in_specs=[_smem()] + [_full((size, columns))] * len(shards),
        out_specs=[_full((rows, c)) for c in widths],
        compiler_params=_params(),
        cost_estimate=_cost(0, 4 * rows * columns),
        name="place",
    )(where, *shards)


def _project_kernel(x0_ref, x1_ref, gain_ref, w_ref, n0_ref, n1_ref, p0_ref, p1_ref):
    def run(x_ref, normed_ref, out_ref):
        normed = (_normed(x_ref[...].astype(jnp.float32))[1] * gain_ref[...]).astype(jnp.bfloat16)
        normed_ref[...] = normed
        out_ref[...] = _dot(normed, w_ref[...], NN).astype(jnp.bfloat16)

    half = pl.num_programs(0) // 2

    @pl.when(pl.program_id(0) < half)
    def _():
        run(x0_ref, n0_ref, p0_ref)

    @pl.when(pl.program_id(0) >= half)
    def _():
        run(x1_ref, n1_ref, p1_ref)


def project(x0, x1, gain, weight, columns):
    rows, depth = x0.shape
    tile = _row_tile(rows)
    steps = rows // tile
    early = lambda c: pl.BlockSpec((tile, c), lambda i: (jnp.minimum(i, steps - 1), 0))
    late = lambda c: pl.BlockSpec((tile, c), lambda i: (jnp.maximum(i - steps, 0), 0))
    out = lambda c: jax.ShapeDtypeStruct((rows, c), jnp.bfloat16)
    return pl.pallas_call(
        _project_kernel,
        grid=(2 * steps,),
        out_shape=[out(depth), out(depth), out(columns), out(columns)],
        in_specs=[early(depth), late(depth), _full((1, depth)), _full((depth, columns))],
        out_specs=[early(depth), late(depth), early(columns), late(columns)],
        compiler_params=_params(),
        cost_estimate=_cost(4 * rows * depth * columns, 4 * rows * (2 * depth + columns)),
        name="project",
    )(x0, x1, gain, weight)


def _mlp_kernel(keep, *refs):
    att_a, att_b, (xa, xb, ca, cb) = refs[:4], refs[4:8], refs[8:12]
    gain_ref, w_hbm, d_hbm, n_hbm, m_hbm = refs[12:17]
    hidden_ref, grad_ref, normed_ref = refs[17:20]
    part_a, part_b, branch_a, branch_b = refs[20:24]
    att_s, x_s, cot_s, o_s, w_s, d_s, sems = refs[-7:]
    width = att_a[0].shape[2]
    count = hidden_ref.shape[2]
    pulls = [
        pltpu.make_async_copy(
            n_hbm, o_s.at[:, pl.ds(0, 2 * width)], sems.at[0]
        ),
        pltpu.make_async_copy(m_hbm, o_s.at[:, pl.ds(2 * width, 2 * width)], sems.at[1]),
        pltpu.make_async_copy(w_hbm, w_s, sems.at[2]),
        pltpu.make_async_copy(d_hbm, d_s, sems.at[3]),
    ]
    first = pl.program_id(0) == 0
    late = pl.program_id(0) >= pl.num_programs(0) // 2

    @pl.when(first)
    def _():
        for pull in pulls:
            pull.start()

    def take(att, x_ref, cot_ref):
        for i, of in enumerate((0, 2, 1, 3)):
            att_s[:, i * width : (i + 1) * width] = att[of][0]
        x_s[...] = x_ref[...]
        cot_s[...] = cot_ref[...]

    @pl.when(jnp.logical_not(late))
    def _():
        take(att_a, xa, ca)

    @pl.when(late)
    def _():
        take(att_b, xb, cb)

    @pl.when(first)
    def _():
        for pull in pulls[:2]:
            pull.wait()

    residual = x_s[...].astype(jnp.float32) + _dot(att_s[...], o_s[...], NT)
    if keep:
        keep_ref = refs[24]

        @pl.when(late)
        def _():
            keep_ref[...] = residual

    normed_ref[0] = (_normed(residual)[1] * gain_ref[...]).astype(jnp.bfloat16)

    @pl.when(first)
    def _():
        pulls[2].wait()

    both = _dot(normed_ref[0], w_s[...], NN).astype(jnp.bfloat16).astype(jnp.float32)
    gate, up = both[:, :count], both[:, count:]

    @pl.when(first)
    def _():
        pulls[3].wait()

    hidden_grad = _dot(cot_s[...], d_s[...], NN)
    sig = 0.5 * jnp.tanh(0.5 * gate) + 0.5
    act = gate * sig
    hidden = (act * up).astype(jnp.bfloat16)
    hidden_ref[0] = hidden
    grad_ref[0, :, :count] = (hidden_grad * up * (sig + act * (1.0 - sig))).astype(jnp.bfloat16)
    grad_ref[0, :, count:] = (hidden_grad * act).astype(jnp.bfloat16)
    part = _dot(grad_ref[0], w_s[...], NT).astype(jnp.bfloat16)
    branch = _dot(hidden, d_s[...], NT).astype(jnp.bfloat16)

    @pl.when(jnp.logical_not(late))
    def _():
        part_a[...] = part
        branch_a[...] = branch

    @pl.when(late)
    def _():
        part_b[...] = part
        branch_b[...] = branch


def mlp(attended_a, attended_b, x, cot, gain, weights, down, out_near, out_mate, keep):
    rows, depth = x[0].shape
    width = attended_a[0][0].shape[2]
    count = weights.shape[1] // 2
    tile = _row_tile(rows)
    steps = rows // tile
    bf16, f32 = jnp.bfloat16, jnp.float32
    early = lambda i: jnp.minimum(i, steps - 1)
    late = lambda i: jnp.maximum(i - steps, 0)
    rows_of = lambda where: pl.BlockSpec((tile, depth), lambda i: (where(i), 0))
    stack = lambda c: pl.BlockSpec((1, tile, c), lambda i: (i // steps, i % steps, 0))
    member = lambda n, where: pl.BlockSpec((1, tile, width), lambda i: (n, where(i), 0))
    outs = [jax.ShapeDtypeStruct((2, rows, c), bf16) for c in (count, 2 * count, depth)]
    outs += [jax.ShapeDtypeStruct((rows, depth), bf16)] * 4
    out_specs = [stack(count), stack(2 * count), stack(depth)] + [rows_of(early), rows_of(late)] * 2
    if keep:
        outs.append(jax.ShapeDtypeStruct((rows, depth), f32))
        out_specs.append(rows_of(late))
    anywhere = pl.BlockSpec(memory_space=pl.ANY)
    return pl.pallas_call(
        functools.partial(_mlp_kernel, keep),
        grid=(2 * steps,),
        out_shape=outs,
        in_specs=[member(n, early) for v, n in attended_a]
        + [member(n, late) for v, n in attended_b]
        + [rows_of(early), rows_of(late)] * 2
        + [_full((1, depth)), anywhere, anywhere, anywhere, anywhere],
        out_specs=out_specs,
        scratch_shapes=[
            pltpu.VMEM((tile, 4 * width), bf16),
            pltpu.VMEM((tile, depth), bf16),
            pltpu.VMEM((tile, depth), bf16),
            pltpu.VMEM((depth, 4 * width), bf16),
            pltpu.VMEM((depth, 2 * count), bf16),
            pltpu.VMEM((depth, count), bf16),
            pltpu.SemaphoreType.DMA((4,)),
        ],
        compiler_params=_params(),
        cost_estimate=_cost(4 * rows * depth * (4 * width + 6 * count), 28 << 20),
        name="mlp",
    )(*[v for v, n in (*attended_a, *attended_b)], *x, *cot, gain, weights, down, out_near, out_mate)


def _pull_groups(right, right_s, row_at, column_at, step, sems, base):
    groups = []
    for c in range(right[0].shape[-1] // step):
        group = []
        at = row_at
        for j, piece in enumerate(right):
            rows = piece.shape[0]
            group.append(
                pltpu.make_async_copy(
                    piece.at[:, pl.ds(c * step, step)],
                    right_s.at[pl.ds(at, rows), pl.ds(column_at + c * step, step)],
                    sems.at[base + c * len(right) + j],
                )
            )
            at += rows
        groups.append(group)
    return groups


def _start_all(groups):
    @pl.when(pl.program_id(0) == 0)
    def _():
        for group in groups:
            for pull in group:
                pull.start()


def _wait_group(group):
    @pl.when(pl.program_id(0) == 0)
    def _():
        for pull in group:
            pull.wait()


def _join(pieces, out):
    at = 0
    for piece in pieces:
        rows = piece.shape[0]
        out[at : at + rows, :] = piece[...]
        at += rows


def _mlp_grad_kernel(n, step, *refs):
    normed, cot = refs[:2], refs[2 : 2 + n]
    grads, hidden = refs[2 + n : 4 + n], refs[4 + n : 6 + n]
    out_ref, left_s, right_s, sems = refs[6 + n :]
    members = lambda pair: [v.at[m] for v in pair for m in (0, 1)]
    wide = grads[0].shape[2]
    rows = left_s.shape[0] // n
    groups = _pull_groups(members(grads), right_s, 0, 0, step, sems, 0)
    groups += _pull_groups(members(hidden), right_s, 0, wide, step, sems, 4 * (wide // step))
    _start_all(groups)
    for m in range(n):
        left_s[m * rows : (m + 1) * rows, :] = normed[m // 2][m % 2]
    for c, group in enumerate(groups):
        at = slice(c * step, (c + 1) * step)
        if c * step == wide:
            _join(cot, left_s)
        _wait_group(group)
        out_ref[:, at] = _dot(left_s[...], right_s[:, at], TN).astype(out_ref.dtype)


def mlp_grads(normed, cot, grads, hidden, block=256):
    n = len(cot)
    piece, depth = cot[0].shape
    rows = n * piece
    columns = grads[0].shape[2] + hidden[0].shape[2]
    step = hidden[0].shape[2]
    anywhere = pl.BlockSpec(memory_space=pl.ANY)
    return pl.pallas_call(
        functools.partial(_mlp_grad_kernel, n, step),
        grid=(depth // block,),
        out_shape=jax.ShapeDtypeStruct((depth, columns), jnp.bfloat16),
        in_specs=[pl.BlockSpec((2, piece, block), lambda i: (0, 0, i))] * 2
        + [pl.BlockSpec((piece, block), lambda i: (0, i))] * n
        + [anywhere] * 4,
        out_specs=_rows(block, columns),
        scratch_shapes=[
            pltpu.VMEM((rows, block), jnp.bfloat16),
            pltpu.VMEM((rows, columns), jnp.bfloat16),
            pltpu.SemaphoreType.DMA((n * (columns // step),)),
        ],
        compiler_params=_params(),
        cost_estimate=_cost(2 * rows * depth * columns, 2 * rows * (depth + columns) + 2 * depth * columns),
        name="mlp_grads",
    )(*normed, *cot, *grads, *hidden)


def _split_rows(acc, y, near, far):
    size = near.shape[1]
    near[...] = acc[pl.ds(pl.multiple_of(y * size, size), size), :].astype(near.dtype)[None]
    far[...] = acc[pl.ds(pl.multiple_of((1 - y) * size, size), size), :].astype(far.dtype)[None]


def _qkv_grad_kernel(n, y_ref, *refs):
    left, right = refs[:n], refs[n : 2 * n]
    w_ref, gain_ref, row_ref, near, far, left_s, right_s, acc, sems = refs[2 * n :]
    columns = right_s.shape[1]
    groups = _pull_groups(right, right_s, 0, 0, columns, sems, 0)
    _start_all(groups)
    _join(left, left_s)
    _wait_group(groups[0])
    total = _dot(left_s[...], right_s[...], TN)
    acc[:, :columns] = total
    row = jnp.concatenate(
        [1.0 / gain_ref[...], row_ref[...], jnp.zeros((SEG - 9, row_ref.shape[1]), jnp.float32)], axis=0
    ).T
    attn = jnp.sum(total * w_ref[...].astype(jnp.float32), axis=-1, keepdims=True) * row[:, 0:1]
    lane = lax.broadcasted_iota(jnp.int32, row.shape, 1)
    acc[:, columns:] = jnp.where(lane == 0, attn, row)
    _split_rows(acc, y_ref[0], near, far)


def qkv_grads(y, normed, grads, weight, gain, mlp_sum, size):
    n, depth = len(normed), normed[0].shape[1]
    rows = sum(v.shape[0] for v in normed)
    columns = grads[0].shape[1]
    block = 2 * size
    anywhere = pl.BlockSpec(memory_space=pl.ANY)
    out = jax.ShapeDtypeStruct((depth // block, size, columns + SEG), jnp.bfloat16)
    out_spec = pl.BlockSpec((1, size, columns + SEG), lambda i: (i, 0, 0))
    lanes = lambda r: pl.BlockSpec((r, block), lambda i: (0, i))
    return pl.pallas_call(
        functools.partial(_qkv_grad_kernel, n),
        grid=(depth // block,),
        out_shape=[out, out],
        in_specs=[_smem()]
        + [lanes(v.shape[0]) for v in normed]
        + [anywhere] * n
        + [_rows(block, columns), lanes(1), lanes(8)],
        out_specs=[out_spec, out_spec],
        scratch_shapes=[
            pltpu.VMEM((rows, block), jnp.bfloat16),
            pltpu.VMEM((rows, columns), jnp.bfloat16),
            pltpu.VMEM((block, columns + SEG), jnp.float32),
            pltpu.SemaphoreType.DMA((n,)),
        ],
        compiler_params=_params(),
        cost_estimate=_cost(0, 0),
        name="qkv_grads",
    )(y, *normed, *grads, weight, gain, mlp_sum)


def _out_grad_kernel(left_ref, a0, a1, a2, a3, mine, theirs, right_s):
    width = a0.shape[2]

    @pl.when(pl.program_id(0) == 0)
    def _():
        for i, a in enumerate((a0, a2, a1, a3)):
            right_s[:, i * width : (i + 1) * width] = a[0]

    total = _dot(left_ref[...], right_s[...], TN).astype(mine.dtype)
    mine[...] = total[:, : 2 * width]
    theirs[...] = total[:, 2 * width :]


def out_grads(left, attended, block=256):
    rows, depth = left.shape
    width = attended[0][0].shape[2]
    out = jax.ShapeDtypeStruct((depth, 2 * width), jnp.bfloat16)
    member = lambda n: pl.BlockSpec((1, rows, width), lambda i: (n, 0, 0))
    return pl.pallas_call(
        _out_grad_kernel,
        grid=(depth // block,),
        out_shape=[out, out],
        in_specs=[pl.BlockSpec((rows, block), lambda i: (0, i))] + [member(n) for v, n in attended],
        out_specs=[_rows(block, 2 * width)] * 2,
        scratch_shapes=[pltpu.VMEM((rows, 4 * width), jnp.bfloat16)],
        compiler_params=_params(),
        cost_estimate=_cost(8 * rows * depth * width, 2 * rows * (depth + 4 * width) + 8 * depth * width),
        name="out_grads",
    )(left, *[v for v, n in attended])


def _pair_kernel(y_ref, a_ref, b_ref, near, far, acc):
    acc[...] = a_ref[...].astype(jnp.float32) + b_ref[...].astype(jnp.float32)
    _split_rows(acc, y_ref[0], near, far)


def pair_sum(y, a, b, size):
    depth, columns = a.shape
    block = 2 * size
    out = jax.ShapeDtypeStruct((depth // block, size, columns), jnp.bfloat16)
    out_spec = pl.BlockSpec((1, size, columns), lambda i: (i, 0, 0))
    return pl.pallas_call(
        _pair_kernel,
        grid=(depth // block,),
        out_shape=[out, out],
        in_specs=[_smem()] + [_rows(block, columns)] * 2,
        out_specs=[out_spec, out_spec],
        scratch_shapes=[pltpu.VMEM((block, columns), jnp.float32)],
        compiler_params=_params(),
        cost_estimate=_cost(0, 6 * depth * columns),
        name="pair_sum",
    )(y, a, b)


def _fold_kernel(z_ref, near, passed, *outs):
    count = near.shape[0]
    for step, out in enumerate(outs):
        row = lax.rem(z_ref[0] + step, count)
        out[...] = (near[row].astype(jnp.float32) + passed[row].astype(jnp.float32)).astype(out.dtype)


def fold(z, near, passed):
    count, size, columns = near.shape
    return pl.pallas_call(
        _fold_kernel,
        grid=(1,),
        out_shape=[jax.ShapeDtypeStruct((size, columns), jnp.bfloat16)] * count,
        in_specs=[_smem(), _full(near.shape), _full(near.shape)],
        out_specs=[_full((size, columns))] * count,
        compiler_params=_params(),
        cost_estimate=_cost(0, 0),
        name="fold",
    )(z, near, passed)


def _mid_kernel(p0, p1, p2, res_ref, cot_ref, gain_ref, near_ref, mate_ref, mid_ref, attn_ref, a0, a1, a2, a3, sum_ref):
    width = a0.shape[1]
    grad = p0[...].astype(jnp.float32) + p1[...].astype(jnp.float32) + p2[...].astype(jnp.float32)
    inverse, normed = _normed(res_ref[...])
    term = jnp.sum(grad * normed, axis=0, keepdims=True)

    @pl.when(pl.program_id(0) == 0)
    def _():
        sum_ref[...] = jnp.zeros_like(sum_ref)

    sum_ref[0:1, :] += term
    scaled = grad * gain_ref[...]
    mid = cot_ref[...] + inverse * (scaled - normed * jnp.mean(scaled * normed, axis=-1, keepdims=True))
    mid_ref[...] = mid
    low = mid.astype(jnp.bfloat16)
    attn_ref[...] = low
    a0[...] = _dot(low, near_ref[:, :width], NN).astype(jnp.bfloat16)
    a1[...] = _dot(low, mate_ref[:, :width], NN).astype(jnp.bfloat16)
    a2[...] = _dot(low, near_ref[:, width : 2 * width], NN).astype(jnp.bfloat16)
    a3[...] = _dot(low, mate_ref[:, width:], NN).astype(jnp.bfloat16)


def middle(parts, residual, cot, gain, weights, out_mate):
    rows, depth = residual.shape
    width = out_mate.shape[1] // 2
    tile = _row_tile(rows)
    return pl.pallas_call(
        _mid_kernel,
        grid=(rows // tile,),
        out_shape=[
            jax.ShapeDtypeStruct((rows, depth), jnp.float32),
            jax.ShapeDtypeStruct((rows, depth), jnp.bfloat16),
        ]
        + [jax.ShapeDtypeStruct((rows, width), jnp.bfloat16)] * 4
        + [jax.ShapeDtypeStruct((8, depth), jnp.float32)],
        in_specs=[_rows(tile, depth)] * 5
        + [
            _full((1, depth)),
            _full((depth, 2 * width)),
            _full(out_mate.shape),
        ],
        out_specs=[_rows(tile, depth)] * 2 + [_rows(tile, width)] * 4 + [_full((8, depth))],
        compiler_params=_params(),
        cost_estimate=_cost(2 * rows * depth * 4 * width, rows * depth * 20),
        name="middle",
    )(*parts, residual, cot, gain, weights, out_mate)


def _back_kernel(add, grad_ref, w_ref, *refs):
    part = _dot(grad_ref[...], w_ref[...], NT)
    if add:
        part = part + refs[0][...].astype(jnp.float32)
    refs[-1][...] = part.astype(refs[-1].dtype)


def project_back(grad, weight, add=None):
    rows, columns = grad.shape
    depth = weight.shape[0]
    tile = _row_tile(rows)
    extra = [] if add is None else [add]
    return pl.pallas_call(
        functools.partial(_back_kernel, add is not None),
        grid=(rows // tile,),
        out_shape=jax.ShapeDtypeStruct((rows, depth), jnp.bfloat16),
        in_specs=[_rows(tile, columns), _full((depth, columns))] + [_rows(tile, depth)] * len(extra),
        out_specs=_rows(tile, depth),
        compiler_params=_params(),
        cost_estimate=_cost(0, 0),
        name="project_back",
    )(grad, weight, *extra)


def _last_kernel(p0, p1, p2, x_ref, mid_ref, gain_ref, out_ref):
    grad = p0[...].astype(jnp.float32) + p1[...].astype(jnp.float32) + p2[...].astype(jnp.float32)
    inverse, normed = _normed(x_ref[...].astype(jnp.float32))
    scaled = grad * gain_ref[...]
    out_ref[...] = mid_ref[...] + inverse * (
        scaled - normed * jnp.mean(scaled * normed, axis=-1, keepdims=True)
    )


def last(parts, x, mid, gain):
    rows, depth = x.shape
    tile = _row_tile(rows)
    return pl.pallas_call(
        _last_kernel,
        grid=(rows // tile,),
        out_shape=jax.ShapeDtypeStruct((rows, depth), jnp.float32),
        in_specs=[_rows(tile, depth)] * 5 + [_full((1, depth))],
        out_specs=_rows(tile, depth),
        compiler_params=_params(),
        cost_estimate=_cost(0, rows * depth * 16),
        name="last",
    )(*parts, x, mid, gain)


def _half_place(info_ref, b, half, piece_blocks):
    block = 2 * b + half
    piece = lax.bitwise_xor(lax.div(block, piece_blocks), info_ref[0])
    return piece, lax.rem(block, piece_blocks) * SEG


def _mask(heads, same, causal):
    key = lax.broadcasted_iota(jnp.int32, (QB, heads * QB), 0)
    query = lax.broadcasted_iota(jnp.int32, (QB, heads * QB), 1) % QB
    allowed = jnp.logical_not(same & ((key // SEG) != (query // SEG)))
    if causal:
        allowed = allowed & (key <= query)
    return allowed


def _spread(block, heads):
    turned = block.T
    lane = lax.broadcasted_iota(jnp.int32, turned.shape, 0) // HDIM
    zero = jnp.zeros_like(turned)
    return jnp.concatenate([jnp.where(lane == h, turned, zero) for h in range(heads)], axis=1)


def _stack(block, heads):
    lane = lax.broadcasted_iota(jnp.int32, block.shape, 1) // HDIM
    zero = jnp.zeros_like(block)
    return jnp.concatenate([jnp.where(lane == h, block, zero) for h in range(heads)], axis=0)


def _parents(info_ref, b):
    leaf = 2 * (b - (TRUNK + 4 * SEG) // QB)
    return [pl.multiple_of(TRUNK - SEG + SEG * info_ref[2 + leaf + side], SEG) for side in (0, 1)]


def _attn_fwd_kernel(heads, piece_count, info_ref, *refs):
    pieces = refs[:piece_count]
    out_ref, lse_ref = refs[piece_count : piece_count + 2]
    q_s, k_s, vt_s, qt_s, s_s, p_s, m_s, l_s, acc_s, kp_s, vp_s = refs[piece_count + 2 :]
    width = heads * HDIM
    piece_rows = pieces[0].shape[0]
    tensor = info_ref[0]
    base = info_ref[1]
    trunk_blocks = TRUNK // QB
    leaf_block = (TRUNK + 4 * SEG) // QB
    for j in range(piece_count):
        at = pl.multiple_of(piece_rows * lax.bitwise_xor(tensor, j), SEG)
        q_s[pl.ds(at, piece_rows), :] = pieces[j][:, :width] * jnp.asarray(HDIM**-0.5, jnp.bfloat16)
        k_s[pl.ds(at, piece_rows), :] = pieces[j][:, width : 2 * width]
        vt_s[:, pl.ds(at, piece_rows)] = pieces[j][:, 2 * width :].T

    def q_block(i, carry):
        b = base + i
        row = pl.multiple_of(b * QB, QB)
        own = pl.ds(row, QB)
        leaf = b >= leaf_block
        qt_s[...] = _spread(q_s[own, :], heads)

        def score(keys, at, size, allowed):
            scores = _dot(keys, qt_s[...], NN)
            if allowed is not None:
                scores = jnp.where(allowed, scores, -1e30)
            s_s[pl.ds(at, size), :] = scores
            return jnp.max(scores, axis=0, keepdims=True)

        m_s[0:1, :] = score(k_s[own, :], TRUNK, QB, _mask(heads, b >= trunk_blocks, True))

        @pl.when(leaf)
        def _():
            for side, at in enumerate(_parents(info_ref, b)):
                kp_s[side * SEG : (side + 1) * SEG, :] = k_s[pl.ds(at, SEG), :]
                vp_s[:, side * SEG : (side + 1) * SEG] = vt_s[:, pl.ds(at, SEG)]
            top = score(kp_s[...], TRUNK + QB, QB, _mask(heads, True, False))
            m_s[0:1, :] = jnp.maximum(m_s[0:1, :], top)

        @pl.when(b >= trunk_blocks)
        def _():
            m_s[0:1, :] = jnp.maximum(m_s[0:1, :], score(k_s[:TRUNK, :], 0, TRUNK, None))

        @pl.when(b < trunk_blocks)
        def _():
            def chunk(c, carry):
                at = pl.multiple_of(c * QB, QB)
                m_s[0:1, :] = jnp.maximum(m_s[0:1, :], score(k_s[pl.ds(at, QB), :], at, QB, None))
                return carry

            lax.fori_loop(0, b, chunk, 0)

        def mix(values, at, size, fresh):
            probs = jnp.exp(s_s[pl.ds(at, size), :] - m_s[0:1, :])
            total = jnp.sum(probs, axis=0, keepdims=True)
            p_s[pl.ds(at, size), :] = probs.astype(jnp.bfloat16)
            l_s[0:1, :] = total if fresh else l_s[0:1, :] + total
            for h in range(heads):
                of = slice(h * HDIM, (h + 1) * HDIM)
                term = _dot(values(of), p_s[pl.ds(at, size), h * QB : (h + 1) * QB], NN)
                acc_s[of, :] = term if fresh else acc_s[of, :] + term

        mix(lambda of: vt_s[of, own], TRUNK, QB, True)

        @pl.when(leaf)
        def _():
            mix(lambda of: vp_s[of, :], TRUNK + QB, QB, False)

        @pl.when(b >= trunk_blocks)
        def _():
            mix(lambda of: vt_s[of, :TRUNK], 0, TRUNK, False)

        @pl.when(b < trunk_blocks)
        def _():
            def chunk(c, carry):
                at = pl.multiple_of(c * QB, QB)
                mix(lambda of: vt_s[of, pl.ds(at, QB)], at, QB, False)
                return carry

            lax.fori_loop(0, b, chunk, 0)

        mixed = []
        for h in range(heads):
            columns = slice(h * QB, (h + 1) * QB)
            total = l_s[0:1, columns]
            lse_ref[h : h + 1, pl.ds(pl.multiple_of(i * QB, QB), QB)] = m_s[0:1, columns] + jnp.log(total)
            mixed.append(acc_s[h * HDIM : (h + 1) * HDIM, :] / total)
        mixed = jnp.concatenate(mixed, axis=0).T.astype(jnp.bfloat16)
        for half in (0, 1):
            piece, at = _half_place(info_ref, b, half, piece_rows // SEG)
            at = pl.multiple_of(at, SEG)
            out_ref[lax.bitwise_and(piece, 1), pl.ds(at, SEG), :] = mixed[half * SEG : (half + 1) * SEG]
        return carry

    lax.fori_loop(0, lse_ref.shape[1] // QB, q_block, 0)


def attention_forward(info, pieces, heads):
    rows = sum(p.shape[0] for p in pieces)
    piece_rows = pieces[0].shape[0]
    width = heads * HDIM
    half = rows // 2
    bf16, f32 = jnp.bfloat16, jnp.float32
    return pl.pallas_call(
        functools.partial(_attn_fwd_kernel, heads, len(pieces)),
        out_shape=[
            jax.ShapeDtypeStruct((2, piece_rows, width), bf16),
            jax.ShapeDtypeStruct((8, half), f32),
        ],
        grid=(1,),
        in_specs=[_smem()] + [_full(p.shape) for p in pieces],
        out_specs=[_full((2, piece_rows, width)), _full((8, half))],
        scratch_shapes=[
            pltpu.VMEM((rows, width), bf16),
            pltpu.VMEM((rows, width), bf16),
            pltpu.VMEM((width, rows), bf16),
            pltpu.VMEM((width, heads * QB), bf16),
            pltpu.VMEM((TRUNK + 2 * QB, heads * QB), f32),
            pltpu.VMEM((TRUNK + 2 * QB, heads * QB), bf16),
            pltpu.VMEM((8, heads * QB), f32),
            pltpu.VMEM((8, heads * QB), f32),
            pltpu.VMEM((width, QB), f32),
            pltpu.VMEM((QB, width), bf16),
            pltpu.VMEM((width, QB), bf16),
        ],
        compiler_params=_params(),
        cost_estimate=_cost(rows * 1400 * width * 4, rows * width * 8),
        name="attn_fwd",
    )(info, *pieces)


def _attn_bwd_kernel(heads, info_ref, *refs):
    n = 4
    pieces, mixed_in, grads = refs[:n], refs[n : n + 2], refs[n + 2 : 2 * n + 2]
    lse_refs = refs[2 * n + 2 : 2 * n + 4]
    outs = refs[2 * n + 4 : 3 * n + 4]
    q_s, k_s, kt_s, v_s, o_s, g_s, dk_s, dv_s, lse_s = refs[3 * n + 4 : 3 * n + 13]
    qt_s, gt_s, qm_s, gm_s, row_s, delta_s, acc_s, kp_s, vp_s, kpt_s = refs[3 * n + 13 :]
    width = heads * HDIM
    piece_rows = pieces[0].shape[0]
    tensor = info_ref[0]
    chip = lax.div(tensor, 2)
    half_rows = lse_refs[0].shape[1]
    scale = HDIM**-0.5
    trunk_blocks = TRUNK // QB
    leaf_block = (TRUNK + 4 * SEG) // QB
    for j in range(n):
        rows_at = pl.ds(pl.multiple_of(piece_rows * lax.bitwise_xor(tensor, j), SEG), piece_rows)
        q_s[rows_at, :] = pieces[j][:, :width] * jnp.asarray(scale, jnp.bfloat16)
        k_s[rows_at, :] = pieces[j][:, width : 2 * width]
        kt_s[:, rows_at] = pieces[j][:, width : 2 * width].T
        v_s[rows_at, :] = pieces[j][:, 2 * width :]
        o_s[rows_at, :] = mixed_in[j // 2][j % 2]
        g_s[rows_at, :] = grads[j][...]
    lse_s[:, pl.ds(pl.multiple_of(chip * half_rows, SEG), half_rows)] = lse_refs[0][...]
    lse_s[:, pl.ds(pl.multiple_of((1 - chip) * half_rows, SEG), half_rows)] = lse_refs[1][...]
    dk_s[...] = jnp.zeros_like(dk_s)
    dv_s[...] = jnp.zeros_like(dv_s)
    head_of_lane = lax.broadcasted_iota(jnp.int32, (8, width), 1) // HDIM
    pick = jnp.where(lax.broadcasted_iota(jnp.int32, (8, width), 0) == head_of_lane, 1.0, 0.0)

    def q_block(b, carry):
        row = pl.multiple_of(b * QB, QB)
        own = pl.ds(row, QB)
        both = o_s[own, :].astype(jnp.float32) * g_s[own, :].astype(jnp.float32)
        delta = lax.dot_general(
            pick, both, NT, precision=lax.Precision.HIGHEST, preferred_element_type=jnp.float32
        )
        for h in range(heads):
            columns = slice(h * QB, (h + 1) * QB)
            delta_s[0:1, columns] = delta[h : h + 1, :]
            row_s[0:1, columns] = lse_s[h : h + 1, own]
        qt_s[...] = _spread(q_s[own, :], heads)
        gt_s[...] = _spread(g_s[own, :], heads)
        qm_s[...] = _stack(q_s[own, :], heads)
        gm_s[...] = _stack(g_s[own, :], heads)

        def step(k, v, kt, allowed, fresh, targets):
            scores = _dot(k, qt_s[...], NN)
            probs_grad = _dot(v, gt_s[...], NN)
            probs = jnp.exp(scores - row_s[0:1, :])
            if allowed is not None:
                probs = jnp.where(allowed, probs, 0.0)
            ds = (probs * (probs_grad - delta_s[0:1, :])).astype(jnp.bfloat16)
            dv = _dot(probs.astype(jnp.bfloat16), gm_s[...], NN)
            dk = _dot(ds, qm_s[...], NN)
            for h in range(heads):
                of = slice(h * HDIM, (h + 1) * HDIM)
                term = _dot(kt(of), ds[:, h * QB : (h + 1) * QB], NN)
                acc_s[of, :] = term if fresh else acc_s[of, :] + term
            first = 0
            for at, size in targets:
                dv_s[pl.ds(at, size), :] += dv[first : first + size]
                dk_s[pl.ds(at, size), :] += dk[first : first + size]
                first += size

        step(
            k_s[own, :], v_s[own, :], lambda of: kt_s[of, own],
            _mask(heads, b >= trunk_blocks, True), True, [(row, QB)],
        )

        @pl.when(b >= leaf_block)
        def _():
            ats = _parents(info_ref, b)
            for side, at in enumerate(ats):
                part = slice(side * SEG, (side + 1) * SEG)
                kp_s[part, :] = k_s[pl.ds(at, SEG), :]
                vp_s[part, :] = v_s[pl.ds(at, SEG), :]
                kpt_s[:, part] = kt_s[:, pl.ds(at, SEG)]
            step(
                kp_s[...], vp_s[...], lambda of: kpt_s[of, :],
                _mask(heads, True, False), False, [(at, SEG) for at in ats],
            )

        def trunk_step(c):
            at = pl.multiple_of(c * QB, QB)
            here = pl.ds(at, QB)
            step(k_s[here, :], v_s[here, :], lambda of: kt_s[of, here], None, False, [(at, QB)])

        def trunk_pair(c, carry):
            trunk_step(2 * c)
            trunk_step(2 * c + 1)
            return carry

        count = jnp.minimum(b, trunk_blocks)
        lax.fori_loop(0, lax.div(count, 2), trunk_pair, 0)

        @pl.when(lax.rem(count, 2) == 1)
        def _():
            trunk_step(count - 1)

        q_s[own, :] = (acc_s[...] * scale).T.astype(jnp.bfloat16)
        return carry

    lax.fori_loop(0, q_s.shape[0] // QB, q_block, 0)
    for j in range(n):
        rows_at = pl.ds(pl.multiple_of(piece_rows * lax.bitwise_xor(tensor, j), SEG), piece_rows)
        outs[j][:, :width] = q_s[rows_at, :]
        outs[j][:, width : 2 * width] = dk_s[rows_at, :].astype(jnp.bfloat16)
        outs[j][:, 2 * width :] = dv_s[rows_at, :].astype(jnp.bfloat16)


def attention_backward(info, pieces, mixed, grads, lses, heads):
    n = len(pieces)
    piece_rows = pieces[0].shape[0]
    rows = n * piece_rows
    width = heads * HDIM
    bf16, f32 = jnp.bfloat16, jnp.float32
    rows_low = pltpu.VMEM((rows, width), bf16)
    return pl.pallas_call(
        functools.partial(_attn_bwd_kernel, heads),
        out_shape=[jax.ShapeDtypeStruct((piece_rows, 3 * width), bf16)] * n,
        grid=(1,),
        in_specs=[_smem()] + [_full(v.shape) for v in (*pieces, *mixed, *grads, *lses)],
        out_specs=[_full((piece_rows, 3 * width))] * n,
        scratch_shapes=[
            rows_low,
            rows_low,
            pltpu.VMEM((width, rows), bf16),
            rows_low,
            rows_low,
            rows_low,
            pltpu.VMEM((rows, width), f32),
            pltpu.VMEM((rows, width), f32),
            pltpu.VMEM((8, rows), f32),
            pltpu.VMEM((width, heads * QB), bf16),
            pltpu.VMEM((width, heads * QB), bf16),
            pltpu.VMEM((heads * QB, width), bf16),
            pltpu.VMEM((heads * QB, width), bf16),
            pltpu.VMEM((8, heads * QB), f32),
            pltpu.VMEM((8, heads * QB), f32),
            pltpu.VMEM((width, QB), f32),
            pltpu.VMEM((QB, width), bf16),
            pltpu.VMEM((QB, width), bf16),
            pltpu.VMEM((width, QB), bf16),
        ],
        compiler_params=_params(),
        cost_estimate=_cost(0, 0),
        name="attn_bwd",
    )(info, *pieces, *mixed, *grads, *lses)


def mate(x):
    return lax.ppermute(x, "tensor", [(i, i ^ 1) for i in range(4)])


def across(x):
    return lax.ppermute(x, "tensor", [(i, i ^ 2) for i in range(4)])


def corner(x):
    return lax.ppermute(x, "tensor", [(i, i ^ 3) for i in range(4)])


def beside(x):
    return lax.ppermute(x, "dp", [(i, i ^ 1) for i in range(8)])


def ahead(x, step):
    return lax.ppermute(x, "dp", [(i, (i + 2 * step) % 8) for i in range(8)])


def after(x, *others):
    return lax.optimization_barrier((x, *others))[0]


def after_all(values, *others):
    return list(lax.optimization_barrier((*values, *others))[: len(values)])


def line_hops(x):
    return [x] + [ahead(x, step) for step in (1, 3, 2)]


def spread_hops(line, far, cut=None):
    dp = lax.axis_index("dp")
    z, y = dp // 2, dp % 2
    order = jnp.array([0, 1, 3, 2], jnp.int32)
    from_z = (z - order) % 4
    where = jnp.concatenate([2 * from_z + y, 2 * from_z + 1 - y]).astype(jnp.int32)
    return place(where, line + far, cut)


def fold_hops(near, passed):
    z = (lax.axis_index("dp") // 2).astype(jnp.int32)[None]
    return fold(z, near, passed)


def send_hops(chunks):
    return [chunks[0]] + [ahead(chunks[step], step) for step in (2, 1, 3)]


def sum_hops(received):
    return sum(v.astype(jnp.float32) for v in received)


def body(
    block_input,
    norm_gains,
    qkv_weight,
    out_weight,
    gate_up_weight,
    down_weight,
    parent_of_row,
    cotangent,
):
    bf16, f32 = jnp.bfloat16, jnp.float32
    shard = qkv_weight.shape[1]
    width = qkv_weight.shape[2]
    hidden_width = gate_up_weight.shape[2]
    heads = width // HDIM
    rows = parent_of_row.shape[0]
    tensor = lax.axis_index("tensor")
    chip = tensor // 2
    y = (lax.axis_index("dp") % 2).astype(jnp.int32)[None]
    leaf_first = TRUNK + 4 * SEG
    parents = parent_of_row[leaf_first::SEG]
    half_blocks = rows // (2 * QB)
    place_own = jnp.stack([tensor, half_blocks * chip]).astype(jnp.int32)
    place_far = jnp.stack([tensor, half_blocks * (1 - chip)]).astype(jnp.int32)
    info_own = jnp.concatenate([place_own, parents])
    info_far = jnp.concatenate([place_far, parents])

    gains_shard = jnp.pad(norm_gains.astype(bf16).T, ((0, 0), (0, SEG - 2)))
    qkv_shard = qkv_weight.astype(bf16).transpose(1, 0, 2).reshape(shard, 3 * width)
    first_line = line_hops(jnp.concatenate([qkv_shard, gains_shard], axis=1))
    out_shard = out_weight.astype(bf16).T
    out_x = across(out_shard)
    beyond = across(after(block_input, out_x))
    near_x = mate(block_input)
    gate_up_shard = gate_up_weight.astype(bf16).transpose(1, 0, 2).reshape(shard, 2 * hidden_width)
    rest = lax.all_gather(after(gate_up_shard, out_x), "dp", axis=0, tiled=True)
    first_far = [beside(v) for v in first_line]
    first = spread_hops(first_line, first_far)[0]
    second_shard = jnp.concatenate([down_weight.astype(bf16).T, out_shard, out_x], axis=1)
    down_line = line_hops(after(second_shard, *first_line))
    gains_low = first[:, 3 * width : 3 * width + 2].T.astype(f32)
    gain_attn, gain_mlp = gains_low[0:1], gains_low[1:2]
    n0, n1, p0, p1 = project(block_input, near_x, gain_attn, first, 3 * width)
    inputs = [block_input, near_x, beyond, mate(beyond)]
    n2, n3, p2, p3 = project(inputs[2], after(inputs[3], p1), gain_attn, first, 3 * width)
    normed_attn, projected = [n0, n1, n2, n3], [p0, p1, p2, p3]
    cot_low = cotangent.astype(bf16)
    cot_x = across(after(cot_low, beyond))

    own, lse_own = attention_forward(info_own, projected, heads)
    own_x, own_m = across(after(own, cot_x)), mate(own)
    down_far = [beside(after(down_line[0], p1)), beside(after(down_line[1], own)), beside(after(down_line[2], own))]
    cot_near = mate(after(cot_low, own))
    far, lse_far = attention_forward(after(info_far, own), projected, heads)
    down_far += [beside(after(v, far)) for v in down_line[3:]]
    far_m, own_xm = mate(far), mate(after(own_x, far))
    far_x = across(far)
    down_low, out_low = spread_hops(down_line, down_far, hidden_width)
    cot_rows = [cot_low, cot_near, cot_x, mate(after(cot_x, far))]
    out_far = mate(out_low)

    own_rows = [(own, 0), (own_m, 1), (far_x, 0), None]
    hidden_far, grads_far, normed_far, part3, part2, branch3, branch2 = mlp(
        [(far, 1), (far_m, 0), (own_x, 1), (own_xm, 0)],
        [(far, 0), (far_m, 1), (own_x, 0), (own_xm, 1)],
        [inputs[3], inputs[2]], [cot_rows[3], cot_rows[2]], gain_mlp, rest, down_low, out_low, out_far, False,
    )
    far_xm = mate(after(far_x, part3))
    own_rows[3] = (far_xm, 1)
    passed = (part2.astype(f32) + mate(after(part3, far_x)).astype(f32)).astype(bf16)
    passed_x = across(passed)
    hidden_own, grads_own, normed_own, part1, part0, branch1, branch0, residual_mid = mlp(
        [(own, 1), (own_m, 0), (far_x, 1), (far_xm, 0)], own_rows,
        [inputs[1], inputs[0]], [after(cot_rows[1], passed), cot_rows[0]],
        gain_mlp, rest, down_low, out_low, out_far, True,
    )
    mlp_parts = [part0, mate(after(part1, passed_x)), passed_x]

    grad_sum = mlp_grads(
        [after(normed_far, passed_x), normed_own],
        [cot_rows[n] for n in (3, 2, 1, 0)],
        [grads_far, grads_own],
        [hidden_far, hidden_own],
    )
    mid_grad, attn_grad, g0, g1, g2, g3, mlp_sum = middle(
        [after(mlp_parts[0], grad_sum), *mlp_parts[1:]], residual_mid, cotangent, gain_mlp, out_low, out_far
    )
    grad_sum = lax.psum_scatter(grad_sum, "dp", scatter_dimension=0, tiled=True)
    g_x, g_c, g_m = across(g2), corner(g3), mate(g1)
    out_mine, out_theirs = out_grads(attn_grad, own_rows)
    out_theirs = mate(out_theirs)
    branch_passed = (branch2.astype(f32) + mate(branch3).astype(f32)).astype(bf16)
    out_pair = pair_sum(y, out_mine, after(out_theirs, branch_passed), shard)
    out_y = beside(out_pair[1])
    branch_x = across(after(branch_passed, g_x, g_c))

    bwd_grads = after_all([g0, g_m, g_x, g_c], out_pair[1], branch_passed)
    projected_grad = attention_backward(
        info_own, projected, [own, far], bwd_grads, [lse_own, lse_far], heads
    )
    back3 = project_back(after(projected_grad[3], out_y, branch_x), first)
    qkv_pair = qkv_grads(
        y, normed_attn, after_all(projected_grad, back3), first, gain_attn, mlp_sum, shard
    )
    qkv_y = beside(qkv_pair[1])
    out_chunks = fold_hops(out_pair[0], after(out_y, qkv_pair[1]))
    out_received = send_hops(out_chunks)
    back2 = project_back(after(projected_grad[2], out_chunks[1]), first, mate(back3))
    back_x = across(back2)
    back1 = project_back(after(projected_grad[1], back2), first)
    qkv_chunks = fold_hops(qkv_pair[0], after(qkv_y, back1))
    qkv_received = send_hops(qkv_chunks)
    back0 = project_back(after(projected_grad[0], qkv_chunks[1]), first)
    back_m = mate(after(back1, qkv_y))
    branch_sum = branch0.astype(f32) + mate(branch1).astype(f32)
    block_output = residual_mid + branch_sum + after(branch_x, back0).astype(f32)
    grad_sum = after(grad_sum, qkv_chunks[1]).astype(f32)
    down_out = grad_sum[:, 2 * hidden_width :].T
    gate_up_out = grad_sum[:, : 2 * hidden_width].reshape(shard, 2, hidden_width).transpose(1, 0, 2)
    input_grad = last(
        [back0, back_m, after(back_x, down_out, gate_up_out, block_output)], block_input, mid_grad, gain_attn
    )
    out_sum = sum_hops(out_received)
    qkv_sum = sum_hops(after_all(qkv_received, input_grad))
    qkv_out = qkv_sum[:, : 3 * width].reshape(shard, 3, width).transpose(1, 0, 2)
    gains_sum = qkv_sum[:, 3 * width :]
    gains_sum = gains_sum + mate(gains_sum.astype(bf16)).astype(f32)
    from_x = across(jnp.concatenate([out_sum[:, width:], gains_sum], axis=1).astype(bf16)).astype(f32)
    out_out = (out_sum[:, :width] + from_x[:, :width]).T
    gains_out = (gains_sum + from_x[:, width:])[:, :2].T
    return (block_output, input_grad, gains_out, qkv_out, out_out, gate_up_out, down_out)


def solution(mesh):
    placed = (
        P(("dp", "tensor"), None),
        P(None, "dp"),
        P(None, "dp", "tensor"),
        P("tensor", "dp"),
        P(None, "dp", "tensor"),
        P("tensor", "dp"),
        P("dp"),
        P(("dp", "tensor"), None),
    )
    four_by_eight = mesh.shape["tensor"] == 4 and mesh.shape["dp"] == 8
    return jax.shard_map(
        body if four_by_eight else body_any_mesh,
        mesh=mesh,
        in_specs=placed,
        out_specs=(
            P(("dp", "tensor"), None),
            P(("dp", "tensor"), None),
            P(None, "dp"),
            P(None, "dp", "tensor"),
            P("tensor", "dp"),
            P(None, "dp", "tensor"),
            P("tensor", "dp"),
        ),
        check_vma=False,
    )
```
